32 devices in a mesh: ens: 2 (over y), lon: 4 (over x, core), lat: 4 (over z).
Axes of the slice: x: 2, y: 2, z: 4, core: 2. Of those that a mesh axis runs over, the one named last changes fastest.
Arguments:
- noise: float32 [64, 64, 512], P('ens', 'lat', 'lon'), parts along dimension 0, may hold values from -6 to 6
- kappa2: float32 [32, 64, 512], P(None, 'lat', 'lon'), may hold values from 0.03 to 0.3
- conduct: float32 [3, 32, 64, 512], P(None, None, 'lat', 'lon'), may hold values from 0.3 to 3
- land: int32 [32, 64, 512], P(None, 'lat', 'lon'), may hold values 0 or 1
Outputs:
- solution_field: float32 [64, 64, 512], P('ens', 'lat', 'lon'), parts along dimension 0
- residual: float32 [64, 64, 512], P('ens', 'lat', 'lon'), parts along dimension 0
The draws below stay inside these ranges and needn't reach their ends.
There are 2 independent parts, one for each index of `ens`. The reference program is written for one: setup_inputs(seed, part) draws one part's arguments, and reference() takes and returns one part's arrays. A program takes and returns all parts, laid end to end along the dimension named above; an argument that names none is the same for every part. Nothing has to cross between parts.
Inputs may be any that keep to these rules, and one draw needn't show every extreme that they name: 1 marks an ocean cell, 0 a land cell.
All inputs are finite; a program needn't handle non-finite values. No bound on the sum of `land` on one device may be relied on, other than what follows from the above.
Results may differ from the reference program's by a relative error of at most 0.00035.
Values sent between devices are 32-bit elements; how exact they have to be, the bound alone decides.
No kernel may reach another device: no remote copies, remote signals or barrier semaphores. Data moves between devices by JAX's collectives and lax.ppermute only.
A program may use at most 64 MiB of HBM per device.

```python
import math
import jax
import jax.numpy as jnp

NZ = 32
ITERS = 2
NLON = 512
NLAT = 64


def set_ends(result, stream_key, smallest, largest):
    shape = result.shape
    place = [jax.random.randint(jax.random.fold_in(stream_key, axis), (), 0, shape[axis]) for axis in range(len(shape))]
    result = result.at[tuple(place)].set(smallest)
    longest = shape.index(max(shape))
    place[longest] = (place[longest] + 1) % shape[longest]
    return result.at[tuple(place)].set(largest)


def shard_levels(own_key, dims, split, smallest, largest):
    loudness = 1.0
    for axis_at, blocks in split:
        steps = jax.random.uniform(jax.random.fold_in(jax.random.fold_in(own_key, 6), axis_at), (blocks,), jnp.float32, smallest / len(split), largest / len(split))
        loudness = loudness * jnp.repeat(jnp.exp(steps), dims[axis_at] // blocks).reshape((-1,) + (1,) * (len(dims) - 1 - axis_at))
    return loudness


def scatter_about(stream_key, dims, spread, limit, cuts=(), dtype=jnp.bfloat16):
    array = jax.random.normal(stream_key, dims, jnp.float32) * spread
    if len(cuts) > 0:
        array = shard_levels(stream_key, dims, cuts, -0.22, 0.18) * array
    return jnp.clip(array, min=-limit, max=limit).astype(dtype)


def setup_inputs(seed: int = 0, part: int = 0) -> dict:
    key_list = jax.random.split(jax.random.key(seed), 5)
    own_keys = jax.random.split(jax.random.fold_in(key_list[4], part), 5)
    return {
        "noise": scatter_about(own_keys[0], (NZ, NLAT, NLON), 1.0, 6.0, ((1, 4), (2, 4)), jnp.float32),
        "kappa2": jnp.clip(jnp.exp(math.log(0.3) - 2.3025852 * jax.random.uniform(key_list[1], (NZ, NLAT, NLON), jnp.float32) ** shard_levels(key_list[1], (NZ, NLAT, NLON), ((1, 4), (2, 4)), -0.2, 0.2)), 0.03, 0.3),
        "conduct": jnp.clip(jnp.exp(math.log(3.0) - 2.3025851 * jax.random.uniform(key_list[2], (3, NZ, NLAT, NLON), jnp.float32) ** shard_levels(key_list[2], (3, NZ, NLAT, NLON), ((2, 4), (3, 4)), -0.2, 0.2)), 0.3, 3.0),
        "land": set_ends((jax.random.randint(key_list[3], (NZ, NLAT, NLON), 0, 10) < 7).astype(jnp.int32), jax.random.fold_in(key_list[3], 1), 0, 1),
    }


base_kappa = 0.001
base_conduct = 1.0


def divergence_form(field, kappa2, conduct):
    east_face = conduct[0]
    row_index = jnp.arange(NLAT)
    north_face = jnp.where((row_index < NLAT - 1)[None, :, None], conduct[1], 0.0)
    level_index = jnp.arange(NZ)
    upper_face = jnp.where((level_index < NZ - 1)[:, None, None], conduct[2], 0.0)
    west_face = jnp.roll(east_face, 1, axis=2)
    zero_rows = jnp.zeros_like(field[:, :1])
    south_face = jnp.concatenate([zero_rows, north_face[:, :-1]], axis=1)
    zero_level = jnp.zeros_like(field[:1])
    lower_face = jnp.concatenate([zero_level, upper_face[:-1]], axis=0)
    east_value = jnp.roll(field, -1, axis=2)
    west_value = jnp.roll(field, 1, axis=2)
    north_value = jnp.concatenate([field[:, 1:], zero_rows], axis=1)
    south_value = jnp.concatenate([zero_rows, field[:, :-1]], axis=1)
    upper_value = jnp.concatenate([field[1:], zero_level], axis=0)
    lower_value = jnp.concatenate([zero_level, field[:-1]], axis=0)
    return (kappa2 * field + east_face * (field - east_value) + west_face * (field - west_value)
            + north_face * (field - north_value) + south_face * (field - south_value)
            + upper_face * (field - upper_value) + lower_face * (field - lower_value))


def operator(field, kappa2, conduct, ocean):
    first = divergence_form(ocean * field, kappa2, conduct)
    second = divergence_form(ocean * first, kappa2, conduct)
    return ocean * second + (1.0 - ocean) * field


def precondition(residual):
    length = NLON
    wave = jnp.arange(length // 2 + 1).astype(jnp.float32)
    symbol = base_kappa + base_conduct * (2.0 - 2.0 * jnp.cos(2.0 * math.pi * wave / length))
    factor = 1.0 / (symbol * symbol)
    spectrum = jnp.fft.rfft(residual, axis=2)
    return jnp.fft.irfft(spectrum * factor, n=length, axis=2)


def reference(noise, kappa2, conduct, land):
    ocean = land.astype(jnp.float32)
    solution = jnp.zeros_like(noise)
    residual = noise
    precond = precondition(residual)
    direction = precond
    energy = jnp.sum(residual * precond)
    for iteration in range(ITERS):
        image = operator(direction, kappa2, conduct, ocean)
        alpha = energy / jnp.sum(direction * image)
        solution = solution + alpha * direction
        residual = residual - alpha * image
        if iteration < ITERS - 1:
            precond = precondition(residual)
            renewed = jnp.sum(residual * precond)
            direction = precond + (renewed / energy) * direction
            energy = renewed
    return solution, residual
```

```python
import functools
import math

import jax
import jax.numpy as jnp
import numpy as np
from jax import lax
from jax.experimental import pallas as pl
from jax.experimental.pallas import tpu as pltpu
from jax.sharding import PartitionSpec as P

base_kappa = 0.001
base_conduct = 1.0

SCALE = 2.0**-31
REACH = 4
EDGE = 8

HIGHEST = lax.Precision.HIGHEST


def dot(a, b):
    return jnp.dot(a, b, precision=HIGHEST, preferred_element_type=jnp.float32)


def circle_kernel(total):
    middle = 2.0 + base_kappa / base_conduct
    rho = (middle - math.sqrt(middle * middle - 4.0)) / 2.0
    height = 1.0 / (1.0 / rho - rho) / base_conduct
    wrap = rho**total
    shift = (1.0 + rho * rho) / (1.0 - rho * rho) + total * wrap / (1.0 - wrap)
    front = height * height / (1.0 - wrap)
    return rho, front, shift


def circle_matrices(count, columns):
    total = count * columns
    rho, front, shift = circle_kernel(total)

    def one_side(n):
        return front * rho**n * (n + shift)

    def both_sides(n):
        return one_side(n) + one_side(total - n)

    place = np.arange(columns)
    rows = columns + 2 * EDGE
    x = np.arange(rows) - EDGE
    used = (x >= -2) & (x < columns + 2)
    near = both_sides(np.abs(x[:, None] - place[None, :])) * used[:, None]
    back = columns - 1 - place
    moments = np.zeros((8, columns))
    moments[0] = rho**place
    moments[1] = place * rho**place
    moments[2] = rho**back
    moments[3] = back * rho**back

    def block(offset):
        a = columns * offset - x
        b = total - columns * offset + x - (columns - 1)
        out = np.zeros((rows, 8))
        out[:, 0] = front * rho**a * (a + shift)
        out[:, 1] = front * rho**a
        out[:, 2] = front * rho**b * (b + shift)
        out[:, 3] = front * rho**b
        amend = both_sides(1) - both_sides(-1)
        if offset == 1:
            out[EDGE + columns + 1, 4] = amend
        if offset == count - 1:
            out[EDGE - 2, 4] += amend
        return out * used[:, None]

    others = [block(count - d) for d in range(2, count - 1)]
    far = np.stack(
        [
            np.concatenate([block(1), block(count - 1)] + others, axis=1),
            np.concatenate([block(count - 1), block(1)] + others, axis=1),
        ]
    )
    as_f32 = lambda m: np.asarray(m, np.float32)
    return as_f32(near), as_f32(moments), as_f32(far)


def pair_perms(count, wrap):
    first = [(i, i + 1) for i in range(0, count - 1, 2)]
    second = [(i, i + 1) for i in range(1, count - 1, 2)]
    if wrap:
        second.append((count - 1, 0))
    both = lambda pairs: pairs + [(j, i) for i, j in pairs]
    return both(first), both(second)


def whole(n):
    return [pl.BlockSpec(memory_space=pltpu.VMEM)] * n


def call(kernel, outs, *args, scratch=()):
    return pl.pallas_call(
        kernel,
        out_shape=[jax.ShapeDtypeStruct(s, jnp.float32) for s in outs],
        in_specs=whole(len(args)),
        out_specs=whole(len(outs)),
        scratch_shapes=[pltpu.VMEM(s, jnp.float32) for s in scratch],
    )(*args)


KINDS = 6


def band_kernel(rows, levels, noise, kappa2, conduct, land, first, second):
    odd = lax.axis_index("lat") % 2
    top = rows - REACH
    for out, start in ((first, (1 - odd) * top), (second, odd * top)):
        for kind in range(KINDS):
            for j in range(REACH):
                at = pl.ds(start + j, levels, stride=rows)
                if kind == 0:
                    plane = noise[at, :]
                elif kind == 1:
                    plane = land[at, :].astype(jnp.float32)
                elif kind == 2:
                    plane = conduct[1, at, :]
                elif kind == 3:
                    plane = kappa2[at, :]
                elif kind == 4:
                    plane = conduct[0, at, :]
                else:
                    plane = conduct[2, at, :]
                out[kind * REACH + j] = plane


def prepare_kernel(
    rows, levels, columns,
    noise, kappa2, conduct, land, got_first, got_second, weights,
    field, statics, to_first, to_second,
):
    lat_odd = lax.axis_index("lat") % 2
    last_band = lax.axis_index("lat") == lax.axis_size("lat") - 1
    lon_odd = lax.axis_index("lon") % 2
    lanes = (rows + 2 * REACH) * levels
    group = REACH * levels

    def ghost(kind, north):
        a = got_first[pl.ds(kind * REACH, REACH)].reshape(group, columns)
        b = got_second[pl.ds(kind * REACH, REACH)].reshape(group, columns)
        from_first = (lat_odd == 0) if north else (lat_odd == 1)
        return jnp.where(from_first, a, b)

    def turned(kind, load):
        blocks = [ghost(kind, False)]
        for j in range(0, rows, REACH):
            blocks.append(jnp.concatenate([load(pl.ds(j + i, levels, stride=rows)) for i in range(REACH)], axis=0))
        blocks.append(ghost(kind, True))
        return jnp.concatenate([b.T for b in blocks], axis=1)

    r = turned(0, lambda at: noise[at, :])
    field[...] = r
    ocean = turned(1, lambda at: land[at, :].astype(jnp.float32))
    north = turned(2, lambda at: conduct[1, at, :])
    kappa = turned(3, lambda at: kappa2[at, :])
    east = turned(4, lambda at: conduct[0, at, :])
    upper = turned(5, lambda at: conduct[2, at, :])
    lane = lax.broadcasted_iota(jnp.int32, (1, lanes), 1)
    top = (rows + REACH - 1) * levels
    ends = last_band & (lane >= top) & (lane < top + levels)
    north = jnp.where(ends, 0.0, north)
    upper = jnp.where(lane % levels == levels - 1, 0.0, upper)
    row = lax.broadcasted_iota(jnp.int32, (columns, 1), 0)
    west = jnp.where(row == 0, 0.0, pltpu.roll(east, 1, 0))
    ocean_east = jnp.where(row == columns - 1, 1.0, pltpu.roll(ocean, columns - 1, 0))
    diagonal = ocean * (
        kappa + east + west + north + pltpu.roll(north, levels, 1) + upper + pltpu.roll(upper, 1, 1)
    )
    to_east = east * ocean * ocean_east
    to_north = north * ocean * pltpu.roll(ocean, lanes - levels, 1)
    to_upper = upper * ocean * pltpu.roll(ocean, lanes - 1, 1)
    statics[0] = diagonal
    statics[1] = to_east
    statics[2] = to_north
    statics[3] = to_upper
    statics[4] = ocean
    statics[5] = east
    m = dot(weights[...], r)[:4]
    end = columns - 1
    blank = jnp.zeros((5, lanes), jnp.float32)
    for_east = [m, r[end:], diagonal[end:], to_east[end - 1 : end], east[end:], ocean[end:], to_north[end:], to_upper[end:], blank]
    for_west = [m, r[:1], diagonal[:1], to_east[:1], east[:1], ocean[:1], to_north[:1], to_upper[:1], blank]
    for_east = jnp.concatenate(for_east, axis=0)
    for_west = jnp.concatenate(for_west, axis=0)
    to_first[...] = jnp.where(lon_odd == 0, for_east, for_west)
    to_second[...] = jnp.where(lon_odd == 0, for_west, for_east)


def circle(near, far, own, received):
    lon_odd = lax.axis_index("lon") % 2
    told = jnp.concatenate([t[0:8] for t in received], axis=0)
    return dot(near[...], own) + dot(far[lon_odd], told)


def stencil(v, east_v, west_v, d, e, w, n, u, levels):
    lanes = v.shape[1]
    return (
        d * v
        - e * east_v
        - w * west_v
        - n * pltpu.roll(v, lanes - levels, 1)
        - pltpu.roll(n * v, levels, 1)
        - u * pltpu.roll(v, lanes - 1, 1)
        - pltpu.roll(u * v, 1, 1)
    )


def apply_twice(levels, columns, v, f, diagonal, to_east, north, upper, ocean, rim):
    own = pl.ds(EDGE, columns)
    after = pl.ds(EDGE + 1, columns)
    before = pl.ds(EDGE - 1, columns)
    end = EDGE + columns
    e, w = to_east[own], to_east[before]
    f[own] = stencil(v[own], v[after], v[before], diagonal[...], e, w, north, upper, levels)
    pick = lambda a, b: jnp.concatenate([v[a : a + 1], v[b : b + 1], jnp.zeros((6, v.shape[1]), jnp.float32)], axis=0)
    g = stencil(
        pick(EDGE - 1, end), pick(EDGE, end + 1), pick(EDGE - 2, end - 1),
        rim[0], rim[1], rim[2], rim[3], rim[4], levels,
    )
    f[EDGE - 1 : EDGE] = g[0:1]
    f[end : end + 1] = g[1:2]
    second = stencil(f[own], f[after], f[before], diagonal[...], e, w, north, upper, levels)
    return jnp.where(ocean > 0.5, second, v[own])


def first_kernel(
    levels, columns, others,
    field, statics, near, far, weights, mine_first, mine_second, *rest,
):
    received = rest[: 2 + others]
    precond, image, diagonal, to_east, rim, to_first, to_second, v, f = rest[2 + others :]
    lon_odd = lax.axis_index("lon") % 2
    even = lon_odd == 0
    a, b = received[0][...], received[1][...]
    east_list = jnp.where(even, a, b)
    west_list = jnp.where(even, b, a)
    v[...] = circle(near, far, field[...], received)
    ocean = statics[4]
    end = columns - 1
    row = lax.broadcasted_iota(jnp.int32, (columns, 1), 0)
    full_east = jnp.where(row == end, statics[1] * east_list[8:9], statics[1])
    to_east[pl.ds(EDGE, columns)] = full_east
    face_west = west_list[7:8] * west_list[8:9] * ocean[0:1]
    to_east[EDGE - 1 : EDGE] = face_west
    diagonal[...] = statics[0] + jnp.where(row == 0, ocean * west_list[7:8], 0.0)
    blank = jnp.zeros((6, ocean.shape[1]), jnp.float32)
    stack = lambda p, q: jnp.concatenate([p, q, blank], axis=0)
    rim[0] = stack(west_list[5:6], east_list[5:6] + east_list[8:9] * statics[5, end:])
    rim[1] = stack(face_west, east_list[6:7])
    rim[2] = stack(west_list[6:7], full_east[end:])
    rim[3] = stack(west_list[9:10], east_list[9:10])
    rim[4] = stack(west_list[10:11], east_list[10:11])
    w0 = apply_twice(levels, columns, v, f, diagonal, to_east, statics[2], statics[3], ocean, rim)
    precond[...] = v[pl.ds(EDGE, columns)]
    image[...] = w0
    scaled = w0 * SCALE
    m = dot(weights[...], scaled)[:4]
    pad = jnp.zeros((3, m.shape[1]), jnp.float32)
    for_east = jnp.concatenate([m, scaled[end:], pad], axis=0)
    for_west = jnp.concatenate([m, scaled[:1], pad], axis=0)
    to_first[...] = jnp.where(even, for_east, for_west)
    to_second[...] = jnp.where(even, for_west, for_east)


def second_kernel(
    levels, columns, rows, others,
    field, precond, image, statics, near, far, diagonal, to_east, rim, *rest,
):
    received = rest[: 2 + others]
    again, along, sums, v, f = rest[2 + others :]
    v[...] = circle(near, far, image[...] * SCALE, received)
    out = apply_twice(levels, columns, v, f, diagonal, to_east, statics[2], statics[3], statics[4], rim)
    own = slice(REACH * levels, (REACH + rows) * levels)
    again[...] = v[pl.ds(EDGE, columns)][:, own]
    along[...] = out[:, own]
    r, p, w = field[:, own], precond[:, own], image[:, own]
    q, z = again[...], along[...]

    def part(x):
        s = jnp.sum(x, axis=0, keepdims=True)
        return sum(s[:, k : k + 128] for k in range(0, s.shape[1], 128))

    parts = [part(r * p), part(p * w), part(w * q), part(q * z), jnp.zeros((4, 128), jnp.float32)]
    sums[...] = jnp.concatenate(parts, axis=0)


def combine_kernel(rows, levels, sums, noise, precond, image, again, along, answer, left):
    total = jnp.sum(sums[...], axis=1, keepdims=True)
    energy, curve, mixed, last = total[0:1], total[1:2], total[2:3], total[3:4]
    alpha = energy / curve
    beta = alpha / SCALE
    growth = alpha * beta * mixed / energy
    step = energy * (growth - 1.0) / (beta * beta * last - growth * growth * curve)
    keep = alpha + step * growth
    back = step * beta
    own = slice(REACH * levels, (REACH + rows) * levels)
    x = keep * precond[:, own] - back * again[...]
    y = keep * image[:, own] - back * along[...]
    group = REACH * levels
    for j in range(0, rows, REACH):
        at = slice(j * levels, j * levels + group)
        xt, yt = x[:, at].T, y[:, at].T
        for i in range(REACH):
            part = slice(i * levels, (i + 1) * levels)
            to = pl.ds(j + i, levels, stride=rows)
            answer[to, :] = xt[part]
            left[to, :] = noise[to, :] - yt[part]


def summed(x, axis):
    count = lax.axis_size(axis)
    step = 1
    while step < count:
        x = x + lax.ppermute(x, axis, [(i, i ^ step) for i in range(count)])
        step *= 2
    return x


def body(near, weights, far, noise, kappa2, conduct, land):
    levels, rows, columns = noise.shape
    count = lax.axis_size("lon")
    others = count - 3
    flat = levels * rows
    lanes = (rows + 2 * REACH) * levels
    tall = columns + 2 * EDGE
    noise = noise.reshape(flat, columns)
    kappa2 = kappa2.reshape(flat, columns)
    land = land.reshape(flat, columns)
    conduct = conduct.reshape(3, flat, columns)

    planes = (KINDS * REACH, levels, columns)
    first, second = call(functools.partial(band_kernel, rows, levels), [planes, planes], noise, kappa2, conduct, land)
    perm_a, perm_b = pair_perms(lax.axis_size("lat"), False)
    got_first = lax.ppermute(first, "lat", perm_a)
    got_second = lax.ppermute(second, "lat", perm_b)

    field, statics, to_first, to_second = call(
        functools.partial(prepare_kernel, rows, levels, columns),
        [(columns, lanes), (6, columns, lanes), (16, lanes), (16, lanes)],
        noise, kappa2, conduct, land, got_first, got_second, weights,
    )
    lon_a, lon_b = pair_perms(count, True)

    def exchange(one, two):
        got = [lax.ppermute(one, "lon", lon_a), lax.ppermute(two, "lon", lon_b)]
        for d in range(2, count - 1):
            got.append(lax.ppermute(one[:8], "lon", [(i, (i + d) % count) for i in range(count)]))
        return got

    told = exchange(to_first, to_second)
    precond, image, diagonal, to_east, rim, to_first2, to_second2 = call(
        functools.partial(first_kernel, levels, columns, others),
        [(columns, lanes), (columns, lanes), (columns, lanes), (tall, lanes), (5, 8, lanes), (8, lanes), (8, lanes)],
        field, statics, near, far, weights, to_first, to_second, *told,
        scratch=[(tall, lanes), (tall, lanes)],
    )
    told = exchange(to_first2, to_second2)
    again, along, sums = call(
        functools.partial(second_kernel, levels, columns, rows, others),
        [(columns, flat), (columns, flat), (8, 128)],
        field, precond, image, statics, near, far, diagonal, to_east, rim, *told,
        scratch=[(tall, lanes), (tall, lanes)],
    )
    sums = summed(summed(sums, "lon"), "lat")
    answer, left = call(
        functools.partial(combine_kernel, rows, levels),
        [(flat, columns), (flat, columns)],
        sums, noise, precond, image, again, along,
    )
    return answer.reshape(levels, rows, columns), left.reshape(levels, rows, columns)


def solution(mesh):
    def run(noise, kappa2, conduct, land):
        count = mesh.shape["lon"]
        near, weights, far = circle_matrices(count, noise.shape[2] // count)
        return jax.shard_map(
            functools.partial(body, near, weights, far),
            mesh=mesh,
            in_specs=(
                P("ens", "lat", "lon"),
                P(None, "lat", "lon"),
                P(None, None, "lat", "lon"),
                P(None, "lat", "lon"),
            ),
            out_specs=(P("ens", "lat", "lon"), P("ens", "lat", "lon")),
            check_vma=False,
        )(noise, kappa2, conduct, land)

    return run
```

```python
import functools
import math

import jax
import jax.numpy as jnp
import numpy as np
from jax import lax
from jax.experimental import pallas as pl
from jax.experimental.pallas import tpu as pltpu
from jax.sharding import PartitionSpec as P

base_kappa = 0.001
base_conduct = 1.0

SCALE = 2.0**-31
REACH = 4
EDGE = 8

HIGHEST = lax.Precision.HIGHEST


def dot(a, b):
    return jnp.dot(a, b, precision=HIGHEST, preferred_element_type=jnp.float32)


def circle_kernel(total):
    middle = 2.0 + base_kappa / base_conduct
    rho = (middle - math.sqrt(middle * middle - 4.0)) / 2.0
    height = 1.0 / (1.0 / rho - rho) / base_conduct
    wrap = rho**total
    shift = (1.0 + rho * rho) / (1.0 - rho * rho) + total * wrap / (1.0 - wrap)
    front = height * height / (1.0 - wrap)
    return rho, front, shift


def circle_matrices(count, columns):
    total = count * columns
    rho, front, shift = circle_kernel(total)

    def one_side(n):
        return front * rho**n * (n + shift)

    def both_sides(n):
        return one_side(n) + one_side(total - n)

    place = np.arange(columns)
    rows = columns + 2 * EDGE
    x = np.arange(rows) - EDGE
    used = (x >= -2) & (x < columns + 2)
    near = both_sides(np.abs(x[:, None] - place[None, :])) * used[:, None]
    back = columns - 1 - place
    moments = np.zeros((8, columns))
    moments[0] = rho**place
    moments[1] = place * rho**place
    moments[2] = rho**back
    moments[3] = back * rho**back

    def block(offset):
        a = columns * offset - x
        b = total - columns * offset + x - (columns - 1)
        out = np.zeros((rows, 8))
        out[:, 0] = front * rho**a * (a + shift)
        out[:, 1] = front * rho**a
        out[:, 2] = front * rho**b * (b + shift)
        out[:, 3] = front * rho**b
        amend = both_sides(1) - both_sides(-1)
        if offset == 1:
            out[EDGE + columns + 1, 4] = amend
        if offset == count - 1:
            out[EDGE - 2, 4] += amend
        return out * used[:, None]

    others = [block(count - d) for d in range(2, count - 1)]
    far = np.stack(
        [
            np.concatenate([block(1), block(count - 1)] + others, axis=1),
            np.concatenate([block(count - 1), block(1)] + others, axis=1),
        ]
    )
    as_f32 = lambda m: np.asarray(m, np.float32)
    return as_f32(near), as_f32(moments), as_f32(far)


def pair_perms(count, wrap):
    first = [(i, i + 1) for i in range(0, count - 1, 2)]
    second = [(i, i + 1) for i in range(1, count - 1, 2)]
    if wrap:
        second.append((count - 1, 0))
    both = lambda pairs: pairs + [(j, i) for i, j in pairs]
    return both(first), both(second)


def whole(n):
    return [pl.BlockSpec(memory_space=pltpu.VMEM)] * n


def call(kernel, outs, *args, near_memory=(), scratch=(), last=False):
    args = [pltpu.with_memory_space_constraint(a, pltpu.VMEM) if k in near_memory else a for k, a in enumerate(args)]
    kind = jax.ShapeDtypeStruct if last else pltpu.VMEM
    return pl.pallas_call(
        kernel,
        out_shape=[kind(s, jnp.float32) for s in outs],
        in_specs=whole(len(args)),
        out_specs=whole(len(outs)),
        scratch_shapes=[pltpu.VMEM(s, jnp.float32) for s in scratch],
        compiler_params=pltpu.CompilerParams(vmem_limit_bytes=24 << 20),
    )(*args)


KINDS = 6


def band_kernel(rows, levels, noise, kappa2, conduct, land, first, second):
    odd = lax.axis_index("lat") % 2
    top = rows - REACH
    for out, start in ((first, (1 - odd) * top), (second, odd * top)):
        for kind in range(KINDS):
            for j in range(REACH):
                at = pl.ds(start + j, levels, stride=rows)
                if kind == 0:
                    plane = noise[at, :]
                elif kind == 1:
                    plane = land[at, :].astype(jnp.float32)
                elif kind == 2:
                    plane = conduct[1, at, :]
                elif kind == 3:
                    plane = kappa2[at, :]
                elif kind == 4:
                    plane = conduct[0, at, :]
                else:
                    plane = conduct[2, at, :]
                out[kind * REACH + j] = plane


def prepare_kernel(
    rows, levels, columns,
    noise, kappa2, conduct, land, got_first, got_second, weights,
    field, statics, to_first, to_second, to_others,
):
    lat_odd = lax.axis_index("lat") % 2
    last_band = lax.axis_index("lat") == lax.axis_size("lat") - 1
    lon_odd = lax.axis_index("lon") % 2
    lanes = (rows + 2 * REACH) * levels
    group = REACH * levels

    def ghost(kind, north):
        a = got_first[pl.ds(kind * REACH, REACH)].reshape(group, columns)
        b = got_second[pl.ds(kind * REACH, REACH)].reshape(group, columns)
        from_first = (lat_odd == 0) if north else (lat_odd == 1)
        return jnp.where(from_first, a, b)

    def turned(kind, load):
        blocks = [ghost(kind, False)]
        for j in range(0, rows, REACH):
            blocks.append(jnp.concatenate([load(pl.ds(j + i, levels, stride=rows)) for i in range(REACH)], axis=0))
        blocks.append(ghost(kind, True))
        return jnp.concatenate([b.T for b in blocks], axis=1)

    r = turned(0, lambda at: noise[at, :])
    field[...] = r
    ocean = turned(1, lambda at: land[at, :].astype(jnp.float32))
    north = turned(2, lambda at: conduct[1, at, :])
    kappa = turned(3, lambda at: kappa2[at, :])
    east = turned(4, lambda at: conduct[0, at, :])
    upper = turned(5, lambda at: conduct[2, at, :])
    lane = lax.broadcasted_iota(jnp.int32, (1, lanes), 1)
    top = (rows + REACH - 1) * levels
    ends = last_band & (lane >= top) & (lane < top + levels)
    north = jnp.where(ends, 0.0, north)
    upper = jnp.where(lane % levels == levels - 1, 0.0, upper)
    row = lax.broadcasted_iota(jnp.int32, (columns, 1), 0)
    west = jnp.where(row == 0, 0.0, pltpu.roll(east, 1, 0))
    ocean_east = jnp.where(row == columns - 1, 1.0, pltpu.roll(ocean, columns - 1, 0))
    diagonal = ocean * (
        kappa + east + west + north + pltpu.roll(north, levels, 1) + upper + pltpu.roll(upper, 1, 1)
    )
    to_east = east * ocean * ocean_east
    to_north = north * ocean * pltpu.roll(ocean, lanes - levels, 1)
    to_upper = upper * ocean * pltpu.roll(ocean, lanes - 1, 1)
    statics[0] = diagonal
    statics[1] = to_east
    statics[2] = to_north
    statics[3] = to_upper
    statics[4] = ocean
    statics[5] = east
    m = dot(weights[...], r)
    to_others[...] = m
    m = m[:4]
    end = columns - 1
    blank = jnp.zeros((5, lanes), jnp.float32)
    for_east = [m, r[end:], diagonal[end:], to_east[end - 1 : end], east[end:], ocean[end:], to_north[end:], to_upper[end:], blank]
    for_west = [m, r[:1], diagonal[:1], to_east[:1], east[:1], ocean[:1], to_north[:1], to_upper[:1], blank]
    for_east = jnp.concatenate(for_east, axis=0)
    for_west = jnp.concatenate(for_west, axis=0)
    to_first[...] = jnp.where(lon_odd == 0, for_east, for_west)
    to_second[...] = jnp.where(lon_odd == 0, for_west, for_east)


def circle(near, far, own, received):
    lon_odd = lax.axis_index("lon") % 2
    told = jnp.concatenate([t[0:8] for t in received], axis=0)
    return dot(near[...], own) + dot(far[lon_odd], told)


def stencil(v, east_v, west_v, d, e, w, n, u, levels):
    lanes = v.shape[1]
    return (
        d * v
        - e * east_v
        - w * west_v
        - n * pltpu.roll(v, lanes - levels, 1)
        - pltpu.roll(n * v, levels, 1)
        - u * pltpu.roll(v, lanes - 1, 1)
        - pltpu.roll(u * v, 1, 1)
    )


def apply_twice(levels, columns, v, f, diagonal, to_east, north, upper, ocean, rim):
    own = pl.ds(EDGE, columns)
    after = pl.ds(EDGE + 1, columns)
    before = pl.ds(EDGE - 1, columns)
    end = EDGE + columns
    e, w = to_east[own], to_east[before]
    f[own] = stencil(v[own], v[after], v[before], diagonal[...], e, w, north, upper, levels)
    pick = lambda a, b: jnp.concatenate([v[a : a + 1], v[b : b + 1], jnp.zeros((6, v.shape[1]), jnp.float32)], axis=0)
    g = stencil(
        pick(EDGE - 1, end), pick(EDGE, end + 1), pick(EDGE - 2, end - 1),
        rim[0], rim[1], rim[2], rim[3], rim[4], levels,
    )
    f[EDGE - 1 : EDGE] = g[0:1]
    f[end : end + 1] = g[1:2]
    second = stencil(f[own], f[after], f[before], diagonal[...], e, w, north, upper, levels)
    return jnp.where(ocean > 0.5, second, v[own])


def first_kernel(
    levels, columns, others,
    field, statics, near, far, weights, mine_first, mine_second, *rest,
):
    received = rest[: 2 + others]
    precond, image, diagonal, to_east, rim, to_first, to_second, v, f = rest[2 + others :]
    lon_odd = lax.axis_index("lon") % 2
    even = lon_odd == 0
    a, b = received[0][...], received[1][...]
    east_list = jnp.where(even, a, b)
    west_list = jnp.where(even, b, a)
    v[...] = circle(near, far, field[...], received)
    ocean = statics[4]
    end = columns - 1
    row = lax.broadcasted_iota(jnp.int32, (columns, 1), 0)
    full_east = jnp.where(row == end, statics[1] * east_list[8:9], statics[1])
    to_east[pl.ds(EDGE, columns)] = full_east
    face_west = west_list[7:8] * west_list[8:9] * ocean[0:1]
    to_east[EDGE - 1 : EDGE] = face_west
    diagonal[...] = statics[0] + jnp.where(row == 0, ocean * west_list[7:8], 0.0)
    blank = jnp.zeros((6, ocean.shape[1]), jnp.float32)
    stack = lambda p, q: jnp.concatenate([p, q, blank], axis=0)
    rim[0] = stack(west_list[5:6], east_list[5:6] + east_list[8:9] * statics[5, end:])
    rim[1] = stack(face_west, east_list[6:7])
    rim[2] = stack(west_list[6:7], full_east[end:])
    rim[3] = stack(west_list[9:10], east_list[9:10])
    rim[4] = stack(west_list[10:11], east_list[10:11])
    w0 = apply_twice(levels, columns, v, f, diagonal, to_east, statics[2], statics[3], ocean, rim)
    precond[...] = v[pl.ds(EDGE, columns)]
    image[...] = w0
    scaled = w0 * SCALE
    m = dot(weights[...], scaled)[:4]
    pad = jnp.zeros((3, m.shape[1]), jnp.float32)
    for_east = jnp.concatenate([m, scaled[end:], pad], axis=0)
    for_west = jnp.concatenate([m, scaled[:1], pad], axis=0)
    to_first[...] = jnp.where(even, for_east, for_west)
    to_second[...] = jnp.where(even, for_west, for_east)


def second_kernel(
    levels, columns, rows, others,
    field, precond, image, statics, near, far, diagonal, to_east, rim, *rest,
):
    received = rest[: 2 + others]
    again, along, sums, v, f = rest[2 + others :]
    v[...] = circle(near, far, image[...] * SCALE, received)
    out = apply_twice(levels, columns, v, f, diagonal, to_east, statics[2], statics[3], statics[4], rim)
    own = slice(REACH * levels, (REACH + rows) * levels)
    again[...] = v[pl.ds(EDGE, columns)][:, own]
    along[...] = out[:, own]
    r, p, w = field[:, own], precond[:, own], image[:, own]
    q, z = again[...], along[...]

    def part(x):
        s = jnp.sum(x, axis=0, keepdims=True)
        return sum(s[:, k : k + 128] for k in range(0, s.shape[1], 128))

    parts = [part(r * p), part(p * w), part(w * q), part(q * z), jnp.zeros((4, 128), jnp.float32)]
    sums[...] = jnp.concatenate(parts, axis=0)


def combine_kernel(rows, levels, sums, noise, precond, image, again, along, answer, left):
    total = jnp.sum(sums[...], axis=1, keepdims=True)
    energy, curve, mixed, last = total[0:1], total[1:2], total[2:3], total[3:4]
    alpha = energy / curve
    beta = alpha / SCALE
    growth = alpha * beta * mixed / energy
    step = energy * (growth - 1.0) / (beta * beta * last - growth * growth * curve)
    keep = alpha + step * growth
    back = step * beta
    own = slice(REACH * levels, (REACH + rows) * levels)
    x = keep * precond[:, own] - back * again[...]
    y = keep * image[:, own] - back * along[...]
    group = REACH * levels
    for j in range(0, rows, REACH):
        at = slice(j * levels, j * levels + group)
        xt, yt = x[:, at].T, y[:, at].T
        for i in range(REACH):
            part = slice(i * levels, (i + 1) * levels)
            to = pl.ds(j + i, levels, stride=rows)
            answer[to, :] = xt[part]
            left[to, :] = noise[to, :] - yt[part]


def summed(x, axis):
    count = lax.axis_size(axis)
    step = 1
    while step < count:
        x = x + lax.ppermute(x, axis, [(i, i ^ step) for i in range(count)])
        step *= 2
    return x


def body(near, weights, far, noise, kappa2, conduct, land):
    levels, rows, columns = noise.shape
    count = lax.axis_size("lon")
    others = count - 3
    flat = levels * rows
    lanes = (rows + 2 * REACH) * levels
    tall = columns + 2 * EDGE
    noise = noise.reshape(flat, columns)
    kappa2 = kappa2.reshape(flat, columns)
    land = land.reshape(flat, columns)
    conduct = conduct.reshape(3, flat, columns)

    planes = (KINDS * REACH, levels, columns)
    first, second = call(functools.partial(band_kernel, rows, levels), [planes, planes], noise, kappa2, conduct, land)
    perm_a, perm_b = pair_perms(lax.axis_size("lat"), False)
    got_first = lax.ppermute(first, "lat", perm_a)
    got_second = lax.ppermute(second, "lat", perm_b)

    field, statics, to_first, to_second, to_others = call(
        functools.partial(prepare_kernel, rows, levels, columns),
        [(columns, lanes), (6, columns, lanes), (16, lanes), (16, lanes), (8, lanes)],
        noise, kappa2, conduct, land, got_first, got_second, weights, near_memory=(4, 5),
    )
    lon_a, lon_b = pair_perms(count, True)

    def exchange(one, two, rest):
        got = [lax.ppermute(one, "lon", lon_a), lax.ppermute(two, "lon", lon_b)]
        for d in range(2, count - 1):
            got.append(lax.ppermute(rest, "lon", [(i, (i + d) % count) for i in range(count)]))
        return got

    told = exchange(to_first, to_second, to_others)
    precond, image, diagonal, to_east, rim, to_first2, to_second2 = call(
        functools.partial(first_kernel, levels, columns, others),
        [(columns, lanes), (columns, lanes), (columns, lanes), (tall, lanes), (5, 8, lanes), (8, lanes), (8, lanes)],
        field, statics, near, far, weights, to_first, to_second, *told, near_memory=(0, 1, 5, 6, *range(7, 9 + others)),
        scratch=[(tall, lanes), (tall, lanes)],
    )
    told = exchange(to_first2, to_second2, to_first2)
    again, along, sums = call(
        functools.partial(second_kernel, levels, columns, rows, others),
        [(columns, flat), (columns, flat), (8, 128)],
        field, precond, image, statics, near, far, diagonal, to_east, rim, *told,
        near_memory=(0, 1, 2, 3, 6, 7, 8, *range(9, 11 + others)),
        scratch=[(tall, lanes), (tall, lanes)],
    )
    sums = summed(summed(sums, "lon"), "lat")
    answer, left = call(
        functools.partial(combine_kernel, rows, levels),
        [(flat, columns), (flat, columns)],
        sums, noise, precond, image, again, along, near_memory=(0, 2, 3, 4, 5), last=True,
    )
    return answer.reshape(levels, rows, columns), left.reshape(levels, rows, columns)


def solution(mesh):
    def run(noise, kappa2, conduct, land):
        count = mesh.shape["lon"]
        near, weights, far = circle_matrices(count, noise.shape[2] // count)
        return jax.shard_map(
            functools.partial(body, near, weights, far),
            mesh=mesh,
            in_specs=(
                P("ens", "lat", "lon"),
                P(None, "lat", "lon"),
                P(None, None, "lat", "lon"),
                P(None, "lat", "lon"),
            ),
            out_specs=(P("ens", "lat", "lon"), P("ens", "lat", "lon")),
            check_vma=False,
        )(noise, kappa2, conduct, land)

    return run
```

```python
import functools
import math

import jax
import jax.numpy as jnp
import numpy as np
from jax import lax
from jax.experimental import pallas as pl
from jax.experimental.pallas import tpu as pltpu
from jax.sharding import PartitionSpec as P

base_kappa = 0.001
base_conduct = 1.0

SCALE = 2.0**-31
REACH = 4
EDGE = 8

HIGHEST = lax.Precision.HIGHEST


def dot(a, b):
    return jnp.dot(a, b, precision=HIGHEST, preferred_element_type=jnp.float32)


def circle_kernel(total):
    middle = 2.0 + base_kappa / base_conduct
    rho = (middle - math.sqrt(middle * middle - 4.0)) / 2.0
    height = 1.0 / (1.0 / rho - rho) / base_conduct
    wrap = rho**total
    shift = (1.0 + rho * rho) / (1.0 - rho * rho) + total * wrap / (1.0 - wrap)
    front = height * height / (1.0 - wrap)
    return rho, front, shift


def circle_matrices(count, columns):
    total = count * columns
    rho, front, shift = circle_kernel(total)

    def one_side(n):
        return front * rho**n * (n + shift)

    def both_sides(n):
        return one_side(n) + one_side(total - n)

    place = np.arange(columns)
    rows = columns + 2 * EDGE
    x = np.arange(rows) - EDGE
    used = (x >= -2) & (x < columns + 2)
    near = both_sides(np.abs(x[:, None] - place[None, :])) * used[:, None]
    back = columns - 1 - place
    moments = np.zeros((8, columns))
    moments[0] = rho**place
    moments[1] = place * rho**place
    moments[2] = rho**back
    moments[3] = back * rho**back

    def block(offset):
        a = columns * offset - x
        b = total - columns * offset + x - (columns - 1)
        out = np.zeros((rows, 8))
        out[:, 0] = front * rho**a * (a + shift)
        out[:, 1] = front * rho**a
        out[:, 2] = front * rho**b * (b + shift)
        out[:, 3] = front * rho**b
        amend = both_sides(1) - both_sides(-1)
        if offset == 1:
            out[EDGE + columns + 1, 4] = amend
        if offset == count - 1:
            out[EDGE - 2, 4] += amend
        return out * used[:, None]

    others = [block(count - d) for d in range(2, count - 1)]
    far = np.stack(
        [
            np.concatenate([block(1), block(count - 1)] + others, axis=1),
            np.concatenate([block(count - 1), block(1)] + others, axis=1),
        ]
    )
    as_f32 = lambda m: np.asarray(m, np.float32)
    return as_f32(near), as_f32(moments), as_f32(far)


def pair_perms(count, wrap):
    first = [(i, i + 1) for i in range(0, count - 1, 2)]
    second = [(i, i + 1) for i in range(1, count - 1, 2)]
    if wrap:
        second.append((count - 1, 0))
    both = lambda pairs: pairs + [(j, i) for i, j in pairs]
    return both(first), both(second)


def whole(n):
    return [pl.BlockSpec(memory_space=pltpu.VMEM)] * n


def call(kernel, outs, *args, near_memory=(), scratch=(), last=False):
    args = [pltpu.with_memory_space_constraint(a, pltpu.VMEM) if k in near_memory else a for k, a in enumerate(args)]
    kind = jax.ShapeDtypeStruct if last else pltpu.VMEM
    return pl.pallas_call(
        kernel,
        out_shape=[kind(s, jnp.float32) for s in outs],
        in_specs=whole(len(args)),
        out_specs=whole(len(outs)),
        scratch_shapes=[pltpu.VMEM(s, jnp.float32) for s in scratch],
        compiler_params=pltpu.CompilerParams(vmem_limit_bytes=24 << 20),
    )(*args)


FULL, PART = REACH, REACH - 1
PLANES = 3 * FULL + 3 * PART


def band_kernel(rows, levels, *refs):
    sources, (second, first), copies, sems = refs[:7], refs[7:9], refs[9:16], refs[16]
    moves = [pltpu.make_async_copy(x, y, sems.at[k]) for k, (x, y) in enumerate(zip(sources, copies))]
    for move in moves:
        move.start()
    for move in moves:
        move.wait()
    noise, kappa2, conduct, land = copies[:4]
    odd = lax.axis_index("lat") % 2
    top = rows - REACH
    loads = (
        lambda at: noise[at, :],
        lambda at: land[at, :].astype(jnp.float32),
        lambda at: conduct[1, at, :],
        lambda at: kappa2[at, :],
        lambda at: conduct[0, at, :],
        lambda at: conduct[2, at, :],
    )
    for out, side in ((first, odd), (second, 1 - odd)):
        k = 0
        for kind, load in enumerate(loads):
            count = FULL if kind < 3 else PART
            start = (1 - side) * (rows - count)
            for j in range(count):
                out[k] = load(pl.ds(start + j, levels, stride=rows))
                k += 1


def prepare_kernel(
    rows, levels, columns,
    noise, kappa2, conduct, land, got_second, got_first, weights,
    field, statics, to_first, to_second, to_others,
):
    lat_odd = lax.axis_index("lat") % 2
    last_band = lax.axis_index("lat") == lax.axis_size("lat") - 1
    lon_odd = lax.axis_index("lon") % 2
    lanes = (rows + 2 * REACH) * levels
    group = REACH * levels

    def ghost(kind, north):
        count = FULL if kind < 3 else PART
        k = kind * FULL if kind < 3 else 3 * FULL + (kind - 3) * PART
        a = got_first[pl.ds(k, count)].reshape(count * levels, columns)
        b = got_second[pl.ds(k, count)].reshape(count * levels, columns)
        from_first = (lat_odd == 0) if north else (lat_odd == 1)
        planes = jnp.where(from_first, a, b)
        if count == REACH:
            return planes
        blank = jnp.zeros((group - count * levels, columns), jnp.float32)
        return jnp.concatenate([planes, blank] if north else [blank, planes], axis=0)

    def turned(kind, load):
        blocks = [ghost(kind, False)]
        for j in range(0, rows, REACH):
            blocks.append(jnp.concatenate([load(pl.ds(j + i, levels, stride=rows)) for i in range(REACH)], axis=0))
        blocks.append(ghost(kind, True))
        return jnp.concatenate([b.T for b in blocks], axis=1)

    r = turned(0, lambda at: noise[at, :])
    field[...] = r
    ocean = turned(1, lambda at: land[at, :].astype(jnp.float32))
    north = turned(2, lambda at: conduct[1, at, :])
    kappa = turned(3, lambda at: kappa2[at, :])
    east = turned(4, lambda at: conduct[0, at, :])
    upper = turned(5, lambda at: conduct[2, at, :])
    lane = lax.broadcasted_iota(jnp.int32, (1, lanes), 1)
    top = (rows + REACH - 1) * levels
    ends = last_band & (lane >= top) & (lane < top + levels)
    north = jnp.where(ends, 0.0, north)
    upper = jnp.where(lane % levels == levels - 1, 0.0, upper)
    row = lax.broadcasted_iota(jnp.int32, (columns, 1), 0)
    west = jnp.where(row == 0, 0.0, pltpu.roll(east, 1, 0))
    ocean_east = jnp.where(row == columns - 1, 1.0, pltpu.roll(ocean, columns - 1, 0))
    diagonal = ocean * (
        kappa + east + west + north + pltpu.roll(north, levels, 1) + upper + pltpu.roll(upper, 1, 1)
    )
    to_east = east * ocean * ocean_east
    to_north = north * ocean * pltpu.roll(ocean, lanes - levels, 1)
    to_upper = upper * ocean * pltpu.roll(ocean, lanes - 1, 1)
    statics[0] = diagonal
    statics[1] = to_east
    statics[2] = to_north
    statics[3] = to_upper
    statics[4] = ocean
    statics[5] = east
    m = dot(weights[...], r)
    to_others[...] = m
    m = m[:4]
    end = columns - 1
    blank = jnp.zeros((5, lanes), jnp.float32)
    for_east = [m, r[end:], diagonal[end:], to_east[end - 1 : end], east[end:], ocean[end:], to_north[end:], to_upper[end:], blank]
    for_west = [m, r[:1], diagonal[:1], to_east[:1], east[:1], ocean[:1], to_north[:1], to_upper[:1], blank]
    for_east = jnp.concatenate(for_east, axis=0)
    for_west = jnp.concatenate(for_west, axis=0)
    to_first[...] = jnp.where(lon_odd == 0, for_east, for_west)
    to_second[...] = jnp.where(lon_odd == 0, for_west, for_east)


def circle(near, far, own, received):
    lon_odd = lax.axis_index("lon") % 2
    told = jnp.concatenate([t[0:8] for t in received], axis=0)
    return dot(near[...], own) + dot(far[lon_odd], told)


def stencil(v, east_v, west_v, d, e, w, n, u, levels):
    lanes = v.shape[1]
    return (
        d * v
        - e * east_v
        - w * west_v
        - n * pltpu.roll(v, lanes - levels, 1)
        - pltpu.roll(n * v, levels, 1)
        - u * pltpu.roll(v, lanes - 1, 1)
        - pltpu.roll(u * v, 1, 1)
    )


def apply_twice(levels, columns, v, f, diagonal, to_east, north, upper, ocean, rim):
    own = pl.ds(EDGE, columns)
    after = pl.ds(EDGE + 1, columns)
    before = pl.ds(EDGE - 1, columns)
    end = EDGE + columns
    e, w = to_east[own], to_east[before]
    f[own] = stencil(v[own], v[after], v[before], diagonal[...], e, w, north, upper, levels)
    pick = lambda a, b: jnp.concatenate([v[a : a + 1], v[b : b + 1], jnp.zeros((6, v.shape[1]), jnp.float32)], axis=0)
    g = stencil(
        pick(EDGE - 1, end), pick(EDGE, end + 1), pick(EDGE - 2, end - 1),
        rim[0], rim[1], rim[2], rim[3], rim[4], levels,
    )
    f[EDGE - 1 : EDGE] = g[0:1]
    f[end : end + 1] = g[1:2]
    second = stencil(f[own], f[after], f[before], diagonal[...], e, w, north, upper, levels)
    return jnp.where(ocean > 0.5, second, v[own])


def first_kernel(
    levels, columns, others,
    field, statics, near, far, weights, mine_first, mine_second, *rest,
):
    received = rest[: 2 + others]
    precond, image, diagonal, to_east, rim, to_first, to_second, v, f = rest[2 + others :]
    lon_odd = lax.axis_index("lon") % 2
    even = lon_odd == 0
    a, b = received[0][...], received[1][...]
    east_list = jnp.where(even, a, b)
    west_list = jnp.where(even, b, a)
    v[...] = circle(near, far, field[...], received)
    ocean = statics[4]
    end = columns - 1
    row = lax.broadcasted_iota(jnp.int32, (columns, 1), 0)
    full_east = jnp.where(row == end, statics[1] * east_list[8:9], statics[1])
    to_east[pl.ds(EDGE, columns)] = full_east
    face_west = west_list[7:8] * west_list[8:9] * ocean[0:1]
    to_east[EDGE - 1 : EDGE] = face_west
    diagonal[...] = statics[0] + jnp.where(row == 0, ocean * west_list[7:8], 0.0)
    blank = jnp.zeros((6, ocean.shape[1]), jnp.float32)
    stack = lambda p, q: jnp.concatenate([p, q, blank], axis=0)
    rim[0] = stack(west_list[5:6], east_list[5:6] + east_list[8:9] * statics[5, end:])
    rim[1] = stack(face_west, east_list[6:7])
    rim[2] = stack(west_list[6:7], full_east[end:])
    rim[3] = stack(west_list[9:10], east_list[9:10])
    rim[4] = stack(west_list[10:11], east_list[10:11])
    w0 = apply_twice(levels, columns, v, f, diagonal, to_east, statics[2], statics[3], ocean, rim)
    precond[...] = v[pl.ds(EDGE, columns)]
    image[...] = w0
    scaled = w0 * SCALE
    m = dot(weights[...], scaled)[:4]
    pad = jnp.zeros((3, m.shape[1]), jnp.float32)
    for_east = jnp.concatenate([m, scaled[end:], pad], axis=0)
    for_west = jnp.concatenate([m, scaled[:1], pad], axis=0)
    to_first[...] = jnp.where(even, for_east, for_west)
    to_second[...] = jnp.where(even, for_west, for_east)


def second_kernel(
    levels, columns, rows, others,
    field, precond, image, statics, near, far, diagonal, to_east, rim, *rest,
):
    received = rest[: 2 + others]
    again, along, sums, v, f = rest[2 + others :]
    v[...] = circle(near, far, image[...] * SCALE, received)
    out = apply_twice(levels, columns, v, f, diagonal, to_east, statics[2], statics[3], statics[4], rim)
    own = slice(REACH * levels, (REACH + rows) * levels)
    again[...] = v[pl.ds(EDGE, columns)][:, own]
    along[...] = out[:, own]
    r, p, w = field[:, own], precond[:, own], image[:, own]
    q, z = again[...], along[...]

    def part(x):
        s = jnp.sum(x, axis=0, keepdims=True)
        return sum(s[:, k : k + 128] for k in range(0, s.shape[1], 128))

    parts = [part(r * p), part(p * w), part(w * q), part(q * z), jnp.zeros((4, 128), jnp.float32)]
    sums[...] = jnp.concatenate(parts, axis=0)


def combine_kernel(rows, levels, sums, noise, precond, image, again, along, answer, left):
    total = jnp.sum(sums[...], axis=1, keepdims=True)
    energy, curve, mixed, last = total[0:1], total[1:2], total[2:3], total[3:4]
    alpha = energy / curve
    beta = alpha / SCALE
    growth = alpha * beta * mixed / energy
    step = energy * (growth - 1.0) / (beta * beta * last - growth * growth * curve)
    keep = alpha + step * growth
    back = step * beta
    own = slice(REACH * levels, (REACH + rows) * levels)
    x = keep * precond[:, own] - back * again[...]
    y = keep * image[:, own] - back * along[...]
    group = REACH * levels
    for j in range(0, rows, REACH):
        at = slice(j * levels, j * levels + group)
        xt, yt = x[:, at].T, y[:, at].T
        for i in range(REACH):
            part = slice(i * levels, (i + 1) * levels)
            to = pl.ds(j + i, levels, stride=rows)
            answer[to, :] = xt[part]
            left[to, :] = noise[to, :] - yt[part]


def summed(x, axis):
    count = lax.axis_size(axis)
    step = 1
    while step < count:
        x = x + lax.ppermute(x, axis, [(i, i ^ step) for i in range(count)])
        step *= 2
    return x


def body(near, weights, far, noise, kappa2, conduct, land):
    levels, rows, columns = noise.shape
    count = lax.axis_size("lon")
    others = count - 3
    flat = levels * rows
    lanes = (rows + 2 * REACH) * levels
    tall = columns + 2 * EDGE
    noise = noise.reshape(flat, columns)
    kappa2 = kappa2.reshape(flat, columns)
    land = land.reshape(flat, columns)
    conduct = conduct.reshape(3, flat, columns)

    sources = (noise, kappa2, conduct, land, near, far, weights)
    planes = (PLANES, levels, columns)
    second, first, noise, kappa2, conduct, land, near, far, weights = pl.pallas_call(
        functools.partial(band_kernel, rows, levels),
        out_shape=[pltpu.VMEM(planes, jnp.float32)] * 2 + [pltpu.VMEM(x.shape, x.dtype) for x in sources],
        in_specs=[pl.BlockSpec(memory_space=pltpu.HBM)] * len(sources),
        out_specs=whole(2 + len(sources)),
        scratch_shapes=[pltpu.SemaphoreType.DMA((len(sources),))],
        compiler_params=pltpu.CompilerParams(vmem_limit_bytes=8 << 20),
    )(*[pltpu.with_memory_space_constraint(x, pltpu.HBM) for x in sources])
    perm_a, perm_b = pair_perms(lax.axis_size("lat"), False)
    got_second = lax.ppermute(second, "lat", perm_b)
    got_first = lax.ppermute(first, "lat", perm_a)

    field, statics, to_first, to_second, to_others = call(
        functools.partial(prepare_kernel, rows, levels, columns),
        [(columns, lanes), (6, columns, lanes), (16, lanes), (16, lanes), (8, lanes)],
        noise, kappa2, conduct, land, got_second, got_first, weights, near_memory=range(7),
    )
    lon_a, lon_b = pair_perms(count, True)

    def exchange(one, two, rest):
        got = [lax.ppermute(one, "lon", lon_a), lax.ppermute(two, "lon", lon_b)]
        for d in range(2, count - 1):
            got.append(lax.ppermute(rest, "lon", [(i, (i + d) % count) for i in range(count)]))
        return got

    told = exchange(to_first, to_second, to_others)
    precond, image, diagonal, to_east, rim, to_first2, to_second2 = call(
        functools.partial(first_kernel, levels, columns, others),
        [(columns, lanes), (columns, lanes), (columns, lanes), (tall, lanes), (5, 8, lanes), (8, lanes), (8, lanes)],
        field, statics, near, far, weights, to_first, to_second, *told, near_memory=range(9 + others),
        scratch=[(tall, lanes), (tall, lanes)],
    )
    told = exchange(to_first2, to_second2, to_first2)
    again, along, sums = call(
        functools.partial(second_kernel, levels, columns, rows, others),
        [(columns, flat), (columns, flat), (8, 128)],
        field, precond, image, statics, near, far, diagonal, to_east, rim, *told,
        near_memory=range(11 + others),
        scratch=[(tall, lanes), (tall, lanes)],
    )
    sums = summed(summed(sums, "lon"), "lat")
    answer, left = call(
        functools.partial(combine_kernel, rows, levels),
        [(flat, columns), (flat, columns)],
        sums, noise, precond, image, again, along, near_memory=range(6), last=True,
    )
    return answer.reshape(levels, rows, columns), left.reshape(levels, rows, columns)


def solution(mesh):
    def run(noise, kappa2, conduct, land):
        count = mesh.shape["lon"]
        near, weights, far = circle_matrices(count, noise.shape[2] // count)
        return jax.shard_map(
            functools.partial(body, near, weights, far),
            mesh=mesh,
            in_specs=(
                P("ens", "lat", "lon"),
                P(None, "lat", "lon"),
                P(None, None, "lat", "lon"),
                P(None, "lat", "lon"),
            ),
            out_specs=(P("ens", "lat", "lon"), P("ens", "lat", "lon")),
            check_vma=False,
        )(noise, kappa2, conduct, land)

    return run
```

```python
import functools
import math

import jax
import jax.numpy as jnp
import numpy as np
from jax import lax
from jax.experimental import pallas as pl
from jax.experimental.pallas import tpu as pltpu
from jax.sharding import PartitionSpec as P

base_kappa = 0.001
base_conduct = 1.0

SCALE = 2.0**-31
REACH = 4
EDGE = 8

HIGHEST = lax.Precision.HIGHEST


def dot(a, b):
    return jnp.dot(a, b, precision=HIGHEST, preferred_element_type=jnp.float32)


def circle_kernel(total):
    middle = 2.0 + base_kappa / base_conduct
    rho = (middle - math.sqrt(middle * middle - 4.0)) / 2.0
    height = 1.0 / (1.0 / rho - rho) / base_conduct
    wrap = rho**total
    shift = (1.0 + rho * rho) / (1.0 - rho * rho) + total * wrap / (1.0 - wrap)
    front = height * height / (1.0 - wrap)
    return rho, front, shift


def circle_matrices(count, columns):
    total = count * columns
    rho, front, shift = circle_kernel(total)

    def one_side(n):
        return front * rho**n * (n + shift)

    def both_sides(n):
        return one_side(n) + one_side(total - n)

    place = np.arange(columns)
    rows = columns + 2 * EDGE
    x = np.arange(rows) - EDGE
    used = (x >= -2) & (x < columns + 2)
    near = both_sides(np.abs(x[:, None] - place[None, :])) * used[:, None]
    back = columns - 1 - place
    moments = np.zeros((8, columns))
    moments[0] = rho**place
    moments[1] = place * rho**place
    moments[2] = rho**back
    moments[3] = back * rho**back

    def block(offset):
        a = columns * offset - x
        b = total - columns * offset + x - (columns - 1)
        out = np.zeros((rows, 8))
        out[:, 0] = front * rho**a * (a + shift)
        out[:, 1] = front * rho**a
        out[:, 2] = front * rho**b * (b + shift)
        out[:, 3] = front * rho**b
        amend = both_sides(1) - both_sides(-1)
        if offset == 1:
            out[EDGE + columns + 1, 4] = amend
        if offset == count - 1:
            out[EDGE - 2, 4] += amend
        return out * used[:, None]

    others = [block(count - d) for d in range(2, count - 1)]
    far = np.stack(
        [
            np.concatenate([block(1), block(count - 1)] + others, axis=1),
            np.concatenate([block(count - 1), block(1)] + others, axis=1),
        ]
    )
    as_f32 = lambda m: np.asarray(m, np.float32)
    return as_f32(near), as_f32(moments), as_f32(far)


def pair_perms(count, wrap):
    first = [(i, i + 1) for i in range(0, count - 1, 2)]
    second = [(i, i + 1) for i in range(1, count - 1, 2)]
    if wrap:
        second.append((count - 1, 0))
    both = lambda pairs: pairs + [(j, i) for i, j in pairs]
    return both(first), both(second)


def whole(n):
    return [pl.BlockSpec(memory_space=pltpu.VMEM)] * n


def call(kernel, outs, *args, scratch=(), last=False):
    args = [pltpu.with_memory_space_constraint(a, pltpu.VMEM) for a in args]
    kind = jax.ShapeDtypeStruct if last else pltpu.VMEM
    return pl.pallas_call(
        kernel,
        out_shape=[kind(s, jnp.float32) for s in outs],
        in_specs=whole(len(args)),
        out_specs=whole(len(outs)),
        scratch_shapes=[pltpu.VMEM(s, jnp.float32) for s in scratch],
        compiler_params=pltpu.CompilerParams(vmem_limit_bytes=24 << 20),
    )(*args)


FULL, PART = REACH, REACH - 1
PLANES = 3 * FULL + 3 * PART


def band_kernel(rows, levels, *refs):
    sources, (second, first), copies, sems = refs[:7], refs[7:9], refs[9:16], refs[16]
    moves = [pltpu.make_async_copy(x, y, sems.at[k]) for k, (x, y) in enumerate(zip(sources, copies))]
    for move in moves:
        move.start()
    for move in moves:
        move.wait()
    noise, kappa2, conduct, land = copies[:4]
    odd = lax.axis_index("lat") % 2
    top = rows - REACH
    loads = (
        lambda at: noise[at, :],
        lambda at: land[at, :].astype(jnp.float32),
        lambda at: conduct[1, at, :],
        lambda at: kappa2[at, :],
        lambda at: conduct[0, at, :],
        lambda at: conduct[2, at, :],
    )
    for out, side in ((first, odd), (second, 1 - odd)):
        k = 0
        for kind, load in enumerate(loads):
            count = FULL if kind < 3 else PART
            start = (1 - side) * (rows - count)
            for j in range(count):
                out[k] = load(pl.ds(start + j, levels, stride=rows))
                k += 1


def turned(planes, rows_of_planes):
    blocks = [jnp.concatenate(planes[j : j + REACH], axis=0) for j in range(0, rows_of_planes, REACH)]
    return jnp.concatenate([b.T for b in blocks], axis=1)


def coefficients(levels, band, kappa, east, north, upper, ocean):
    columns, lanes = kappa.shape
    lane = lax.broadcasted_iota(jnp.int32, (1, lanes), 1)
    row = lax.broadcasted_iota(jnp.int32, (columns, 1), 0)
    upper = jnp.where(lane % levels == levels - 1, 0.0, upper)
    south = jnp.where(lane % band < levels, 0.0, pltpu.roll(north, levels, 1))
    west = jnp.where(row == 0, 0.0, pltpu.roll(east, 1, 0))
    ocean_east = jnp.where(row == columns - 1, 1.0, pltpu.roll(ocean, columns - 1, 0))
    diagonal = ocean * (kappa + east + west + north + south + upper + pltpu.roll(upper, 1, 1))
    return diagonal, east * ocean * ocean_east, upper * ocean * pltpu.roll(ocean, lanes - 1, 1)


def store(statics, edge, diagonal, to_east, north, to_upper, ocean, east):
    for k, x in enumerate((diagonal, to_east, north, to_upper, ocean)):
        statics[k] = x
    edge[0:1] = east[east.shape[0] - 1 :]


def own_kernel(
    rows, levels, columns,
    noise, kappa2, conduct, land, weights,
    field, statics, edge, to_first, to_second, to_others,
):
    last_band = lax.axis_index("lat") == lax.axis_size("lat") - 1
    lon_odd = lax.axis_index("lon") % 2
    lanes = rows * levels

    def own(load):
        return turned([load(pl.ds(j, levels, stride=rows)) for j in range(rows)], rows)

    r = own(lambda at: noise[at, :])
    field[...] = r
    ocean = own(lambda at: land[at, :].astype(jnp.float32))
    north = own(lambda at: conduct[1, at, :])
    kappa = own(lambda at: kappa2[at, :])
    east = own(lambda at: conduct[0, at, :])
    upper = own(lambda at: conduct[2, at, :])
    lane = lax.broadcasted_iota(jnp.int32, (1, lanes), 1)
    north = jnp.where(last_band & (lane >= lanes - levels), 0.0, north)
    diagonal, to_east, to_upper = coefficients(levels, lanes, kappa, east, north, upper, ocean)
    store(statics, edge, diagonal, to_east, north, to_upper, ocean, east)
    m = dot(weights[...], r)
    to_others[...] = m
    m = m[:4]
    end = columns - 1
    blank = jnp.zeros((5, lanes), jnp.float32)
    for_east = [m, r[end:], diagonal[end:], to_east[end - 1 : end], east[end:], ocean[end:], north[end:], to_upper[end:], blank]
    for_west = [m, r[:1], diagonal[:1], to_east[:1], east[:1], ocean[:1], north[:1], to_upper[:1], blank]
    for_east = jnp.concatenate(for_east, axis=0)
    for_west = jnp.concatenate(for_west, axis=0)
    to_first[...] = jnp.where(lon_odd == 0, for_east, for_west)
    to_second[...] = jnp.where(lon_odd == 0, for_west, for_east)


def ghost_kernel(levels, columns, got_second, got_first, field, statics, edge):
    lat_odd = lax.axis_index("lat") % 2
    group = REACH * levels

    def ghost(kind, north):
        count = FULL if kind < 3 else PART
        k = kind * FULL if kind < 3 else 3 * FULL + (kind - 3) * PART
        a = got_first[pl.ds(k, count)].reshape(count * levels, columns)
        b = got_second[pl.ds(k, count)].reshape(count * levels, columns)
        from_first = (lat_odd == 0) if north else (lat_odd == 1)
        planes = jnp.where(from_first, a, b)
        if count == REACH:
            return planes.T
        blank = jnp.zeros((group - count * levels, columns), jnp.float32)
        return jnp.concatenate([planes, blank] if north else [blank, planes], axis=0).T

    r, ocean, north, kappa, east, upper = (
        jnp.concatenate([ghost(kind, False), ghost(kind, True)], axis=1) for kind in range(6)
    )
    field[...] = r
    diagonal, to_east, to_upper = coefficients(levels, group, kappa, east, north, upper, ocean)
    store(statics, edge, diagonal, to_east, north, to_upper, ocean, east)


def forward_kernel(group, *refs):
    lists, (second, first) = refs[:-2], refs[-2:]
    odd = lax.axis_index("lat") % 2
    k = 0
    for x in lists:
        count, lanes = x.shape
        low, high = x[:, 0:group], x[:, lanes - group :]
        first[pl.ds(k, count)] = jnp.where(odd == 0, high, low)
        second[pl.ds(k, count)] = jnp.where(odd == 0, low, high)
        k += count


def circle(near, far, own, lists):
    lon_odd = lax.axis_index("lon") % 2
    told = jnp.concatenate([t[0:8] for t in lists], axis=0)
    return dot(near[...], own) + dot(far[lon_odd], told)


def stencil(v, east_v, west_v, d, e, w, n, u, levels):
    lanes = v.shape[1]
    return (
        d * v
        - e * east_v
        - w * west_v
        - n * pltpu.roll(v, lanes - levels, 1)
        - pltpu.roll(n * v, levels, 1)
        - u * pltpu.roll(v, lanes - 1, 1)
        - pltpu.roll(u * v, 1, 1)
    )


def apply_twice(levels, columns, v, f, statics, to_east, rim):
    diagonal, north, upper, ocean = (statics[k] for k in range(4))
    own = pl.ds(EDGE, columns)
    after = pl.ds(EDGE + 1, columns)
    before = pl.ds(EDGE - 1, columns)
    end = EDGE + columns
    e, w = to_east[own], to_east[before]
    f[own] = stencil(v[own], v[after], v[before], diagonal, e, w, north, upper, levels)
    pick = lambda a, b: jnp.concatenate([v[a : a + 1], v[b : b + 1], jnp.zeros((6, v.shape[1]), jnp.float32)], axis=0)
    g = stencil(
        pick(EDGE - 1, end), pick(EDGE, end + 1), pick(EDGE - 2, end - 1),
        rim[0], rim[1], rim[2], rim[3], rim[4], levels,
    )
    f[EDGE - 1 : EDGE] = g[0:1]
    f[end : end + 1] = g[1:2]
    second = stencil(f[own], f[after], f[before], diagonal, e, w, north, upper, levels)
    return jnp.where(ocean > 0.5, second, v[own])


def first_kernel(
    rows, levels, columns, others,
    own_field, own_statics, own_edge, field, ghost_statics, edge, near, far, weights, side_second, side_first, *rest,
):
    received = rest[: 2 + others]
    precond, image, statics, to_east, rim, to_first, to_second, v, f = rest[2 + others :]
    lat_odd = lax.axis_index("lat") % 2
    even = lax.axis_index("lon") % 2 == 0
    group = REACH * levels
    lanes = rows * levels + 2 * group

    def joined(own, ghost):
        return jnp.concatenate([ghost[:, :group], own, ghost[:, group:]], axis=1)

    lists, k = [], 0
    for x in received:
        count = x.shape[0]
        a, b = side_first[pl.ds(k, count)], side_second[pl.ds(k, count)]
        lists.append(jnp.concatenate([jnp.where(lat_odd == 1, a, b), x[...], jnp.where(lat_odd == 1, b, a)], axis=1))
        k += count
    v[...] = circle(near, far, joined(own_field[...], field[...]), lists)

    lane = lax.broadcasted_iota(jnp.int32, (1, lanes), 1)
    first_of_band = ((lane >= group) & (lane < group + levels)) | ((lane >= lanes - group) & (lane < lanes - group + levels))

    def completed(diagonal, north, ocean):
        diagonal = diagonal + jnp.where(first_of_band, ocean * pltpu.roll(north, levels, 1), 0.0)
        return diagonal, north * ocean * pltpu.roll(ocean, lanes - levels, 1)

    ocean = joined(own_statics[4], ghost_statics[4])
    diagonal, north = completed(
        joined(own_statics[0], ghost_statics[0]), joined(own_statics[2], ghost_statics[2]), ocean
    )
    east_list = jnp.where(even, lists[0], lists[1])
    west_list = jnp.where(even, lists[1], lists[0])
    end = columns - 1
    row = lax.broadcasted_iota(jnp.int32, (columns, 1), 0)
    full_east = joined(own_statics[1], ghost_statics[1])
    full_east = jnp.where(row == end, full_east * east_list[8:9], full_east)
    to_east[pl.ds(EDGE, columns)] = full_east
    face_west = west_list[7:8] * west_list[8:9] * ocean[0:1]
    to_east[EDGE - 1 : EDGE] = face_west
    statics[0] = diagonal + jnp.where(row == 0, ocean * west_list[7:8], 0.0)
    statics[1] = north
    statics[2] = joined(own_statics[3], ghost_statics[3])
    statics[3] = ocean
    blank = jnp.zeros((6, lanes), jnp.float32)
    stack = lambda p, q: jnp.concatenate([p, q, blank], axis=0)
    last_face = joined(own_edge[0:1], edge[0:1])
    rim_ocean = stack(west_list[8:9], east_list[8:9])
    rim_diagonal, rim_north = completed(
        stack(west_list[5:6], east_list[5:6] + east_list[8:9] * last_face),
        stack(west_list[9:10], east_list[9:10]),
        rim_ocean,
    )
    rim[0] = rim_diagonal
    rim[1] = stack(face_west, east_list[6:7])
    rim[2] = stack(west_list[6:7], full_east[end:])
    rim[3] = rim_north
    rim[4] = stack(west_list[10:11], east_list[10:11])
    w0 = apply_twice(levels, columns, v, f, statics, to_east, rim)
    precond[...] = v[pl.ds(EDGE, columns)]
    image[...] = w0
    scaled = w0 * SCALE
    m = dot(weights[...], scaled)[:4]
    pad = jnp.zeros((3, m.shape[1]), jnp.float32)
    for_east = jnp.concatenate([m, scaled[end:], pad], axis=0)
    for_west = jnp.concatenate([m, scaled[:1], pad], axis=0)
    to_first[...] = jnp.where(even, for_east, for_west)
    to_second[...] = jnp.where(even, for_west, for_east)


def second_kernel(
    levels, columns, rows, others,
    field, precond, image, statics, near, far, to_east, rim, *rest,
):
    received = rest[: 2 + others]
    again, along, sums, v, f = rest[2 + others :]
    v[...] = circle(near, far, image[...] * SCALE, received)
    out = apply_twice(levels, columns, v, f, statics, to_east, rim)
    own = slice(REACH * levels, (REACH + rows) * levels)
    again[...] = v[pl.ds(EDGE, columns)][:, own]
    along[...] = out[:, own]
    r, p, w = field[...], precond[:, own], image[:, own]
    q, z = again[...], along[...]

    def part(x):
        s = jnp.sum(x, axis=0, keepdims=True)
        return sum(s[:, k : k + 128] for k in range(0, s.shape[1], 128))

    parts = [part(r * p), part(p * w), part(w * q), part(q * z), jnp.zeros((4, 128), jnp.float32)]
    sums[...] = jnp.concatenate(parts, axis=0)


def combine_kernel(rows, levels, sums, noise, precond, image, again, along, answer, left):
    total = jnp.sum(sums[...], axis=1, keepdims=True)
    energy, curve, mixed, last = total[0:1], total[1:2], total[2:3], total[3:4]
    alpha = energy / curve
    beta = alpha / SCALE
    growth = alpha * beta * mixed / energy
    step = energy * (growth - 1.0) / (beta * beta * last - growth * growth * curve)
    keep = alpha + step * growth
    back = step * beta
    own = slice(REACH * levels, (REACH + rows) * levels)
    x = keep * precond[:, own] - back * again[...]
    y = keep * image[:, own] - back * along[...]
    group = REACH * levels
    for j in range(0, rows, REACH):
        at = slice(j * levels, j * levels + group)
        xt, yt = x[:, at].T, y[:, at].T
        for i in range(REACH):
            part = slice(i * levels, (i + 1) * levels)
            to = pl.ds(j + i, levels, stride=rows)
            answer[to, :] = xt[part]
            left[to, :] = noise[to, :] - yt[part]


def summed(x, axis):
    count = lax.axis_size(axis)
    step = 1
    while step < count:
        x = x + lax.ppermute(x, axis, [(i, i ^ step) for i in range(count)])
        step *= 2
    return x


def body(near, weights, far, noise, kappa2, conduct, land):
    levels, rows, columns = noise.shape
    count = lax.axis_size("lon")
    others = count - 3
    flat = levels * rows
    lanes = (rows + 2 * REACH) * levels
    tall = columns + 2 * EDGE
    noise = noise.reshape(flat, columns)
    kappa2 = kappa2.reshape(flat, columns)
    land = land.reshape(flat, columns)
    conduct = conduct.reshape(3, flat, columns)

    sources = (noise, kappa2, conduct, land, near, far, weights)
    planes = (PLANES, levels, columns)
    second, first, noise, kappa2, conduct, land, near, far, weights = pl.pallas_call(
        functools.partial(band_kernel, rows, levels),
        out_shape=[pltpu.VMEM(planes, jnp.float32)] * 2 + [pltpu.VMEM(x.shape, x.dtype) for x in sources],
        in_specs=[pl.BlockSpec(memory_space=pltpu.HBM)] * len(sources),
        out_specs=whole(2 + len(sources)),
        scratch_shapes=[pltpu.SemaphoreType.DMA((len(sources),))],
        compiler_params=pltpu.CompilerParams(vmem_limit_bytes=8 << 20),
    )(*[pltpu.with_memory_space_constraint(x, pltpu.HBM) for x in sources])
    perm_a, perm_b = pair_perms(lax.axis_size("lat"), False)
    got_second = lax.ppermute(second, "lat", perm_b)
    got_first = lax.ppermute(first, "lat", perm_a)

    own_field, own_statics, own_edge, to_first, to_second, to_others = call(
        functools.partial(own_kernel, rows, levels, columns),
        [(columns, flat), (5, columns, flat), (8, flat), (16, flat), (16, flat), (8, flat)],
        noise, kappa2, conduct, land, weights,
    )
    lon_a, lon_b = pair_perms(count, True)

    def exchange(one, two, rest):
        got = [lax.ppermute(one, "lon", lon_a), lax.ppermute(two, "lon", lon_b)]
        for d in range(2, count - 1):
            got.append(lax.ppermute(rest, "lon", [(i, (i + d) % count) for i in range(count)]))
        return got

    told = exchange(to_first, to_second, to_others)
    heights = sum(x.shape[0] for x in told)
    group = REACH * levels
    side_second, side_first = call(functools.partial(forward_kernel, group), [(heights, group)] * 2, *told)
    side_second = lax.ppermute(side_second, "lat", perm_b)
    side_first = lax.ppermute(side_first, "lat", perm_a)
    field, ghost_statics, edge = call(
        functools.partial(ghost_kernel, levels, columns),
        [(columns, 2 * group), (5, columns, 2 * group), (8, 2 * group)],
        got_second, got_first,
    )
    precond, image, statics, to_east, rim, to_first, to_second = call(
        functools.partial(first_kernel, rows, levels, columns, others),
        [(columns, lanes), (columns, lanes), (4, columns, lanes), (tall, lanes), (5, 8, lanes), (8, lanes), (8, lanes)],
        own_field, own_statics, own_edge, field, ghost_statics, edge, near, far, weights, side_second, side_first, *told,
        scratch=[(tall, lanes), (tall, lanes)],
    )
    told = exchange(to_first, to_second, to_first)
    again, along, sums = call(
        functools.partial(second_kernel, levels, columns, rows, others),
        [(columns, flat), (columns, flat), (8, 128)],
        own_field, precond, image, statics, near, far, to_east, rim, *told,
        scratch=[(tall, lanes), (tall, lanes)],
    )
    sums = summed(summed(sums, "lon"), "lat")
    answer, left = call(
        functools.partial(combine_kernel, rows, levels),
        [(flat, columns), (flat, columns)],
        sums, noise, precond, image, again, along, last=True,
    )
    return answer.reshape(levels, rows, columns), left.reshape(levels, rows, columns)


def solution(mesh):
    def run(noise, kappa2, conduct, land):
        count = mesh.shape["lon"]
        near, weights, far = circle_matrices(count, noise.shape[2] // count)
        return jax.shard_map(
            functools.partial(body, near, weights, far),
            mesh=mesh,
            in_specs=(
                P("ens", "lat", "lon"),
                P(None, "lat", "lon"),
                P(None, None, "lat", "lon"),
                P(None, "lat", "lon"),
            ),
            out_specs=(P("ens", "lat", "lon"), P("ens", "lat", "lon")),
            check_vma=False,
        )(noise, kappa2, conduct, land)

    return run
```

```python
import functools
import math

import jax
import jax.numpy as jnp
import numpy as np
from jax import lax
from jax.experimental import pallas as pl
from jax.experimental.pallas import tpu as pltpu
from jax.sharding import PartitionSpec as P

base_kappa = 0.001
base_conduct = 1.0

SCALE = 2.0**-31
REACH = 4
EDGE = 8

HIGHEST = lax.Precision.HIGHEST


def dot(a, b):
    return jnp.dot(a, b, precision=HIGHEST, preferred_element_type=jnp.float32)


def circle_kernel(total):
    middle = 2.0 + base_kappa / base_conduct
    rho = (middle - math.sqrt(middle * middle - 4.0)) / 2.0
    height = 1.0 / (1.0 / rho - rho) / base_conduct
    wrap = rho**total
    shift = (1.0 + rho * rho) / (1.0 - rho * rho) + total * wrap / (1.0 - wrap)
    front = height * height / (1.0 - wrap)
    return rho, front, shift


def circle_matrices(count, columns):
    total = count * columns
    rho, front, shift = circle_kernel(total)

    def one_side(n):
        return front * rho**n * (n + shift)

    def both_sides(n):
        return one_side(n) + one_side(total - n)

    place = np.arange(columns)
    rows = columns + 2 * EDGE
    x = np.arange(rows) - EDGE
    used = (x >= -2) & (x < columns + 2)
    near = both_sides(np.abs(x[:, None] - place[None, :])) * used[:, None]
    back = columns - 1 - place
    moments = np.zeros((8, columns))
    moments[0] = rho**place
    moments[1] = place * rho**place
    moments[2] = rho**back
    moments[3] = back * rho**back

    def block(offset):
        a = columns * offset - x
        b = total - columns * offset + x - (columns - 1)
        out = np.zeros((rows, 8))
        out[:, 0] = front * rho**a * (a + shift)
        out[:, 1] = front * rho**a
        out[:, 2] = front * rho**b * (b + shift)
        out[:, 3] = front * rho**b
        amend = both_sides(1) - both_sides(-1)
        if offset == 1:
            out[EDGE + columns + 1, 4] = amend
        if offset == count - 1:
            out[EDGE - 2, 4] += amend
        return out * used[:, None]

    others = [block(count - d) for d in range(2, count - 1)]
    far = np.stack(
        [
            np.concatenate([block(1), block(count - 1)] + others, axis=1),
            np.concatenate([block(count - 1), block(1)] + others, axis=1),
        ]
    )
    spread = np.stack([np.concatenate([near, f], axis=1) for f in far])
    return np.asarray(spread, np.float32), np.asarray(moments, np.float32)


def pair_perms(count, wrap):
    first = [(i, i + 1) for i in range(0, count - 1, 2)]
    second = [(i, i + 1) for i in range(1, count - 1, 2)]
    if wrap:
        second.append((count - 1, 0))
    both = lambda pairs: pairs + [(j, i) for i, j in pairs]
    return both(first), both(second)


def whole(n):
    return [pl.BlockSpec(memory_space=pltpu.VMEM)] * n


def call(kernel, outs, *args, scratch=(), last=False):
    args = [pltpu.with_memory_space_constraint(a, pltpu.VMEM) for a in args]
    kind = jax.ShapeDtypeStruct if last else pltpu.VMEM
    return pl.pallas_call(
        kernel,
        out_shape=[kind(s, jnp.float32) for s in outs],
        in_specs=whole(len(args)),
        out_specs=whole(len(outs)),
        scratch_shapes=[pltpu.VMEM(s, jnp.float32) for s in scratch],
        compiler_params=pltpu.CompilerParams(vmem_limit_bytes=24 << 20),
        name=kernel.func.__name__,
    )(*args)


FULL, PART = REACH, REACH - 1
PLANES = 3 * FULL + 3 * PART


def band_kernel(rows, levels, *refs):
    sources, (second, first), copies, sems = refs[:6], refs[6:8], refs[8:14], refs[14]
    moves = [pltpu.make_async_copy(x, y, sems.at[k]) for k, (x, y) in enumerate(zip(sources, copies))]
    for move in moves:
        move.start()
    for move in moves:
        move.wait()
    noise, kappa2, conduct, land = copies[:4]
    odd = lax.axis_index("lat") % 2
    top = rows - REACH
    loads = (
        lambda at: noise[at, :],
        lambda at: land[at, :].astype(jnp.float32),
        lambda at: conduct[1, at, :],
        lambda at: kappa2[at, :],
        lambda at: conduct[0, at, :],
        lambda at: conduct[2, at, :],
    )
    for out, side in ((first, odd), (second, 1 - odd)):
        k = 0
        for kind, load in enumerate(loads):
            count = FULL if kind < 3 else PART
            start = (1 - side) * (rows - count)
            for j in range(count):
                out[k] = load(pl.ds(start + j, levels, stride=rows))
                k += 1


def turned(planes, rows_of_planes):
    blocks = [jnp.concatenate(planes[j : j + REACH], axis=0) for j in range(0, rows_of_planes, REACH)]
    return jnp.concatenate([b.T for b in blocks], axis=1)


def coefficients(levels, band, kappa, east, north, upper, ocean):
    columns, lanes = kappa.shape
    lane = lax.broadcasted_iota(jnp.int32, (1, lanes), 1)
    row = lax.broadcasted_iota(jnp.int32, (columns, 1), 0)
    upper = jnp.where(lane % levels == levels - 1, 0.0, upper)
    south = jnp.where(lane % band < levels, 0.0, pltpu.roll(north, levels, 1))
    west = jnp.where(row == 0, 0.0, pltpu.roll(east, 1, 0))
    ocean_east = jnp.where(row == columns - 1, 1.0, pltpu.roll(ocean, columns - 1, 0))
    diagonal = ocean * (kappa + east + west + north + south + upper + pltpu.roll(upper, 1, 1))
    return diagonal, east * ocean * ocean_east, upper * ocean * pltpu.roll(ocean, lanes - 1, 1)


def store(statics, edge, diagonal, to_east, north, to_upper, ocean, east):
    for k, x in enumerate((diagonal, to_east, north, to_upper, ocean)):
        statics[k] = x
    edge[0:1] = east[east.shape[0] - 1 :]


def own_kernel(
    rows, levels, columns,
    noise, kappa2, conduct, land, weights,
    field, statics, edge, to_first, to_second, to_others,
):
    last_band = lax.axis_index("lat") == lax.axis_size("lat") - 1
    lon_odd = lax.axis_index("lon") % 2
    lanes = rows * levels

    def own(load):
        return turned([load(pl.ds(j, levels, stride=rows)) for j in range(rows)], rows)

    r = own(lambda at: noise[at, :])
    field[...] = r
    ocean = own(lambda at: land[at, :].astype(jnp.float32))
    north = own(lambda at: conduct[1, at, :])
    kappa = own(lambda at: kappa2[at, :])
    east = own(lambda at: conduct[0, at, :])
    upper = own(lambda at: conduct[2, at, :])
    lane = lax.broadcasted_iota(jnp.int32, (1, lanes), 1)
    north = jnp.where(last_band & (lane >= lanes - levels), 0.0, north)
    diagonal, to_east, to_upper = coefficients(levels, lanes, kappa, east, north, upper, ocean)
    store(statics, edge, diagonal, to_east, north, to_upper, ocean, east)
    m = dot(weights[...], r)
    to_others[...] = m
    m = m[:4]
    end = columns - 1
    blank = jnp.zeros((5, lanes), jnp.float32)
    for_east = [m, r[end:], diagonal[end:], to_east[end - 1 : end], east[end:], ocean[end:], north[end:], to_upper[end:], blank]
    for_west = [m, r[:1], diagonal[:1], to_east[:1], east[:1], ocean[:1], north[:1], to_upper[:1], blank]
    for_east = jnp.concatenate(for_east, axis=0)
    for_west = jnp.concatenate(for_west, axis=0)
    to_first[...] = jnp.where(lon_odd == 0, for_east, for_west)
    to_second[...] = jnp.where(lon_odd == 0, for_west, for_east)


def ghost_kernel(levels, columns, got_second, got_first, field, statics, edge):
    lat_odd = lax.axis_index("lat") % 2
    group = REACH * levels

    def ghost(kind, north):
        count = FULL if kind < 3 else PART
        k = kind * FULL if kind < 3 else 3 * FULL + (kind - 3) * PART
        a = got_first[pl.ds(k, count)].reshape(count * levels, columns)
        b = got_second[pl.ds(k, count)].reshape(count * levels, columns)
        from_first = (lat_odd == 0) if north else (lat_odd == 1)
        planes = jnp.where(from_first, a, b)
        if count == REACH:
            return planes.T
        blank = jnp.zeros((group - count * levels, columns), jnp.float32)
        return jnp.concatenate([planes, blank] if north else [blank, planes], axis=0).T

    r, ocean, north, kappa, east, upper = (
        jnp.concatenate([ghost(kind, False), ghost(kind, True)], axis=1) for kind in range(6)
    )
    field[...] = r
    diagonal, to_east, to_upper = coefficients(levels, group, kappa, east, north, upper, ocean)
    store(statics, edge, diagonal, to_east, north, to_upper, ocean, east)


def forward_kernel(group, *refs):
    lists, (second, first) = refs[:-2], refs[-2:]
    odd = lax.axis_index("lat") % 2
    k = 0
    for x in lists:
        count, lanes = x.shape
        low, high = x[:, 0:group], x[:, lanes - group :]
        first[pl.ds(k, count)] = jnp.where(odd == 0, high, low)
        second[pl.ds(k, count)] = jnp.where(odd == 0, low, high)
        k += count


def circle(spread, own, lists):
    lon_odd = lax.axis_index("lon") % 2
    told = jnp.concatenate([own] + [t[0:8] for t in lists], axis=0)
    return dot(spread[lon_odd], told)


def stencil(v, east_v, west_v, d, e, w, n, u, levels):
    lanes = v.shape[1]
    return (
        d * v
        - e * east_v
        - w * west_v
        - n * pltpu.roll(v, lanes - levels, 1)
        - pltpu.roll(n * v, levels, 1)
        - u * pltpu.roll(v, lanes - 1, 1)
        - pltpu.roll(u * v, 1, 1)
    )


def apply_twice(levels, columns, v, f, statics, to_east, rim):
    diagonal, north, upper, ocean = (statics[k] for k in range(4))
    own = pl.ds(EDGE, columns)
    after = pl.ds(EDGE + 1, columns)
    before = pl.ds(EDGE - 1, columns)
    end = EDGE + columns
    e, w = to_east[own], to_east[before]
    f[own] = stencil(v[own], v[after], v[before], diagonal, e, w, north, upper, levels)
    pick = lambda a, b: jnp.concatenate([v[a : a + 1], v[b : b + 1], jnp.zeros((6, v.shape[1]), jnp.float32)], axis=0)
    g = stencil(
        pick(EDGE - 1, end), pick(EDGE, end + 1), pick(EDGE - 2, end - 1),
        rim[0], rim[1], rim[2], rim[3], rim[4], levels,
    )
    f[EDGE - 1 : EDGE] = g[0:1]
    f[end : end + 1] = g[1:2]
    second = stencil(f[own], f[after], f[before], diagonal, e, w, north, upper, levels)
    return jnp.where(ocean > 0.5, second, v[own])


def first_kernel(
    rows, levels, columns, others,
    own_field, own_statics, own_edge, field, ghost_statics, edge, spread, weights, side_second, side_first, *rest,
):
    received = rest[: 2 + others]
    precond, image, statics, to_east, rim, to_first, to_second, v, f = rest[2 + others :]
    lat_odd = lax.axis_index("lat") % 2
    even = lax.axis_index("lon") % 2 == 0
    group = REACH * levels
    lanes = rows * levels + 2 * group

    def joined(own, ghost):
        return jnp.concatenate([ghost[:, :group], own, ghost[:, group:]], axis=1)

    lists, k = [], 0
    for x in received:
        count = x.shape[0]
        a, b = side_first[pl.ds(k, count)], side_second[pl.ds(k, count)]
        lists.append(jnp.concatenate([jnp.where(lat_odd == 1, a, b), x[...], jnp.where(lat_odd == 1, b, a)], axis=1))
        k += count
    v[...] = circle(spread, joined(own_field[...], field[...]), lists)

    lane = lax.broadcasted_iota(jnp.int32, (1, lanes), 1)
    first_of_band = ((lane >= group) & (lane < group + levels)) | ((lane >= lanes - group) & (lane < lanes - group + levels))

    def completed(diagonal, north, ocean):
        diagonal = diagonal + jnp.where(first_of_band, ocean * pltpu.roll(north, levels, 1), 0.0)
        return diagonal, north * ocean * pltpu.roll(ocean, lanes - levels, 1)

    ocean = joined(own_statics[4], ghost_statics[4])
    diagonal, north = completed(
        joined(own_statics[0], ghost_statics[0]), joined(own_statics[2], ghost_statics[2]), ocean
    )
    east_list = jnp.where(even, lists[0], lists[1])
    west_list = jnp.where(even, lists[1], lists[0])
    end = columns - 1
    row = lax.broadcasted_iota(jnp.int32, (columns, 1), 0)
    full_east = joined(own_statics[1], ghost_statics[1])
    full_east = jnp.where(row == end, full_east * east_list[8:9], full_east)
    to_east[pl.ds(EDGE, columns)] = full_east
    face_west = west_list[7:8] * west_list[8:9] * ocean[0:1]
    to_east[EDGE - 1 : EDGE] = face_west
    statics[0] = diagonal + jnp.where(row == 0, ocean * west_list[7:8], 0.0)
    statics[1] = north
    statics[2] = joined(own_statics[3], ghost_statics[3])
    statics[3] = ocean
    blank = jnp.zeros((6, lanes), jnp.float32)
    stack = lambda p, q: jnp.concatenate([p, q, blank], axis=0)
    last_face = joined(own_edge[0:1], edge[0:1])
    rim_ocean = stack(west_list[8:9], east_list[8:9])
    rim_diagonal, rim_north = completed(
        stack(west_list[5:6], east_list[5:6] + east_list[8:9] * last_face),
        stack(west_list[9:10], east_list[9:10]),
        rim_ocean,
    )
    rim[0] = rim_diagonal
    rim[1] = stack(face_west, east_list[6:7])
    rim[2] = stack(west_list[6:7], full_east[end:])
    rim[3] = rim_north
    rim[4] = stack(west_list[10:11], east_list[10:11])
    w0 = apply_twice(levels, columns, v, f, statics, to_east, rim)
    precond[...] = v[pl.ds(EDGE, columns)]
    image[...] = w0
    scaled = w0 * SCALE
    m = dot(weights[...], scaled)[:4]
    pad = jnp.zeros((3, m.shape[1]), jnp.float32)
    for_east = jnp.concatenate([m, scaled[end:], pad], axis=0)
    for_west = jnp.concatenate([m, scaled[:1], pad], axis=0)
    to_first[...] = jnp.where(even, for_east, for_west)
    to_second[...] = jnp.where(even, for_west, for_east)


def second_kernel(
    levels, columns, rows, others,
    field, precond, image, statics, spread, to_east, rim, *rest,
):
    received = rest[: 2 + others]
    again, along, sums, v, f = rest[2 + others :]
    v[...] = circle(spread, image[...] * SCALE, received)
    out = apply_twice(levels, columns, v, f, statics, to_east, rim)
    own = slice(REACH * levels, (REACH + rows) * levels)
    again[...] = v[pl.ds(EDGE, columns)][:, own]
    along[...] = out[:, own]
    r, p, w = field[...], precond[:, own], image[:, own]
    q, z = again[...], along[...]

    def part(x):
        s = jnp.sum(x, axis=0, keepdims=True)
        return sum(s[:, k : k + 128] for k in range(0, s.shape[1], 128))

    parts = [part(r * p), part(p * w), part(w * q), part(q * z), jnp.zeros((4, 128), jnp.float32)]
    sums[...] = jnp.concatenate(parts, axis=0)


def combine_kernel(rows, levels, here, beside, noise, precond, image, again, along, answer, left):
    odd = lax.axis_index("lon") % 2 == 1
    total = jnp.sum(jnp.where(odd, here[...], beside[...]), axis=1, keepdims=True)
    energy, curve, mixed, last = total[0:1], total[1:2], total[2:3], total[3:4]
    alpha = energy / curve
    beta = alpha / SCALE
    growth = alpha * beta * mixed / energy
    step = energy * (growth - 1.0) / (beta * beta * last - growth * growth * curve)
    keep = alpha + step * growth
    back = step * beta
    own = slice(REACH * levels, (REACH + rows) * levels)
    x = keep * precond[:, own] - back * again[...]
    y = keep * image[:, own] - back * along[...]
    group = REACH * levels
    for j in range(0, rows, REACH):
        at = slice(j * levels, j * levels + group)
        xt, yt = x[:, at].T, y[:, at].T
        for i in range(REACH):
            part = slice(i * levels, (i + 1) * levels)
            to = pl.ds(j + i, levels, stride=rows)
            answer[to, :] = xt[part]
            left[to, :] = noise[to, :] - yt[part]


def doubling(count):
    steps = []
    while 2 ** len(steps) < count:
        steps.append(2 ** len(steps))
    return steps


def summed(x):
    count, bands = lax.axis_size("lon"), lax.axis_size("lat")
    x = x + lax.ppermute(x, "lon", [(i, i + 1) for i in range(0, count, 2)])
    odd = range(1, count, 2)
    for step in doubling(count)[1:]:
        x = x + lax.ppermute(x, "lon", [(i, i ^ step) for i in odd])
    for step in doubling(bands):
        pairs = [(i * bands + j, i * bands + (j ^ step)) for i in odd for j in range(bands)]
        x = x + lax.ppermute(x, ("lon", "lat"), pairs)
    return x, lax.ppermute(x, "lon", [(i, i - 1) for i in odd])


def body(spread, weights, noise, kappa2, conduct, land):
    levels, rows, columns = noise.shape
    count = lax.axis_size("lon")
    others = count - 3
    flat = levels * rows
    lanes = (rows + 2 * REACH) * levels
    tall = columns + 2 * EDGE
    noise = noise.reshape(flat, columns)
    kappa2 = kappa2.reshape(flat, columns)
    land = land.reshape(flat, columns)
    conduct = conduct.reshape(3, flat, columns)

    sources = (noise, kappa2, conduct, land, spread, weights)
    planes = (PLANES, levels, columns)
    second, first, noise, kappa2, conduct, land, spread, weights = pl.pallas_call(
        functools.partial(band_kernel, rows, levels),
        out_shape=[pltpu.VMEM(planes, jnp.float32)] * 2 + [pltpu.VMEM(x.shape, x.dtype) for x in sources],
        in_specs=[pl.BlockSpec(memory_space=pltpu.HBM)] * len(sources),
        out_specs=whole(2 + len(sources)),
        scratch_shapes=[pltpu.SemaphoreType.DMA((len(sources),))],
        compiler_params=pltpu.CompilerParams(vmem_limit_bytes=8 << 20),
        name="band_kernel",
    )(*[pltpu.with_memory_space_constraint(x, pltpu.HBM) for x in sources])
    perm_a, perm_b = pair_perms(lax.axis_size("lat"), False)
    got_second = lax.ppermute(second, "lat", perm_b)
    got_first = lax.ppermute(first, "lat", perm_a)

    own_field, own_statics, own_edge, to_first, to_second, to_others = call(
        functools.partial(own_kernel, rows, levels, columns),
        [(columns, flat), (5, columns, flat), (8, flat), (16, flat), (16, flat), (8, flat)],
        noise, kappa2, conduct, land, weights,
    )
    lon_a, lon_b = pair_perms(count, True)

    def exchange(one, two, rest):
        got = [lax.ppermute(one, "lon", lon_a), lax.ppermute(two, "lon", lon_b)]
        for d in range(2, count - 1):
            got.append(lax.ppermute(rest, "lon", [(i, (i + d) % count) for i in range(count)]))
        return got

    told = exchange(to_first, to_second, to_others)
    heights = sum(x.shape[0] for x in told)
    group = REACH * levels
    side_second, side_first = call(functools.partial(forward_kernel, group), [(heights, group)] * 2, *told)
    side_second = lax.ppermute(side_second, "lat", perm_b)
    side_first = lax.ppermute(side_first, "lat", perm_a)
    field, ghost_statics, edge = call(
        functools.partial(ghost_kernel, levels, columns),
        [(columns, 2 * group), (5, columns, 2 * group), (8, 2 * group)],
        got_second, got_first,
    )
    precond, image, statics, to_east, rim, to_first, to_second = call(
        functools.partial(first_kernel, rows, levels, columns, others),
        [(columns, lanes), (columns, lanes), (4, columns, lanes), (tall, lanes), (5, 8, lanes), (8, lanes), (8, lanes)],
        own_field, own_statics, own_edge, field, ghost_statics, edge, spread, weights, side_second, side_first, *told,
        scratch=[(tall, lanes), (tall, lanes)],
    )
    told = exchange(to_first, to_second, to_first)
    again, along, sums = call(
        functools.partial(second_kernel, levels, columns, rows, others),
        [(columns, flat), (columns, flat), (8, 128)],
        own_field, precond, image, statics, spread, to_east, rim, *told,
        scratch=[(tall, lanes), (tall, lanes)],
    )
    here, beside = summed(sums)
    answer, left = call(
        functools.partial(combine_kernel, rows, levels),
        [(flat, columns), (flat, columns)],
        here, beside, noise, precond, image, again, along, last=True,
    )
    return answer.reshape(levels, rows, columns), left.reshape(levels, rows, columns)


def solution(mesh):
    def run(noise, kappa2, conduct, land):
        count = mesh.shape["lon"]
        spread, weights = circle_matrices(count, noise.shape[2] // count)
        return jax.shard_map(
            functools.partial(body, spread, weights),
            mesh=mesh,
            in_specs=(
                P("ens", "lat", "lon"),
                P(None, "lat", "lon"),
                P(None, None, "lat", "lon"),
                P(None, "lat", "lon"),
            ),
            out_specs=(P("ens", "lat", "lon"), P("ens", "lat", "lon")),
            check_vma=False,
        )(noise, kappa2, conduct, land)

    return run
```

```python
import functools
import math

import jax
import jax.numpy as jnp
import numpy as np
from jax import lax
from jax.experimental import pallas as pl
from jax.experimental.pallas import tpu as pltpu
from jax.sharding import PartitionSpec as P

base_kappa = 0.001
base_conduct = 1.0

SCALE = 2.0**-31
REACH = 4
EDGE = 8

HIGHEST = lax.Precision.HIGHEST


def dot(a, b):
    return jnp.dot(a, b, precision=HIGHEST, preferred_element_type=jnp.float32)


def circle_kernel(total):
    middle = 2.0 + base_kappa / base_conduct
    rho = (middle - math.sqrt(middle * middle - 4.0)) / 2.0
    height = 1.0 / (1.0 / rho - rho) / base_conduct
    wrap = rho**total
    shift = (1.0 + rho * rho) / (1.0 - rho * rho) + total * wrap / (1.0 - wrap)
    front = height * height / (1.0 - wrap)
    return rho, front, shift


def circle_matrices(count, columns):
    total = count * columns
    rho, front, shift = circle_kernel(total)

    def one_side(n):
        return front * rho**n * (n + shift)

    def both_sides(n):
        return one_side(n) + one_side(total - n)

    place = np.arange(columns)
    rows = columns + 2 * EDGE
    x = np.arange(rows) - EDGE
    used = (x >= -2) & (x < columns + 2)
    near = both_sides(np.abs(x[:, None] - place[None, :])) * used[:, None]
    back = columns - 1 - place
    moments = np.zeros((8, columns))
    moments[0] = rho**place
    moments[1] = place * rho**place
    moments[2] = rho**back
    moments[3] = back * rho**back

    def block(offset):
        a = columns * offset - x
        b = total - columns * offset + x - (columns - 1)
        out = np.zeros((rows, 8))
        out[:, 0] = front * rho**a * (a + shift)
        out[:, 1] = front * rho**a
        out[:, 2] = front * rho**b * (b + shift)
        out[:, 3] = front * rho**b
        amend = both_sides(1) - both_sides(-1)
        if offset == 1:
            out[EDGE + columns + 1, 4] = amend
        if offset == count - 1:
            out[EDGE - 2, 4] += amend
        return out * used[:, None]

    def blocks(sign):
        offsets = [(e, 0) for e in (1, -1, -2)] + [(e, k) for k in range(4, count, 4) for e in (0, 1, -1, -2)]
        return np.concatenate([block((sign * e - k) % count) for e, k in offsets], axis=1)

    spread = np.stack([np.concatenate([near, blocks(sign)], axis=1) for sign in (1, -1)])
    return np.asarray(spread, np.float32), np.asarray(moments, np.float32)


def lon_perms(count):
    first = [(i, i ^ 1) for i in range(count)]
    return first, [(i, (i - 1 + 2 * (i % 2)) % count) for i in range(count)]


def lat_perms(count, bands):
    first, second = [], []
    for i in range(count):
        for j in range(bands):
            k = j - 1 + 2 * (j % 2)
            first.append((i * bands + j, i * bands + (j ^ 1)))
            second.append((i * bands + j, i * bands + k if 0 <= k < bands else (i ^ 1) * bands + j))
    return first, second


def inner_band():
    return (lax.axis_index("lat") > 0) & (lax.axis_index("lat") < lax.axis_size("lat") - 1)


def whole(n):
    return [pl.BlockSpec(memory_space=pltpu.VMEM)] * n


def call(kernel, outs, *args, scratch=(), last=False):
    args = [pltpu.with_memory_space_constraint(a, pltpu.VMEM) for a in args]
    kind = jax.ShapeDtypeStruct if last else pltpu.VMEM
    return pl.pallas_call(
        kernel,
        out_shape=[kind(s, jnp.float32) for s in outs],
        in_specs=whole(len(args)),
        out_specs=whole(len(outs)),
        scratch_shapes=[pltpu.VMEM(s, jnp.float32) for s in scratch],
        compiler_params=pltpu.CompilerParams(vmem_limit_bytes=24 << 20),
        name=getattr(kernel, "func", kernel).__name__,
    )(*args)


FULL, PART = REACH, REACH - 1
PLANES = 3 * FULL + 3 * PART


def band_kernel(rows, levels, *refs):
    sources, (second, first), copies, sems = refs[:6], refs[6:8], refs[8:14], refs[14]
    moves = [pltpu.make_async_copy(x, y, sems.at[k]) for k, (x, y) in enumerate(zip(sources, copies))]
    for move in moves:
        move.start()
    for move in moves:
        move.wait()
    noise, kappa2, conduct, land = copies[:4]
    odd = lax.axis_index("lat") % 2
    top = rows - REACH
    loads = (
        lambda at: noise[at, :],
        lambda at: land[at, :].astype(jnp.float32),
        lambda at: conduct[1, at, :],
        lambda at: kappa2[at, :],
        lambda at: conduct[0, at, :],
        lambda at: conduct[2, at, :],
    )
    for out, side in ((first, odd), (second, 1 - odd)):
        k = 0
        for kind, load in enumerate(loads):
            count = FULL if kind < 3 else PART
            start = (1 - side) * (rows - count)
            for j in range(count):
                out[k] = load(pl.ds(start + j, levels, stride=rows))
                k += 1


def turned(planes, rows_of_planes):
    blocks = [jnp.concatenate(planes[j : j + REACH], axis=0) for j in range(0, rows_of_planes, REACH)]
    return jnp.concatenate([b.T for b in blocks], axis=1)


def coefficients(levels, band, kappa, east, north, upper, ocean):
    columns, lanes = kappa.shape
    lane = lax.broadcasted_iota(jnp.int32, (1, lanes), 1)
    row = lax.broadcasted_iota(jnp.int32, (columns, 1), 0)
    upper = jnp.where(lane % levels == levels - 1, 0.0, upper)
    south = jnp.where(lane % band < levels, 0.0, pltpu.roll(north, levels, 1))
    west = jnp.where(row == 0, 0.0, pltpu.roll(east, 1, 0))
    ocean_east = jnp.where(row == columns - 1, 1.0, pltpu.roll(ocean, columns - 1, 0))
    diagonal = ocean * (kappa + east + west + north + south + upper + pltpu.roll(upper, 1, 1))
    return diagonal, east * ocean * ocean_east, upper * ocean * pltpu.roll(ocean, lanes - 1, 1)


def store(statics, edge, diagonal, to_east, north, to_upper, ocean, east):
    for k, x in enumerate((diagonal, to_east, north, to_upper, ocean)):
        statics[k] = x
    edge[0:1] = east[east.shape[0] - 1 :]


def own_kernel(
    rows, levels, columns,
    noise, kappa2, conduct, land, weights,
    field, statics, edge, to_first, to_second,
):
    last_band = lax.axis_index("lat") == lax.axis_size("lat") - 1
    lon_odd = lax.axis_index("lon") % 2
    lanes = rows * levels

    def own(load):
        return turned([load(pl.ds(j, levels, stride=rows)) for j in range(rows)], rows)

    r = own(lambda at: noise[at, :])
    field[...] = r
    ocean = own(lambda at: land[at, :].astype(jnp.float32))
    north = own(lambda at: conduct[1, at, :])
    kappa = own(lambda at: kappa2[at, :])
    east = own(lambda at: conduct[0, at, :])
    upper = own(lambda at: conduct[2, at, :])
    lane = lax.broadcasted_iota(jnp.int32, (1, lanes), 1)
    north = jnp.where(last_band & (lane >= lanes - levels), 0.0, north)
    diagonal, to_east, to_upper = coefficients(levels, lanes, kappa, east, north, upper, ocean)
    store(statics, edge, diagonal, to_east, north, to_upper, ocean, east)
    m = dot(weights[...], r)[:4]
    end = columns - 1
    blank = jnp.zeros((5, lanes), jnp.float32)
    for_east = [m, r[end:], diagonal[end:], to_east[end - 1 : end], east[end:], ocean[end:], north[end:], to_upper[end:], blank]
    for_west = [m, r[:1], diagonal[:1], to_east[:1], east[:1], ocean[:1], north[:1], to_upper[:1], blank]
    for_east = jnp.concatenate(for_east, axis=0)
    for_west = jnp.concatenate(for_west, axis=0)
    to_first[...] = jnp.where(lon_odd == 0, for_east, for_west)
    to_second[...] = jnp.where(lon_odd == 0, for_west, for_east)


def ghost_kernel(levels, columns, got_second, got_first, field, statics, edge):
    lat_odd = lax.axis_index("lat") % 2
    group = REACH * levels

    def ghost(kind, north):
        count = FULL if kind < 3 else PART
        k = kind * FULL if kind < 3 else 3 * FULL + (kind - 3) * PART
        a = got_first[pl.ds(k, count)].reshape(count * levels, columns)
        b = jnp.where(inner_band(), got_second[pl.ds(k, count)], 0.0).reshape(count * levels, columns)
        from_first = (lat_odd == 0) if north else (lat_odd == 1)
        planes = jnp.where(from_first, a, b)
        if count == REACH:
            return planes.T
        blank = jnp.zeros((group - count * levels, columns), jnp.float32)
        return jnp.concatenate([planes, blank] if north else [blank, planes], axis=0).T

    r, ocean, north, kappa, east, upper = (
        jnp.concatenate([ghost(kind, False), ghost(kind, True)], axis=1) for kind in range(6)
    )
    field[...] = r
    diagonal, to_east, to_upper = coefficients(levels, group, kappa, east, north, upper, ocean)
    store(statics, edge, diagonal, to_east, north, to_upper, ocean, east)


def forward_kernel(group, *refs):
    lists, (second, first) = refs[:-2], refs[-2:]
    odd = lax.axis_index("lat") % 2
    k = 0
    for x in lists:
        count, lanes = x.shape
        low, high = x[:, 0:group], x[:, lanes - group :]
        first[pl.ds(k, count)] = jnp.where(odd == 0, high, low)
        second[pl.ds(k, count)] = jnp.where(odd == 0, low, high)
        k += count


def circle(spread, own, lists):
    lon_odd = lax.axis_index("lon") % 2
    first, second = lists[0], lists[1]
    told = [first[0:8], second[0:8], second[second.shape[0] - 8 :]] + [t[...] for t in lists[2:]]
    return dot(spread[lon_odd], jnp.concatenate([own] + told, axis=0))


def stack_kernel(own, got, out):
    out[0 : own.shape[0]] = own[...]
    out[own.shape[0] :] = got[0:8]


def quad_kernel(own, first, second, out):
    out[0:8] = own[0:8]
    out[8:16] = first[0:8]
    out[16:24] = second[0:8]
    out[24:32] = second[second.shape[0] - 8 :]


def stencil(v, east_v, west_v, d, e, w, n, u, levels):
    lanes = v.shape[1]
    return (
        d * v
        - e * east_v
        - w * west_v
        - n * pltpu.roll(v, lanes - levels, 1)
        - pltpu.roll(n * v, levels, 1)
        - u * pltpu.roll(v, lanes - 1, 1)
        - pltpu.roll(u * v, 1, 1)
    )


def apply_twice(levels, columns, v, f, statics, to_east, rim):
    diagonal, north, upper, ocean = (statics[k] for k in range(4))
    own = pl.ds(EDGE, columns)
    after = pl.ds(EDGE + 1, columns)
    before = pl.ds(EDGE - 1, columns)
    end = EDGE + columns
    e, w = to_east[own], to_east[before]
    f[own] = stencil(v[own], v[after], v[before], diagonal, e, w, north, upper, levels)
    pick = lambda a, b: jnp.concatenate([v[a : a + 1], v[b : b + 1], jnp.zeros((6, v.shape[1]), jnp.float32)], axis=0)
    g = stencil(
        pick(EDGE - 1, end), pick(EDGE, end + 1), pick(EDGE - 2, end - 1),
        rim[0], rim[1], rim[2], rim[3], rim[4], levels,
    )
    f[EDGE - 1 : EDGE] = g[0:1]
    f[end : end + 1] = g[1:2]
    second = stencil(f[own], f[after], f[before], diagonal, e, w, north, upper, levels)
    return jnp.where(ocean > 0.5, second, v[own])


def first_kernel(
    rows, levels, columns, others,
    own_field, own_statics, own_edge, field, ghost_statics, edge, spread, weights, side_second, side_first, *rest,
):
    received = rest[: 1 + others]
    precond, image, statics, to_east, rim, to_first, to_second, v, f = rest[1 + others :]
    lat_odd = lax.axis_index("lat") % 2
    even = lax.axis_index("lon") % 2 == 0
    group = REACH * levels
    lanes = rows * levels + 2 * group

    def joined(own, ghost):
        return jnp.concatenate([ghost[:, :group], own, ghost[:, group:]], axis=1)

    lists, k = [], 0
    for x in received:
        count = x.shape[0]
        a = side_first[pl.ds(k, count)]
        b = jnp.where(inner_band(), side_second[pl.ds(k, count)], 0.0)
        lists.append(jnp.concatenate([jnp.where(lat_odd == 1, a, b), x[...], jnp.where(lat_odd == 1, b, a)], axis=1))
        k += count
    v[...] = circle(spread, joined(own_field[...], field[...]), lists)

    lane = lax.broadcasted_iota(jnp.int32, (1, lanes), 1)
    first_of_band = ((lane >= group) & (lane < group + levels)) | ((lane >= lanes - group) & (lane < lanes - group + levels))

    def completed(diagonal, north, ocean):
        diagonal = diagonal + jnp.where(first_of_band, ocean * pltpu.roll(north, levels, 1), 0.0)
        return diagonal, north * ocean * pltpu.roll(ocean, lanes - levels, 1)

    ocean = joined(own_statics[4], ghost_statics[4])
    diagonal, north = completed(
        joined(own_statics[0], ghost_statics[0]), joined(own_statics[2], ghost_statics[2]), ocean
    )
    one, two = lists[0][0:16], lists[1][0:16]
    east_list, west_list = jnp.where(even, one, two), jnp.where(even, two, one)
    end = columns - 1
    row = lax.broadcasted_iota(jnp.int32, (columns, 1), 0)
    full_east = joined(own_statics[1], ghost_statics[1])
    full_east = jnp.where(row == end, full_east * east_list[8:9], full_east)
    to_east[pl.ds(EDGE, columns)] = full_east
    face_west = west_list[7:8] * west_list[8:9] * ocean[0:1]
    to_east[EDGE - 1 : EDGE] = face_west
    statics[0] = diagonal + jnp.where(row == 0, ocean * west_list[7:8], 0.0)
    statics[1] = north
    statics[2] = joined(own_statics[3], ghost_statics[3])
    statics[3] = ocean
    blank = jnp.zeros((6, lanes), jnp.float32)
    stack = lambda p, q: jnp.concatenate([p, q, blank], axis=0)
    last_face = joined(own_edge[0:1], edge[0:1])
    rim_ocean = stack(west_list[8:9], east_list[8:9])
    rim_diagonal, rim_north = completed(
        stack(west_list[5:6], east_list[5:6] + east_list[8:9] * last_face),
        stack(west_list[9:10], east_list[9:10]),
        rim_ocean,
    )
    rim[0] = rim_diagonal
    rim[1] = stack(face_west, east_list[6:7])
    rim[2] = stack(west_list[6:7], full_east[end:])
    rim[3] = rim_north
    rim[4] = stack(west_list[10:11], east_list[10:11])
    w0 = apply_twice(levels, columns, v, f, statics, to_east, rim)
    precond[...] = v[pl.ds(EDGE, columns)]
    image[...] = w0
    scaled = w0 * SCALE
    m = dot(weights[...], scaled)[:4]
    pad = jnp.zeros((3, m.shape[1]), jnp.float32)
    for_east = jnp.concatenate([m, scaled[end:], pad], axis=0)
    for_west = jnp.concatenate([m, scaled[:1], pad], axis=0)
    to_first[...] = jnp.where(even, for_east, for_west)
    to_second[...] = jnp.where(even, for_west, for_east)


def second_kernel(
    levels, columns, rows, others,
    field, precond, image, statics, spread, to_east, rim, *rest,
):
    received = rest[: 1 + others]
    again, along, sums, v, f = rest[1 + others :]
    v[...] = circle(spread, image[...] * SCALE, received)
    out = apply_twice(levels, columns, v, f, statics, to_east, rim)
    own = slice(REACH * levels, (REACH + rows) * levels)
    again[...] = v[pl.ds(EDGE, columns)][:, own]
    along[...] = out[:, own]
    r, p, w = field[...], precond[:, own], image[:, own]
    q, z = again[...], along[...]

    def part(x):
        s = jnp.sum(x, axis=0, keepdims=True)
        return sum(s[:, k : k + 128] for k in range(0, s.shape[1], 128))

    parts = [part(r * p), part(p * w), part(w * q), part(q * z), jnp.zeros((4, 128), jnp.float32)]
    sums[...] = jnp.concatenate(parts, axis=0)


def combine_kernel(rows, levels, sums, noise, precond, image, again, along, answer, left):
    total = jnp.sum(sums[...], axis=1, keepdims=True)
    energy, curve, mixed, last = total[0:1], total[1:2], total[2:3], total[3:4]
    alpha = energy / curve
    beta = alpha / SCALE
    growth = alpha * beta * mixed / energy
    step = energy * (growth - 1.0) / (beta * beta * last - growth * growth * curve)
    keep = alpha + step * growth
    back = step * beta
    own = slice(REACH * levels, (REACH + rows) * levels)
    x = keep * precond[:, own] - back * again[...]
    y = keep * image[:, own] - back * along[...]
    group = REACH * levels
    for j in range(0, rows, REACH):
        at = slice(j * levels, j * levels + group)
        xt, yt = x[:, at].T, y[:, at].T
        for i in range(REACH):
            part = slice(i * levels, (i + 1) * levels)
            to = pl.ds(j + i, levels, stride=rows)
            answer[to, :] = xt[part]
            left[to, :] = noise[to, :] - yt[part]


def doubling(count):
    steps = []
    while 2 ** len(steps) < count:
        steps.append(2 ** len(steps))
    return steps


def summed(x):
    count, bands = lax.axis_size("lon"), lax.axis_size("lat")
    x = x + lax.ppermute(x, "lon", [(i, i ^ 1) for i in range(count)])
    for step in doubling(count)[1:]:
        x = x + lax.ppermute(x, "lon", [(i, i ^ step ^ 1) for i in range(count)])
    for step in doubling(bands):
        pairs = [(i * bands + j, (i ^ 1) * bands + (j ^ step)) for i in range(count) for j in range(bands)]
        x = x + lax.ppermute(x, ("lon", "lat"), pairs)
    return x


def body(spread, weights, noise, kappa2, conduct, land):
    levels, rows, columns = noise.shape
    count = lax.axis_size("lon")
    others = count // 4
    flat = levels * rows
    lanes = (rows + 2 * REACH) * levels
    tall = columns + 2 * EDGE
    noise = noise.reshape(flat, columns)
    kappa2 = kappa2.reshape(flat, columns)
    land = land.reshape(flat, columns)
    conduct = conduct.reshape(3, flat, columns)

    sources = (noise, kappa2, conduct, land, spread, weights)
    planes = (PLANES, levels, columns)
    second, first, noise, kappa2, conduct, land, spread, weights = pl.pallas_call(
        functools.partial(band_kernel, rows, levels),
        out_shape=[pltpu.VMEM(planes, jnp.float32)] * 2 + [pltpu.VMEM(x.shape, x.dtype) for x in sources],
        in_specs=[pl.BlockSpec(memory_space=pltpu.HBM)] * len(sources),
        out_specs=whole(2 + len(sources)),
        scratch_shapes=[pltpu.SemaphoreType.DMA((len(sources),))],
        compiler_params=pltpu.CompilerParams(vmem_limit_bytes=8 << 20),
        name="band_kernel",
    )(*[pltpu.with_memory_space_constraint(x, pltpu.HBM) for x in sources])
    perm_a, perm_b = lat_perms(count, lax.axis_size("lat"))
    got_second = lax.ppermute(second, ("lon", "lat"), perm_b)
    got_first = lax.ppermute(first, ("lon", "lat"), perm_a)

    own_field, own_statics, own_edge, to_first, to_second = call(
        functools.partial(own_kernel, rows, levels, columns),
        [(columns, flat), (5, columns, flat), (8, flat), (16, flat), (16, flat)],
        noise, kappa2, conduct, land, weights,
    )
    lon_a, lon_b = lon_perms(count)

    def exchange(one, two):
        height, wide = two.shape
        got_one = lax.ppermute(one, "lon", lon_a)
        (two,) = call(stack_kernel, [(height + 8, wide)], two, got_one)
        got_two = lax.ppermute(two, "lon", lon_b)
        if count == 4:
            return [got_one, got_two]
        (four,) = call(quad_kernel, [(32, wide)], two, got_one, got_two)
        return [got_one, got_two] + [
            lax.ppermute(four, "lon", [(i, (i + d) % count) for i in range(count)]) for d in range(4, count, 4)
        ]

    told = exchange(to_first, to_second)
    heights = sum(x.shape[0] for x in told)
    group = REACH * levels
    side_second, side_first = call(functools.partial(forward_kernel, group), [(heights, group)] * 2, *told)
    side_second = lax.ppermute(side_second, ("lon", "lat"), perm_b)
    side_first = lax.ppermute(side_first, ("lon", "lat"), perm_a)
    field, ghost_statics, edge = call(
        functools.partial(ghost_kernel, levels, columns),
        [(columns, 2 * group), (5, columns, 2 * group), (8, 2 * group)],
        got_second, got_first,
    )
    precond, image, statics, to_east, rim, to_first, to_second = call(
        functools.partial(first_kernel, rows, levels, columns, others),
        [(columns, lanes), (columns, lanes), (4, columns, lanes), (tall, lanes), (5, 8, lanes), (8, lanes), (8, lanes)],
        own_field, own_statics, own_edge, field, ghost_statics, edge, spread, weights, side_second, side_first, *told,
        scratch=[(tall, lanes), (tall, lanes)],
    )
    told = exchange(to_first, to_second)
    again, along, sums = call(
        functools.partial(second_kernel, levels, columns, rows, others),
        [(columns, flat), (columns, flat), (8, 128)],
        own_field, precond, image, statics, spread, to_east, rim, *told,
        scratch=[(tall, lanes), (tall, lanes)],
    )
    sums = summed(sums)
    answer, left = call(
        functools.partial(combine_kernel, rows, levels),
        [(flat, columns), (flat, columns)],
        sums, noise, precond, image, again, along, last=True,
    )
    return answer.reshape(levels, rows, columns), left.reshape(levels, rows, columns)


def solution(mesh):
    def run(noise, kappa2, conduct, land):
        count = mesh.shape["lon"]
        spread, weights = circle_matrices(count, noise.shape[2] // count)
        return jax.shard_map(
            functools.partial(body, spread, weights),
            mesh=mesh,
            in_specs=(
                P("ens", "lat", "lon"),
                P(None, "lat", "lon"),
                P(None, None, "lat", "lon"),
                P(None, "lat", "lon"),
            ),
            out_specs=(P("ens", "lat", "lon"), P("ens", "lat", "lon")),
            check_vma=False,
        )(noise, kappa2, conduct, land)

    return run
```

```python
import functools
import math

import jax
import jax.numpy as jnp
import numpy as np
from jax import lax
from jax.experimental import pallas as pl
from jax.experimental.pallas import tpu as pltpu
from jax.sharding import PartitionSpec as P

base_kappa = 0.001
base_conduct = 1.0

SCALE = 2.0**-31
REACH = 4
EDGE = 8

HIGHEST = lax.Precision.HIGHEST


def dot(a, b):
    return jnp.dot(a, b, precision=HIGHEST, preferred_element_type=jnp.float32)


def circle_kernel(total):
    middle = 2.0 + base_kappa / base_conduct
    rho = (middle - math.sqrt(middle * middle - 4.0)) / 2.0
    height = 1.0 / (1.0 / rho - rho) / base_conduct
    wrap = rho**total
    shift = (1.0 + rho * rho) / (1.0 - rho * rho) + total * wrap / (1.0 - wrap)
    front = height * height / (1.0 - wrap)
    return rho, front, shift


def circle_matrices(count, columns):
    total = count * columns
    rho, front, shift = circle_kernel(total)

    def one_side(n):
        return front * rho**n * (n + shift)

    def both_sides(n):
        return one_side(n) + one_side(total - n)

    place = np.arange(columns)
    rows = columns + 2 * EDGE
    x = np.arange(rows) - EDGE
    used = (x >= -2) & (x < columns + 2)
    near = both_sides(np.abs(x[:, None] - place[None, :])) * used[:, None]
    back = columns - 1 - place
    moments = np.zeros((8, columns))
    moments[0] = rho**place
    moments[1] = place * rho**place
    moments[2] = rho**back
    moments[3] = back * rho**back

    def block(start, size, neighbour):
        start = start % count * columns
        a = start - x
        b = total - start + x - (size * columns - 1)
        out = np.zeros((rows, 8))
        out[:, 0] = front * rho**a * (a + shift)
        out[:, 1] = front * rho**a
        out[:, 2] = front * rho**b * (b + shift)
        out[:, 3] = front * rho**b
        amend = both_sides(1) - both_sides(-1)
        if neighbour == "east":
            out[EDGE + columns + 1, 4] = amend
        if neighbour == "west":
            out[EDGE - 2, 4] = amend
        return out * used[:, None]

    fours = range(4, count, 4)
    even = [block(1, 1, "east"), block(-2, 2, "west")] + [block(-2 - d, 4, "") for d in fours]
    odd = [block(-1, 1, "west"), block(1, 2, "east")] + [block(-1 - d, 4, "") for d in fours]
    far = np.stack([np.concatenate(even, axis=1), np.concatenate(odd, axis=1)])
    as_f32 = lambda m: np.asarray(m, np.float32)
    return as_f32(near), as_f32(far), as_f32(moments)


def lon_perms(count):
    first = [(i, i ^ 1) for i in range(count)]
    return first, [(i, (i - 1 + 2 * (i % 2)) % count) for i in range(count)]


def lat_perms(count, bands):
    first, second = [], []
    for i in range(count):
        for j in range(bands):
            k = j - 1 + 2 * (j % 2)
            first.append((i * bands + j, i * bands + (j ^ 1)))
            second.append((i * bands + j, i * bands + k if 0 <= k < bands else (i ^ 1) * bands + j))
    return first, second


def inner_band():
    return (lax.axis_index("lat") > 0) & (lax.axis_index("lat") < lax.axis_size("lat") - 1)


def whole(n):
    return [pl.BlockSpec(memory_space=pltpu.VMEM)] * n


def call(kernel, outs, *args, scratch=()):
    args = [pltpu.with_memory_space_constraint(a, pltpu.VMEM) for a in args]
    return pl.pallas_call(
        kernel,
        out_shape=[pltpu.VMEM(s, jnp.float32) for s in outs],
        in_specs=whole(len(args)),
        out_specs=whole(len(outs)),
        scratch_shapes=[pltpu.VMEM(s, jnp.float32) for s in scratch],
        compiler_params=pltpu.CompilerParams(vmem_limit_bytes=24 << 20),
        name=getattr(kernel, "func", kernel).__name__,
    )(*args)


FULL, PART = REACH, REACH - 1
PLANES = 3 * FULL + 3 * PART


def band_kernel(rows, levels, *refs):
    sources, (second, first), copies, sems = refs[:7], refs[7:9], refs[9:16], refs[16]
    moves = [pltpu.make_async_copy(x, y, sems.at[k]) for k, (x, y) in enumerate(zip(sources, copies))]
    for move in moves:
        move.start()
    for move in moves:
        move.wait()
    noise, kappa2, conduct, land = copies[:4]
    odd = lax.axis_index("lat") % 2
    top = rows - REACH
    loads = (
        lambda at: noise[at, :],
        lambda at: land[at, :].astype(jnp.float32),
        lambda at: conduct[1, at, :],
        lambda at: kappa2[at, :],
        lambda at: conduct[0, at, :],
        lambda at: conduct[2, at, :],
    )
    for out, side in ((first, odd), (second, 1 - odd)):
        k = 0
        for kind, load in enumerate(loads):
            count = FULL if kind < 3 else PART
            start = (1 - side) * (rows - count)
            for j in range(count):
                out[k] = load(pl.ds(start + j, levels, stride=rows))
                k += 1


def turned(planes, rows_of_planes):
    blocks = [jnp.concatenate(planes[j : j + REACH], axis=0) for j in range(0, rows_of_planes, REACH)]
    return jnp.concatenate([b.T for b in blocks], axis=1)


def coefficients(levels, band, kappa, east, north, upper, ocean):
    columns, lanes = kappa.shape
    lane = lax.broadcasted_iota(jnp.int32, (1, lanes), 1)
    row = lax.broadcasted_iota(jnp.int32, (columns, 1), 0)
    upper = jnp.where(lane % levels == levels - 1, 0.0, upper)
    south = jnp.where(lane % band < levels, 0.0, pltpu.roll(north, levels, 1))
    west = jnp.where(row == 0, 0.0, pltpu.roll(east, 1, 0))
    ocean_east = jnp.where(row == columns - 1, 1.0, pltpu.roll(ocean, columns - 1, 0))
    diagonal = ocean * (kappa + east + west + north + south + upper + pltpu.roll(upper, 1, 1))
    return diagonal, east * ocean * ocean_east, upper * ocean * pltpu.roll(ocean, lanes - 1, 1)


def store(statics, edge, diagonal, to_east, north, to_upper, ocean, east):
    for k, x in enumerate((diagonal, to_east, north, to_upper, ocean)):
        statics[k] = x
    edge[0:1] = east[east.shape[0] - 1 :]


def own_kernel(
    rows, levels, columns,
    noise, kappa2, conduct, land, weights,
    field, statics, edge, to_first, to_second,
):
    last_band = lax.axis_index("lat") == lax.axis_size("lat") - 1
    lon_odd = lax.axis_index("lon") % 2
    lanes = rows * levels

    def own(load):
        return turned([load(pl.ds(j, levels, stride=rows)) for j in range(rows)], rows)

    r = own(lambda at: noise[at, :])
    field[...] = r
    ocean = own(lambda at: land[at, :].astype(jnp.float32))
    north = own(lambda at: conduct[1, at, :])
    kappa = own(lambda at: kappa2[at, :])
    east = own(lambda at: conduct[0, at, :])
    upper = own(lambda at: conduct[2, at, :])
    lane = lax.broadcasted_iota(jnp.int32, (1, lanes), 1)
    north = jnp.where(last_band & (lane >= lanes - levels), 0.0, north)
    diagonal, to_east, to_upper = coefficients(levels, lanes, kappa, east, north, upper, ocean)
    store(statics, edge, diagonal, to_east, north, to_upper, ocean, east)
    m = dot(weights[...], r)[:4]
    end = columns - 1
    blank = jnp.zeros((5, lanes), jnp.float32)
    for_east = [m, r[end:], diagonal[end:], to_east[end - 1 : end], east[end:], ocean[end:], north[end:], to_upper[end:], blank]
    for_west = [m, r[:1], diagonal[:1], to_east[:1], east[:1], ocean[:1], north[:1], to_upper[:1], blank]
    for_east = jnp.concatenate(for_east, axis=0)
    for_west = jnp.concatenate(for_west, axis=0)
    to_first[...] = jnp.where(lon_odd == 0, for_east, for_west)
    to_second[...] = jnp.where(lon_odd == 0, for_west, for_east)


def ghost_kernel(levels, columns, got_second, got_first, near, spread, statics, edge):
    lat_odd = lax.axis_index("lat") % 2
    group = REACH * levels

    def ghost(kind, north):
        count = FULL if kind < 3 else PART
        k = kind * FULL if kind < 3 else 3 * FULL + (kind - 3) * PART
        a = got_first[pl.ds(k, count)].reshape(count * levels, columns)
        b = jnp.where(inner_band(), got_second[pl.ds(k, count)], 0.0).reshape(count * levels, columns)
        from_first = (lat_odd == 0) if north else (lat_odd == 1)
        planes = jnp.where(from_first, a, b)
        if count == REACH:
            return planes.T
        blank = jnp.zeros((group - count * levels, columns), jnp.float32)
        return jnp.concatenate([planes, blank] if north else [blank, planes], axis=0).T

    r, ocean, north, kappa, east, upper = (
        jnp.concatenate([ghost(kind, False), ghost(kind, True)], axis=1) for kind in range(6)
    )
    spread[...] = dot(near[...], r)
    diagonal, to_east, to_upper = coefficients(levels, group, kappa, east, north, upper, ocean)
    store(statics, edge, diagonal, to_east, north, to_upper, ocean, east)


def forward_kernel(group, *refs):
    lists, (second, first) = refs[:-2], refs[-2:]
    odd = lax.axis_index("lat") % 2
    k = 0
    for x in lists:
        count, lanes = x.shape
        low, high = x[:, 0:group], x[:, lanes - group :]
        first[pl.ds(k, count)] = jnp.where(odd == 0, high, low)
        second[pl.ds(k, count)] = jnp.where(odd == 0, low, high)
        k += count


def joint_moments(left, right, rho, width):
    c = rho**width
    return jnp.concatenate(
        [
            left[0:1] + c * right[0:1],
            left[1:2] + c * (right[1:2] + width * right[0:1]),
            right[2:3] + c * left[2:3],
            right[3:4] + c * (left[3:4] + width * left[2:3]),
        ],
        axis=0,
    )


def chip_kernel(rho, columns, own, got, out):
    even = lax.axis_index("lon") % 2 == 0
    mine, its = own[0:4], got[0:4]
    out[...] = own[...]
    out[0:4] = joint_moments(jnp.where(even, mine, its), jnp.where(even, its, mine), rho, columns)


def quad_kernel(rho, columns, mine, got, out):
    even = lax.axis_index("lon") % 2 == 0
    a, b = mine[0:4], got[0:4]
    m = joint_moments(jnp.where(even, b, a), jnp.where(even, a, b), rho, 2 * columns)
    out[...] = jnp.concatenate([m, jnp.zeros_like(m)], axis=0)


def near_kernel(near, field, spread):
    spread[...] = dot(near[...], field[...])


def told(far, lists):
    return dot(far[lax.axis_index("lon") % 2], jnp.concatenate([t[0:8] for t in lists], axis=0))


TILE = 8


def faces(v, n, s, u, low, levels):
    lanes = v.shape[1]
    return (
        n * pltpu.roll(v, lanes - levels, 1)
        + s * pltpu.roll(v, levels, 1)
        + u * pltpu.roll(v, lanes - 1, 1)
        + low * pltpu.roll(v, 1, 1)
    )


def apply_tile(levels, v, statics, at):
    d, e, w, n, s, u, low = (statics[k, pl.ds(at, TILE)] for k in range(7))
    i = at + EDGE
    here = v[pl.ds(i, TILE)]
    out = d * here - e * v[pl.ds(i + 1, TILE)] - w * v[pl.ds(i - 1, TILE)]
    return here, out - faces(here, n, s, u, low, levels)


def apply_rim(levels, columns, v, f, rim):
    end = EDGE + columns
    pick = lambda a, b: jnp.concatenate([v[a : a + 1], v[b : b + 1], jnp.zeros((6, v.shape[1]), jnp.float32)], axis=0)
    here = pick(EDGE - 1, end)
    g = rim[0] * here - rim[1] * pick(EDGE, end + 1) - rim[2] * pick(EDGE - 2, end - 1)
    g = g - faces(here, rim[3], rim[4], rim[5], rim[6], levels)
    f[EDGE - 1 : EDGE] = g[0:1]
    f[end : end + 1] = g[1:2]


def first_kernel(
    rows, levels, columns, others,
    own_spread, own_statics, own_edge, ghost_spread, ghost_statics, edge, far, weights, side_second, side_first, *rest,
):
    received = rest[: 1 + others]
    v, image, statics, rim, to_first, to_second, f, scaled = rest[1 + others :]
    lat_odd = lax.axis_index("lat") % 2
    even = lax.axis_index("lon") % 2 == 0
    group = REACH * levels
    lanes = rows * levels + 2 * group

    def joined(own, ghost):
        return jnp.concatenate([ghost[:, :group], own, ghost[:, group:]], axis=1)

    lists, k = [], 0
    for x in received:
        count = x.shape[0]
        a = side_first[pl.ds(k, count)]
        b = jnp.where(inner_band(), side_second[pl.ds(k, count)], 0.0)
        lists.append(jnp.concatenate([jnp.where(lat_odd == 1, a, b), x[...], jnp.where(lat_odd == 1, b, a)], axis=1))
        k += count
    v[...] = joined(own_spread[...], ghost_spread[...]) + told(far, lists)

    lane = lax.broadcasted_iota(jnp.int32, (1, lanes), 1)
    first_of_band = ((lane >= group) & (lane < group + levels)) | ((lane >= lanes - group) & (lane < lanes - group + levels))

    def completed(diagonal, north, ocean):
        diagonal = diagonal + jnp.where(first_of_band, ocean * pltpu.roll(north, levels, 1), 0.0)
        return diagonal, north * ocean * pltpu.roll(ocean, lanes - levels, 1)

    one, two = lists[0][0:16], lists[1][0:16]
    east_list, west_list = jnp.where(even, one, two), jnp.where(even, two, one)
    end = columns - 1
    for at in range(0, columns, TILE):
        tile = pl.ds(at, TILE)
        d, e, n, u, ocean = (joined(own_statics[k, tile], ghost_statics[k, tile]) for k in range(5))
        row = at + lax.broadcasted_iota(jnp.int32, (TILE, 1), 0)
        d, n = completed(d, n, ocean)
        if at == 0:
            face_west = west_list[7:8] * west_list[8:9] * ocean[0:1]
            d = d + jnp.where(row == 0, ocean * west_list[7:8], 0.0)
            carried = face_west
        if at + TILE == columns:
            e = jnp.where(row == end, e * east_list[8:9], e)
            last_east = e[TILE - 1 :]
        statics[0, tile] = d
        statics[1, tile] = e
        statics[2, tile] = jnp.where(row == at, carried, pltpu.roll(e, 1, 0))
        statics[3, tile] = n
        statics[4, tile] = pltpu.roll(n, levels, 1)
        statics[5, tile] = u
        statics[6, tile] = pltpu.roll(u, 1, 1)
        statics[7, tile] = ocean
        carried = e[TILE - 1 :]
    blank = jnp.zeros((6, lanes), jnp.float32)
    stack = lambda p, q: jnp.concatenate([p, q, blank], axis=0)
    last_face = joined(own_edge[0:1], edge[0:1])
    rim_diagonal, rim_north = completed(
        stack(west_list[5:6], east_list[5:6] + east_list[8:9] * last_face),
        stack(west_list[9:10], east_list[9:10]),
        stack(west_list[8:9], east_list[8:9]),
    )
    rim_upper = stack(west_list[10:11], east_list[10:11])
    rim[0] = rim_diagonal
    rim[1] = stack(face_west, east_list[6:7])
    rim[2] = stack(west_list[6:7], last_east)
    rim[3] = rim_north
    rim[4] = pltpu.roll(rim_north, levels, 1)
    rim[5] = rim_upper
    rim[6] = pltpu.roll(rim_upper, 1, 1)

    for at in range(0, columns, TILE):
        f[pl.ds(EDGE + at, TILE)] = apply_tile(levels, v, statics, at)[1]
    apply_rim(levels, columns, v, f, rim)
    for at in range(0, columns, TILE):
        second = apply_tile(levels, f, statics, at)[1]
        w = jnp.where(statics[7, pl.ds(at, TILE)] > 0.5, second, v[pl.ds(EDGE + at, TILE)])
        image[pl.ds(at, TILE)] = w
        scaled[pl.ds(at, TILE)] = w * SCALE
    m = dot(weights[...], scaled[...])[:4]
    pad = jnp.zeros((3, lanes), jnp.float32)
    for_east = jnp.concatenate([m, scaled[end:], pad], axis=0)
    for_west = jnp.concatenate([m, scaled[:1], pad], axis=0)
    to_first[...] = jnp.where(even, for_east, for_west)
    to_second[...] = jnp.where(even, for_west, for_east)


def lane_sums(tiles):
    total = functools.reduce(lambda a, b: a + b, tiles)
    s = jnp.sum(total, axis=0, keepdims=True)
    return functools.reduce(lambda a, b: a + b, [s[:, k : k + 128] for k in range(0, s.shape[1], 128)])


def own_lanes(rows, levels):
    return slice(REACH * levels, (REACH + rows) * levels)


def between_kernel(rows, levels, columns, near, field, precond, image, spread, sums):
    own = own_lanes(rows, levels)
    spread[...] = dot(near[...], image[...] * SCALE)
    energy, curve = [], []
    for at in range(0, columns, TILE):
        tile = pl.ds(at, TILE)
        p = precond[pl.ds(EDGE + at, TILE), own]
        energy.append(field[tile] * p)
        curve.append(p * image[tile, own])
    sums[...] = jnp.concatenate([lane_sums(energy), lane_sums(curve), jnp.zeros((6, 128), jnp.float32)], axis=0)


def second_kernel(levels, columns, rows, others, spread, early, image, statics, far, rim, *rest):
    received = rest[: 1 + others]
    v, f, sums = rest[1 + others :]
    v[...] = spread[...] + told(far, received)
    own = own_lanes(rows, levels)
    mixed, last = [], []
    for at in range(0, columns, TILE):
        tile = pl.ds(at, TILE)
        q, b = apply_tile(levels, v, statics, at)
        f[pl.ds(EDGE + at, TILE)] = b
        q, b, ocean = q[:, own], b[:, own], statics[7, tile, own]
        mixed.append(image[tile, own] * q)
        still = jnp.where(ocean > 0.5, b, q)
        last.append(still * still)
    apply_rim(levels, columns, v, f, rim)
    sums[...] = jnp.concatenate([early[0:2], lane_sums(mixed), lane_sums(last), early[4:8]], axis=0)


def turn_kernel(rows, levels, columns, precond, image, again, f, statics, *outs):
    z = outs[4]
    own = own_lanes(rows, levels)
    for at in range(0, columns, TILE):
        second = apply_tile(levels, f, statics, at)[1]
        tile = pl.ds(at, TILE)
        z[tile] = jnp.where(statics[7, tile] > 0.5, second, again[pl.ds(EDGE + at, TILE)])
    group = REACH * levels
    slab = pl.ds(EDGE, columns)
    for j in range(0, rows, REACH):
        at = slice(own.start + j * levels, own.start + j * levels + group)
        for out, x in zip(outs, (precond[slab, at], image[:, at], again[slab, at], z[:, at])):
            t = x.T
            for i in range(REACH):
                out[pl.ds(j + i, levels, stride=rows), :] = t[i * levels : (i + 1) * levels]


PIECES = 4


def combine_kernel(sums, noise, precond, image, again, along, answer, left, x, y, sems):
    total = jnp.sum(sums[...], axis=1, keepdims=True)
    energy, curve, mixed, last = total[0:1], total[1:2], total[2:3], total[3:4]
    alpha = energy / curve
    beta = alpha / SCALE
    growth = alpha * beta * mixed / energy
    step = energy * (growth - 1.0) / (beta * beta * last - growth * growth * curve)
    keep = alpha + step * growth
    back = step * beta
    size = noise.shape[0] // PIECES
    moves = []
    for k in range(PIECES):
        part = pl.ds(k * size, size)
        x[part] = keep * precond[part] - back * again[part]
        moves.append(pltpu.make_async_copy(x.at[part], answer.at[part], sems.at[0, k]))
        moves[-1].start()
        y[part] = noise[part] - (keep * image[part] - back * along[part])
        moves.append(pltpu.make_async_copy(y.at[part], left.at[part], sems.at[1, k]))
        moves[-1].start()
    for move in moves:
        move.wait()


def doubling(count):
    steps = []
    while 2 ** len(steps) < count:
        steps.append(2 ** len(steps))
    return steps


def summed(x):
    count, bands = lax.axis_size("lon"), lax.axis_size("lat")
    x = x + lax.ppermute(x, "lon", [(i, i ^ 1) for i in range(count)])
    for step in doubling(count)[1:]:
        x = x + lax.ppermute(x, "lon", [(i, i ^ step ^ 1) for i in range(count)])
    for step in doubling(bands):
        pairs = [(i * bands + j, (i ^ 1) * bands + (j ^ step)) for i in range(count) for j in range(bands)]
        x = x + lax.ppermute(x, ("lon", "lat"), pairs)
    return x


def body(near, far, weights, noise, kappa2, conduct, land):
    levels, rows, columns = noise.shape
    count = lax.axis_size("lon")
    others = count // 4
    flat = levels * rows
    group = REACH * levels
    lanes = flat + 2 * group
    tall = columns + 2 * EDGE
    rho = circle_kernel(count * columns)[0]
    noise = noise.reshape(flat, columns)
    kappa2 = kappa2.reshape(flat, columns)
    land = land.reshape(flat, columns)
    conduct = conduct.reshape(3, flat, columns)

    sources = (noise, kappa2, conduct, land, near, far, weights)
    planes = (PLANES, levels, columns)
    second, first, noise, kappa2, conduct, land, near, far, weights = pl.pallas_call(
        functools.partial(band_kernel, rows, levels),
        out_shape=[pltpu.VMEM(planes, jnp.float32)] * 2 + [pltpu.VMEM(x.shape, x.dtype) for x in sources],
        in_specs=[pl.BlockSpec(memory_space=pltpu.HBM)] * len(sources),
        out_specs=whole(2 + len(sources)),
        scratch_shapes=[pltpu.SemaphoreType.DMA((len(sources),))],
        compiler_params=pltpu.CompilerParams(vmem_limit_bytes=8 << 20),
        name="band_kernel",
    )(*[pltpu.with_memory_space_constraint(x, pltpu.HBM) for x in sources])
    lat_a, lat_b = lat_perms(count, lax.axis_size("lat"))
    to_band = lambda x, pairs: lax.ppermute(x, ("lon", "lat"), pairs)
    got_second, got_first = to_band(second, lat_b), to_band(first, lat_a)

    own_field, own_statics, own_edge, to_first, to_second = call(
        functools.partial(own_kernel, rows, levels, columns),
        [(columns, flat), (5, columns, flat), (8, flat), (16, flat), (16, flat)],
        noise, kappa2, conduct, land, weights,
    )
    lon_a, lon_b = lon_perms(count)

    def exchange(one, two):
        wide = two.shape[1]
        got_one = lax.ppermute(one, "lon", lon_a)
        (two,) = call(functools.partial(chip_kernel, rho, columns), [two.shape], two, got_one)
        got_two = lax.ppermute(two, "lon", lon_b)
        if count == 4:
            return [got_one, got_two]
        (four,) = call(functools.partial(quad_kernel, rho, columns), [(8, wide)], two, got_two)
        return [got_one, got_two] + [
            lax.ppermute(four, "lon", [(i, (i + d) % count) for i in range(count)]) for d in range(4, count, 4)
        ]

    lists = exchange(to_first, to_second)
    (own_spread,) = call(near_kernel, [(tall, flat)], near, own_field)
    heights = sum(x.shape[0] for x in lists)
    side_second, side_first = call(functools.partial(forward_kernel, group), [(heights, group)] * 2, *lists)
    side_second, side_first = to_band(side_second, lat_b), to_band(side_first, lat_a)
    ghost_spread, ghost_statics, edge = call(
        functools.partial(ghost_kernel, levels, columns),
        [(tall, 2 * group), (5, columns, 2 * group), (8, 2 * group)],
        got_second, got_first, near,
    )
    precond, image, statics, rim, to_first, to_second = call(
        functools.partial(first_kernel, rows, levels, columns, others),
        [(tall, lanes), (columns, lanes), (8, columns, lanes), (7, 8, lanes), (8, lanes), (8, lanes)],
        own_spread, own_statics, own_edge, ghost_spread, ghost_statics, edge, far, weights, side_second, side_first, *lists,
        scratch=[(tall, lanes), (columns, lanes)],
    )
    lists = exchange(to_first, to_second)
    spread, sums = call(
        functools.partial(between_kernel, rows, levels, columns),
        [(tall, lanes), (8, 128)],
        near, own_field, precond, image,
    )
    again, half, sums = call(
        functools.partial(second_kernel, levels, columns, rows, others),
        [(tall, lanes), (tall, lanes), (8, 128)],
        spread, sums, image, statics, far, rim, *lists,
    )
    sums = summed(sums)
    turned_back = call(
        functools.partial(turn_kernel, rows, levels, columns),
        [(flat, columns)] * 4 + [(columns, lanes)],
        precond, image, again, half, statics,
    )[:4]
    operands = [pltpu.with_memory_space_constraint(x, pltpu.VMEM) for x in (sums, noise, *turned_back)]
    answer, left = pl.pallas_call(
        combine_kernel,
        out_shape=[jax.ShapeDtypeStruct((flat, columns), jnp.float32)] * 2,
        in_specs=whole(len(operands)),
        out_specs=[pl.BlockSpec(memory_space=pltpu.HBM)] * 2,
        scratch_shapes=[pltpu.VMEM((flat, columns), jnp.float32)] * 2 + [pltpu.SemaphoreType.DMA((2, PIECES))],
        compiler_params=pltpu.CompilerParams(vmem_limit_bytes=8 << 20),
        name="combine_kernel",
    )(*operands)
    return answer.reshape(levels, rows, columns), left.reshape(levels, rows, columns)


def solution(mesh):
    def run(noise, kappa2, conduct, land):
        count = mesh.shape["lon"]
        matrices = circle_matrices(count, noise.shape[2] // count)
        return jax.shard_map(
            functools.partial(body, *matrices),
            mesh=mesh,
            in_specs=(
                P("ens", "lat", "lon"),
                P(None, "lat", "lon"),
                P(None, None, "lat", "lon"),
                P(None, "lat", "lon"),
            ),
            out_specs=(P("ens", "lat", "lon"), P("ens", "lat", "lon")),
            check_vma=False,
        )(noise, kappa2, conduct, land)

    return run
```

```python
import functools
import math

import jax
import jax.numpy as jnp
import numpy as np
from jax import lax
from jax.experimental import pallas as pl
from jax.experimental.pallas import tpu as pltpu
from jax.sharding import PartitionSpec as P

base_kappa = 0.001
base_conduct = 1.0

SCALE = 2.0**-31
REACH = 4
TILE = 8
EDGE = 8

HIGHEST = lax.Precision.HIGHEST


def dot(a, b):
    return jnp.dot(a, b, precision=HIGHEST, preferred_element_type=jnp.float32)


def circle_kernel(total):
    middle = 2.0 + base_kappa / base_conduct
    rho = (middle - math.sqrt(middle * middle - 4.0)) / 2.0
    height = 1.0 / (1.0 / rho - rho) / base_conduct
    wrap = rho**total
    shift = (1.0 + rho * rho) / (1.0 - rho * rho) + total * wrap / (1.0 - wrap)
    front = height * height / (1.0 - wrap)
    return rho, front, shift


def circle_matrices(count, columns):
    total = count * columns
    rho, front, shift = circle_kernel(total)

    def one_side(n):
        return front * rho**n * (n + shift)

    def both_sides(n):
        return one_side(n) + one_side(total - n)

    place = np.arange(columns)
    rows = columns + 2 * EDGE
    x = np.arange(rows) - EDGE
    used = (x >= -2) & (x < columns + 2)
    near = both_sides(np.abs(x[:, None] - place[None, :])) * used[:, None]
    back = columns - 1 - place
    moments = np.zeros((8, columns))
    moments[0] = rho**place
    moments[1] = place * rho**place
    moments[2] = rho**back
    moments[3] = back * rho**back

    def block(start, size, neighbour):
        start = start % count * columns
        a = start - x
        b = total - start + x - (size * columns - 1)
        out = np.zeros((rows, 8))
        out[:, 0] = front * rho**a * (a + shift)
        out[:, 1] = front * rho**a
        out[:, 2] = front * rho**b * (b + shift)
        out[:, 3] = front * rho**b
        amend = both_sides(1) - both_sides(-1)
        if neighbour == "east":
            out[EDGE + columns + 1, 4] = amend
        if neighbour == "west":
            out[EDGE - 2, 4] = amend
        return out * used[:, None]

    fours = range(4, count, 4)
    even = [block(1, 1, "east"), block(-2, 2, "west")] + [block(-2 - d, 4, "") for d in fours]
    odd = [block(-1, 1, "west"), block(1, 2, "east")] + [block(-1 - d, 4, "") for d in fours]
    far = np.stack([np.concatenate(even, axis=1), np.concatenate(odd, axis=1)])
    far = np.pad(far, ((0, 0), (0, 0), (0, -far.shape[2] % 16))).astype(np.float32)
    high, middle, low = thirds(far, lambda x: x.astype(np.float32))
    far = np.concatenate([high, high, middle, high, middle, low], axis=2)
    columns_of = np.broadcast_to(moments[:4, :, None], (4, columns, 128))
    as_f32 = lambda m: np.asarray(m, np.float32)
    return as_f32(near), far, as_f32(moments), as_f32(columns_of)


def lon_perms(count):
    first = [(i, i ^ 1) for i in range(count)]
    return first, [(i, (i - 1 + 2 * (i % 2)) % count) for i in range(count)]


def lat_perms(count, bands):
    first, second = [], []
    for i in range(count):
        for j in range(bands):
            k = j - 1 + 2 * (j % 2)
            first.append((i * bands + j, i * bands + (j ^ 1)))
            second.append((i * bands + j, i * bands + k if 0 <= k < bands else (i ^ 1) * bands + j))
    return first, second


def inner_band():
    return (lax.axis_index("lat") > 0) & (lax.axis_index("lat") < lax.axis_size("lat") - 1)


def lane_roll(x, by):
    count = x.shape[1] // 128
    skip, by = divmod(by % x.shape[1], 128)
    parts = [x[:, k * 128 : (k + 1) * 128] for k in range(count)]
    if by:
        turned = [pltpu.roll(p, by, 1) for p in parts]
        lane = lax.broadcasted_iota(jnp.int32, (1, 128), 1)
        parts = [jnp.where(lane < by, turned[k - 1], turned[k]) for k in range(count)]
    return jnp.concatenate([parts[(k - skip) % count] for k in range(count)], axis=1)


def thirds(x, cast):
    high = x.astype(jnp.bfloat16)
    rest = x - cast(high)
    middle = rest.astype(jnp.bfloat16)
    return high, middle, (rest - cast(middle)).astype(jnp.bfloat16)


def whole(n):
    return [pl.BlockSpec(memory_space=pltpu.VMEM)] * n


def call(kernel, outs, *args, scratch=()):
    args = [pltpu.with_memory_space_constraint(a, pltpu.VMEM) for a in args]
    return pl.pallas_call(
        kernel,
        out_shape=[pltpu.VMEM(s, jnp.float32) for s in outs],
        in_specs=whole(len(args)),
        out_specs=whole(len(outs)),
        scratch_shapes=[pltpu.VMEM(s, jnp.float32) for s in scratch],
        compiler_params=pltpu.CompilerParams(vmem_limit_bytes=24 << 20),
        name=getattr(kernel, "func", kernel).__name__,
    )(*args)


FULL, PART = REACH, REACH - 1
PLANES = 3 * FULL + 3 * PART


def band_kernel(rows, levels, *refs):
    sources, (second, first), copies, sems = refs[:8], refs[8:10], refs[10:18], refs[18]
    moves = [pltpu.make_async_copy(x, y, sems.at[k]) for k, (x, y) in enumerate(zip(sources, copies))]
    for move in moves:
        move.start()
    for move in moves:
        move.wait()
    noise, kappa2, conduct, land = copies[:4]
    odd = lax.axis_index("lat") % 2
    top = rows - REACH
    loads = (
        lambda at: noise[at, :],
        lambda at: land[at, :].astype(jnp.float32),
        lambda at: conduct[1, at, :],
        lambda at: kappa2[at, :],
        lambda at: conduct[0, at, :],
        lambda at: conduct[2, at, :],
    )
    for out, side in ((first, odd), (second, 1 - odd)):
        k = 0
        for kind, load in enumerate(loads):
            count = FULL if kind < 3 else PART
            start = (1 - side) * (rows - count)
            for j in range(count):
                out[k] = load(pl.ds(start + j, levels, stride=rows))
                k += 1


def turned(planes, rows_of_planes):
    blocks = [jnp.concatenate(planes[j : j + REACH], axis=0) for j in range(0, rows_of_planes, REACH)]
    return jnp.concatenate([b.T for b in blocks], axis=1)


def coefficients(levels, band, kappa, east, north, upper, ocean):
    columns, lanes = kappa.shape
    lane = lax.broadcasted_iota(jnp.int32, (1, lanes), 1)
    row = lax.broadcasted_iota(jnp.int32, (columns, 1), 0)
    upper = jnp.where(lane % levels == levels - 1, 0.0, upper)
    south = jnp.where(lane % band < levels, 0.0, lane_roll(north, levels))
    west = jnp.where(row == 0, 0.0, pltpu.roll(east, 1, 0))
    ocean_east = jnp.where(row == columns - 1, 1.0, pltpu.roll(ocean, columns - 1, 0))
    diagonal = ocean * (kappa + east + west + north + south + upper + lane_roll(upper, 1))
    return diagonal, east * ocean * ocean_east, upper * ocean * lane_roll(ocean, -1)


def own_kernel(
    rows, levels, columns,
    noise, kappa2, conduct, land, weights,
    field, statics, edge, to_first, to_second,
):
    last_band = lax.axis_index("lat") == lax.axis_size("lat") - 1
    lon_odd = lax.axis_index("lon") % 2
    lanes = rows * levels

    def own(load):
        return turned([load(pl.ds(j, levels, stride=rows)) for j in range(rows)], rows)

    r = own(lambda at: noise[at, :])
    field[...] = r
    ocean = own(lambda at: land[at, :].astype(jnp.float32))
    north = own(lambda at: conduct[1, at, :])
    kappa = own(lambda at: kappa2[at, :])
    east = own(lambda at: conduct[0, at, :])
    upper = own(lambda at: conduct[2, at, :])
    lane = lax.broadcasted_iota(jnp.int32, (1, lanes), 1)
    north = jnp.where(last_band & (lane >= lanes - levels), 0.0, north)
    diagonal, to_east, to_upper = coefficients(levels, lanes, kappa, east, north, upper, ocean)
    for k, x in enumerate((diagonal, to_east, north, to_upper, ocean)):
        statics[k] = x
    edge[0:1] = east[columns - 1 :]
    m = dot(weights[...], r)[:4]
    end = columns - 1
    blank = jnp.zeros((5, lanes), jnp.float32)
    for_east = [m, r[end:], diagonal[end:], to_east[end - 1 : end], east[end:], ocean[end:], north[end:], to_upper[end:], blank]
    for_west = [m, r[:1], diagonal[:1], to_east[:1], east[:1], ocean[:1], north[:1], to_upper[:1], blank]
    for_east = jnp.concatenate(for_east, axis=0)
    for_west = jnp.concatenate(for_west, axis=0)
    to_first[...] = jnp.where(lon_odd == 0, for_east, for_west)
    to_second[...] = jnp.where(lon_odd == 0, for_west, for_east)


def ghost_kernel(levels, columns, got_second, got_first, near, own, spread, statics, edge):
    lat_odd = lax.axis_index("lat") % 2
    group = REACH * levels

    def ghost(kind, north):
        count = FULL if kind < 3 else PART
        k = kind * FULL if kind < 3 else 3 * FULL + (kind - 3) * PART
        a = got_first[pl.ds(k, count)].reshape(count * levels, columns)
        b = jnp.where(inner_band(), got_second[pl.ds(k, count)], 0.0).reshape(count * levels, columns)
        from_first = (lat_odd == 0) if north else (lat_odd == 1)
        planes = jnp.where(from_first, a, b)
        if count == REACH:
            return planes.T
        blank = jnp.zeros((group - count * levels, columns), jnp.float32)
        return jnp.concatenate([planes, blank] if north else [blank, planes], axis=0).T

    r, ocean, north, kappa, east, upper = (
        jnp.concatenate([ghost(kind, False), ghost(kind, True)], axis=1) for kind in range(6)
    )
    spread[...] = dot(near[...], r)
    diagonal, to_east, to_upper = coefficients(levels, group, kappa, east, north, upper, ocean)
    edge[0:1] = east[columns - 1 :]
    for at in range(0, columns, TILE):
        tile = slice(at, at + TILE)
        d, e, n, u, o = (
            joined(own[k, pl.ds(at, TILE)], x[tile]) for k, x in enumerate((diagonal, to_east, north, to_upper, ocean))
        )
        d, n = completed(levels, group, d, n, o)
        row = lax.broadcasted_iota(jnp.int32, (TILE, 1), 0)
        w = pltpu.roll(e, 1, 0)
        w = jnp.where(row == 0, carried, w) if at else w
        carried = e[TILE - 1 :]
        for k, x in enumerate((d, e, w, n, lane_roll(n, levels), u, lane_roll(u, 1), o)):
            statics[k, pl.ds(at, TILE)] = x


def forward_kernel(group, *refs):
    lists, (second, first) = refs[:-2], refs[-2:]
    odd = lax.axis_index("lat") % 2
    k = 0
    for x in lists:
        count, lanes = x.shape
        low, high = x[:, 0:group], x[:, lanes - group :]
        first[pl.ds(k, count)] = jnp.where(odd == 0, high, low)
        second[pl.ds(k, count)] = jnp.where(odd == 0, low, high)
        k += count


def joint_moments(left, right, rho, width):
    c = rho**width
    return jnp.concatenate(
        [
            left[0:1] + c * right[0:1],
            left[1:2] + c * (right[1:2] + width * right[0:1]),
            right[2:3] + c * left[2:3],
            right[3:4] + c * (left[3:4] + width * left[2:3]),
        ],
        axis=0,
    )


def chip_kernel(rho, columns, own, got, out):
    even = lax.axis_index("lon") % 2 == 0
    mine, its = own[0:4], got[0:4]
    out[...] = own[...]
    out[0:4] = joint_moments(jnp.where(even, mine, its), jnp.where(even, its, mine), rho, columns)


def quad_kernel(rho, columns, mine, got, out):
    even = lax.axis_index("lon") % 2 == 0
    a, b = mine[0:4], got[0:4]
    m = joint_moments(jnp.where(even, b, a), jnp.where(even, a, b), rho, 2 * columns)
    out[...] = jnp.concatenate([m, jnp.zeros_like(m)], axis=0)


def near_kernel(near, field, spread):
    spread[...] = dot(near[...], field[...])


def told(far, lists):
    x = jnp.concatenate([t[0:8] for t in lists], axis=0)
    if x.shape[0] % 16:
        x = jnp.concatenate([x, jnp.zeros((8, x.shape[1]), jnp.float32)], axis=0)
    high, middle, low = thirds(x, lambda p: p.astype(jnp.float32))
    stacked = jnp.concatenate([high, middle, high, low, middle, high], axis=0)
    return jnp.dot(far[lax.axis_index("lon") % 2], stacked, preferred_element_type=jnp.float32)


def faces(v, n, s, u, low, levels):
    return n * lane_roll(v, -levels) + s * lane_roll(v, levels) + u * lane_roll(v, -1) + low * lane_roll(v, 1)


def apply_tile(levels, v, statics, ends, at):
    source, k = statics, at
    if at == 0:
        source, k = ends, 0
    if at + TILE == statics.shape[1]:
        source, k = ends, TILE
    d, e, w, n, s, u, low = (source[i, pl.ds(k, TILE)] for i in range(7))
    i = at + EDGE
    here = v[pl.ds(i, TILE)]
    out = d * here - e * v[pl.ds(i + 1, TILE)] - w * v[pl.ds(i - 1, TILE)]
    return here, out - faces(here, n, s, u, low, levels)


def apply_rim(levels, columns, v, f, rim):
    end = EDGE + columns
    pick = lambda a, b: jnp.concatenate([v[a : a + 1], v[b : b + 1], jnp.zeros((6, v.shape[1]), jnp.float32)], axis=0)
    here = pick(EDGE - 1, end)
    g = rim[0] * here - rim[1] * pick(EDGE, end + 1) - rim[2] * pick(EDGE - 2, end - 1)
    g = g - faces(here, rim[3], rim[4], rim[5], rim[6], levels)
    f[EDGE - 1 : EDGE] = g[0:1]
    f[end : end + 1] = g[1:2]


def joined(own, ghost):
    group = ghost.shape[1] // 2
    return jnp.concatenate([ghost[:, :group], own, ghost[:, group:]], axis=1)


def completed(levels, group, diagonal, north, ocean):
    lanes = ocean.shape[1]
    lane = lax.broadcasted_iota(jnp.int32, (1, lanes), 1)
    first_of_band = ((lane >= group) & (lane < group + levels)) | ((lane >= lanes - group) & (lane < lanes - group + levels))
    diagonal = diagonal + jnp.where(first_of_band, ocean * lane_roll(north, levels), 0.0)
    return diagonal, north * ocean * lane_roll(ocean, -levels)


def first_kernel(
    rows, levels, columns, others,
    own_spread, own_edge, ghost_spread, statics, edge, far, weights, side_second, side_first, *rest,
):
    received = rest[: 1 + others]
    v, image, ends, rim, to_first, to_second, f = rest[1 + others :]
    lat_odd = lax.axis_index("lat") % 2
    even = lax.axis_index("lon") % 2 == 0
    group = REACH * levels
    lanes = rows * levels + 2 * group
    lists, k = [], 0
    for x in received:
        count = x.shape[0]
        a = side_first[pl.ds(k, count)]
        b = jnp.where(inner_band(), side_second[pl.ds(k, count)], 0.0)
        lists.append(jnp.concatenate([jnp.where(lat_odd == 1, a, b), x[...], jnp.where(lat_odd == 1, b, a)], axis=1))
        k += count
    v[...] = joined(own_spread[...], ghost_spread[...]) + told(far, lists)

    one, two = lists[0], lists[1]
    east_list, west_list = jnp.where(even, one, two), jnp.where(even, two, one)
    end = columns - 1
    low_tile, high_tile = pl.ds(0, TILE), pl.ds(columns - TILE, TILE)
    for k in range(7):
        ends[k, 0:TILE] = statics[k, low_tile]
        ends[k, TILE : 2 * TILE] = statics[k, high_tile]
    ocean = statics[7, 0:1]
    face_west = west_list[7:8] * west_list[8:9] * ocean
    last_east = statics[1, end:] * east_list[8:9]
    ends[0, 0:1] = statics[0, 0:1] + ocean * west_list[7:8]
    ends[2, 0:1] = face_west
    ends[1, 2 * TILE - 1 : 2 * TILE] = last_east
    blank = jnp.zeros((6, lanes), jnp.float32)
    stack = lambda p, q: jnp.concatenate([p, q, blank], axis=0)
    last_face = joined(own_edge[0:1], edge[0:1])
    rim_diagonal, rim_north = completed(
        levels, group,
        stack(west_list[5:6], east_list[5:6] + east_list[8:9] * last_face),
        stack(west_list[9:10], east_list[9:10]),
        stack(west_list[8:9], east_list[8:9]),
    )
    rim_upper = stack(west_list[10:11], east_list[10:11])
    rim[0] = rim_diagonal
    rim[1] = stack(face_west, east_list[6:7])
    rim[2] = stack(west_list[6:7], last_east)
    rim[3] = rim_north
    rim[4] = lane_roll(rim_north, levels)
    rim[5] = rim_upper
    rim[6] = lane_roll(rim_upper, 1)

    for at in range(0, columns, TILE):
        f[pl.ds(EDGE + at, TILE)] = apply_tile(levels, v, statics, ends, at)[1]
    apply_rim(levels, columns, v, f, rim)
    m = [0.0] * 4
    for at in range(0, columns, TILE):
        tile = pl.ds(at, TILE)
        second = apply_tile(levels, f, statics, ends, at)[1]
        w = jnp.where(statics[7, tile] > 0.5, second, v[pl.ds(EDGE + at, TILE)])
        image[tile] = w
        for k in range(4):
            spread = weights[k, tile]
            m[k] = m[k] + w * jnp.concatenate([spread] * (lanes // 128), axis=1)
    m = [jnp.sum(x, axis=0, keepdims=True) * SCALE for x in m]
    pad = jnp.zeros((3, lanes), jnp.float32)
    for_east = jnp.concatenate(m + [image[end:] * SCALE, pad], axis=0)
    for_west = jnp.concatenate(m + [image[:1] * SCALE, pad], axis=0)
    to_first[...] = jnp.where(even, for_east, for_west)
    to_second[...] = jnp.where(even, for_west, for_east)


def lane_sums(tiles):
    total = functools.reduce(lambda a, b: a + b, tiles)
    s = jnp.sum(total, axis=0, keepdims=True)
    return functools.reduce(lambda a, b: a + b, [s[:, k : k + 128] for k in range(0, s.shape[1], 128)])


def own_lanes(rows, levels):
    return slice(REACH * levels, (REACH + rows) * levels)


def between_kernel(rows, levels, columns, near, field, precond, image, spread, sums):
    own = own_lanes(rows, levels)
    spread[...] = dot(near[...], image[...] * SCALE)
    energy, curve = [], []
    for at in range(0, columns, TILE):
        tile = pl.ds(at, TILE)
        p = precond[pl.ds(EDGE + at, TILE), own]
        energy.append(field[tile] * p)
        curve.append(p * image[tile, own])
    sums[...] = jnp.concatenate([lane_sums(energy), lane_sums(curve), jnp.zeros((6, 128), jnp.float32)], axis=0)


def second_kernel(levels, columns, rows, others, spread, early, image, statics, ends, far, rim, *rest):
    received = rest[: 1 + others]
    v, f, sums = rest[1 + others :]
    v[...] = spread[...] + told(far, received)
    own = own_lanes(rows, levels)
    mixed, last = [], []
    for at in range(0, columns, TILE):
        tile = pl.ds(at, TILE)
        q, b = apply_tile(levels, v, statics, ends, at)
        f[pl.ds(EDGE + at, TILE)] = b
        q, b, ocean = q[:, own], b[:, own], statics[7, tile, own]
        mixed.append(image[tile, own] * q)
        still = jnp.where(ocean > 0.5, b, q)
        last.append(still * still)
    apply_rim(levels, columns, v, f, rim)
    sums[...] = jnp.concatenate([early[0:2], lane_sums(mixed), lane_sums(last), early[4:8]], axis=0)


def turn_kernel(rows, levels, columns, precond, image, again, f, statics, ends, *outs):
    z = outs[4]
    own = own_lanes(rows, levels)
    for at in range(0, columns, TILE):
        second = apply_tile(levels, f, statics, ends, at)[1]
        tile = pl.ds(at, TILE)
        z[tile] = jnp.where(statics[7, tile] > 0.5, second, again[pl.ds(EDGE + at, TILE)])
    group = REACH * levels
    slab = pl.ds(EDGE, columns)
    for j in range(0, rows, REACH):
        at = slice(own.start + j * levels, own.start + j * levels + group)
        for out, x in zip(outs, (precond[slab, at], image[:, at], again[slab, at], z[:, at])):
            t = x.T
            for i in range(REACH):
                out[pl.ds(j + i, levels, stride=rows), :] = t[i * levels : (i + 1) * levels]


PIECES = 4


def combine_kernel(sums, noise, precond, image, again, along, answer, left, x, y, sems):
    total = jnp.sum(sums[...], axis=1, keepdims=True)
    energy, curve, mixed, last = total[0:1], total[1:2], total[2:3], total[3:4]
    alpha = energy / curve
    beta = alpha / SCALE
    growth = alpha * beta * mixed / energy
    step = energy * (growth - 1.0) / (beta * beta * last - growth * growth * curve)
    keep = alpha + step * growth
    back = step * beta
    size = noise.shape[0] // PIECES
    moves = []
    for k in range(PIECES):
        part = pl.ds(k * size, size)
        x[part] = keep * precond[part] - back * again[part]
        moves.append(pltpu.make_async_copy(x.at[part], answer.at[part], sems.at[0, k]))
        moves[-1].start()
        y[part] = noise[part] - (keep * image[part] - back * along[part])
        moves.append(pltpu.make_async_copy(y.at[part], left.at[part], sems.at[1, k]))
        moves[-1].start()
    for move in moves:
        move.wait()


def doubling(count):
    steps = []
    while 2 ** len(steps) < count:
        steps.append(2 ** len(steps))
    return steps


def summed(x):
    count, bands = lax.axis_size("lon"), lax.axis_size("lat")
    x = x + lax.ppermute(x, "lon", [(i, i ^ 1) for i in range(count)])
    for step in doubling(count)[1:]:
        x = x + lax.ppermute(x, "lon", [(i, i ^ step ^ 1) for i in range(count)])
    for step in doubling(bands):
        pairs = [(i * bands + j, (i ^ 1) * bands + (j ^ step)) for i in range(count) for j in range(bands)]
        x = x + lax.ppermute(x, ("lon", "lat"), pairs)
    return x


def body(near, far, weights, columns_of, noise, kappa2, conduct, land):
    levels, rows, columns = noise.shape
    count = lax.axis_size("lon")
    others = count // 4
    flat = levels * rows
    group = REACH * levels
    lanes = flat + 2 * group
    tall = columns + 2 * EDGE
    rho = circle_kernel(count * columns)[0]
    noise = noise.reshape(flat, columns)
    kappa2 = kappa2.reshape(flat, columns)
    land = land.reshape(flat, columns)
    conduct = conduct.reshape(3, flat, columns)

    sources = (noise, kappa2, conduct, land, near, far, weights, columns_of)
    planes = (PLANES, levels, columns)
    second, first, noise, kappa2, conduct, land, near, far, weights, columns_of = pl.pallas_call(
        functools.partial(band_kernel, rows, levels),
        out_shape=[pltpu.VMEM(planes, jnp.float32)] * 2 + [pltpu.VMEM(x.shape, x.dtype) for x in sources],
        in_specs=[pl.BlockSpec(memory_space=pltpu.HBM)] * len(sources),
        out_specs=whole(2 + len(sources)),
        scratch_shapes=[pltpu.SemaphoreType.DMA((len(sources),))],
        compiler_params=pltpu.CompilerParams(vmem_limit_bytes=8 << 20),
        name="band_kernel",
    )(*[pltpu.with_memory_space_constraint(x, pltpu.HBM) for x in sources])
    lat_a, lat_b = lat_perms(count, lax.axis_size("lat"))
    to_band = lambda x, pairs: lax.ppermute(x, ("lon", "lat"), pairs)
    got_second, got_first = to_band(second, lat_b), to_band(first, lat_a)

    own_field, own_statics, own_edge, to_first, to_second = call(
        functools.partial(own_kernel, rows, levels, columns),
        [(columns, flat), (5, columns, flat), (8, flat), (16, flat), (16, flat)],
        noise, kappa2, conduct, land, weights,
    )
    lon_a, lon_b = lon_perms(count)

    def exchange(one, two):
        wide = two.shape[1]
        got_one = lax.ppermute(one, "lon", lon_a)
        (two,) = call(functools.partial(chip_kernel, rho, columns), [two.shape], two, got_one)
        got_two = lax.ppermute(two, "lon", lon_b)
        if count == 4:
            return [got_one, got_two]
        (four,) = call(functools.partial(quad_kernel, rho, columns), [(8, wide)], two, got_two)
        return [got_one, got_two] + [
            lax.ppermute(four, "lon", [(i, (i + d) % count) for i in range(count)]) for d in range(4, count, 4)
        ]

    lists = exchange(to_first, to_second)
    (own_spread,) = call(near_kernel, [(tall, flat)], near, own_field)
    heights = sum(x.shape[0] for x in lists)
    side_second, side_first = call(functools.partial(forward_kernel, group), [(heights, group)] * 2, *lists)
    side_second, side_first = to_band(side_second, lat_b), to_band(side_first, lat_a)
    ghost_spread, statics, edge = call(
        functools.partial(ghost_kernel, levels, columns),
        [(tall, 2 * group), (8, columns, lanes), (8, 2 * group)],
        got_second, got_first, near, own_statics,
    )
    precond, image, ends, rim, to_first, to_second = call(
        functools.partial(first_kernel, rows, levels, columns, others),
        [(tall, lanes), (columns, lanes), (7, 2 * TILE, lanes), (7, 8, lanes), (8, lanes), (8, lanes)],
        own_spread, own_edge, ghost_spread, statics, edge, far, columns_of, side_second, side_first, *lists,
        scratch=[(tall, lanes)],
    )
    lists = exchange(to_first, to_second)
    spread, sums = call(
        functools.partial(between_kernel, rows, levels, columns),
        [(tall, lanes), (8, 128)],
        near, own_field, precond, image,
    )
    again, half, sums = call(
        functools.partial(second_kernel, levels, columns, rows, others),
        [(tall, lanes), (tall, lanes), (8, 128)],
        spread, sums, image, statics, ends, far, rim, *lists,
    )
    sums = summed(sums)
    turned_back = call(
        functools.partial(turn_kernel, rows, levels, columns),
        [(flat, columns)] * 4 + [(columns, lanes)],
        precond, image, again, half, statics, ends,
    )[:4]
    operands = [pltpu.with_memory_space_constraint(x, pltpu.VMEM) for x in (sums, noise, *turned_back)]
    answer, left = pl.pallas_call(
        combine_kernel,
        out_shape=[jax.ShapeDtypeStruct((flat, columns), jnp.float32)] * 2,
        in_specs=whole(len(operands)),
        out_specs=[pl.BlockSpec(memory_space=pltpu.HBM)] * 2,
        scratch_shapes=[pltpu.VMEM((flat, columns), jnp.float32)] * 2 + [pltpu.SemaphoreType.DMA((2, PIECES))],
        compiler_params=pltpu.CompilerParams(vmem_limit_bytes=8 << 20),
        name="combine_kernel",
    )(*operands)
    return answer.reshape(levels, rows, columns), left.reshape(levels, rows, columns)


def solution(mesh):
    def run(noise, kappa2, conduct, land):
        count = mesh.shape["lon"]
        matrices = circle_matrices(count, noise.shape[2] // count)
        return jax.shard_map(
            functools.partial(body, *matrices),
            mesh=mesh,
            in_specs=(
                P("ens", "lat", "lon"),
                P(None, "lat", "lon"),
                P(None, None, "lat", "lon"),
                P(None, "lat", "lon"),
            ),
            out_specs=(P("ens", "lat", "lon"), P("ens", "lat", "lon")),
            check_vma=False,
        )(noise, kappa2, conduct, land)

    return run
```

```python
import functools
import math

import jax
import jax.numpy as jnp
import numpy as np
from jax import lax
from jax.experimental import pallas as pl
from jax.experimental.pallas import tpu as pltpu
from jax.sharding import PartitionSpec as P

base_kappa = 0.001
base_conduct = 1.0

SCALE = 2.0**-31
REACH = 4
TILE = 8
EDGE = 8

HIGHEST = lax.Precision.HIGHEST


def dot(a, b):
    return jnp.dot(a, b, precision=HIGHEST, preferred_element_type=jnp.float32)


def circle_kernel(total):
    middle = 2.0 + base_kappa / base_conduct
    rho = (middle - math.sqrt(middle * middle - 4.0)) / 2.0
    height = 1.0 / (1.0 / rho - rho) / base_conduct
    wrap = rho**total
    shift = (1.0 + rho * rho) / (1.0 - rho * rho) + total * wrap / (1.0 - wrap)
    front = height * height / (1.0 - wrap)
    return rho, front, shift


def circle_matrices(count, columns):
    total = count * columns
    rho, front, shift = circle_kernel(total)

    def one_side(n):
        return front * rho**n * (n + shift)

    def both_sides(n):
        return one_side(n) + one_side(total - n)

    place = np.arange(columns)
    rows = columns + 2 * EDGE
    x = np.arange(rows) - EDGE
    used = (x >= -2) & (x < columns + 2)
    near = both_sides(np.abs(x[:, None] - place[None, :])) * used[:, None]
    back = columns - 1 - place
    moments = np.zeros((8, columns))
    moments[0] = rho**place
    moments[1] = place * rho**place
    moments[2] = rho**back
    moments[3] = back * rho**back

    def block(start, size, neighbour):
        start = start % count * columns
        a = start - x
        b = total - start + x - (size * columns - 1)
        out = np.zeros((rows, 8))
        out[:, 0] = front * rho**a * (a + shift)
        out[:, 1] = front * rho**a
        out[:, 2] = front * rho**b * (b + shift)
        out[:, 3] = front * rho**b
        amend = both_sides(1) - both_sides(-1)
        if neighbour == "east":
            out[EDGE + columns + 1, 4] = amend
        if neighbour == "west":
            out[EDGE - 2, 4] = amend
        return out * used[:, None]

    fours = range(4, count, 4)
    even = [block(1, 1, "east"), block(-2, 2, "west")] + [block(-2 - d, 4, "") for d in fours]
    odd = [block(-1, 1, "west"), block(1, 2, "east")] + [block(-1 - d, 4, "") for d in fours]
    far = np.stack([np.concatenate(even, axis=1), np.concatenate(odd, axis=1)])
    far = np.pad(far, ((0, 0), (0, 0), (0, -far.shape[2] % 16))).astype(np.float32)
    high, middle, low = thirds(far, lambda x: x.astype(np.float32))
    far = np.concatenate([high, high, middle, high, middle, low], axis=2)
    columns_of = np.broadcast_to(moments[:4, :, None], (4, columns, 128))
    as_f32 = lambda m: np.asarray(m, np.float32)
    return as_f32(near), far, as_f32(moments), as_f32(columns_of)


def lon_perms(count):
    first = [(i, i ^ 1) for i in range(count)]
    return first, [(i, (i - 1 + 2 * (i % 2)) % count) for i in range(count)]


def lat_perms(count, bands):
    first, second = [], []
    for i in range(count):
        for j in range(bands):
            k = j - 1 + 2 * (j % 2)
            first.append((i * bands + j, i * bands + (j ^ 1)))
            second.append((i * bands + j, i * bands + k if 0 <= k < bands else (i ^ 1) * bands + j))
    return first, second


def inner_band():
    return (lax.axis_index("lat") > 0) & (lax.axis_index("lat") < lax.axis_size("lat") - 1)


def lane_roll(x, by):
    count = x.shape[1] // 128
    skip, by = divmod(by % x.shape[1], 128)
    parts = [x[:, k * 128 : (k + 1) * 128] for k in range(count)]
    if by:
        turned = [pltpu.roll(p, by, 1) for p in parts]
        lane = lax.broadcasted_iota(jnp.int32, (1, 128), 1)
        parts = [jnp.where(lane < by, turned[k - 1], turned[k]) for k in range(count)]
    return jnp.concatenate([parts[(k - skip) % count] for k in range(count)], axis=1)


def thirds(x, cast):
    high = x.astype(jnp.bfloat16)
    rest = x - cast(high)
    middle = rest.astype(jnp.bfloat16)
    return high, middle, (rest - cast(middle)).astype(jnp.bfloat16)


def whole(n):
    return [pl.BlockSpec(memory_space=pltpu.VMEM)] * n


def call(kernel, outs, *args, scratch=()):
    args = [pltpu.with_memory_space_constraint(a, pltpu.VMEM) for a in args]
    return pl.pallas_call(
        kernel,
        out_shape=[pltpu.VMEM(s, jnp.float32) for s in outs],
        in_specs=whole(len(args)),
        out_specs=whole(len(outs)),
        scratch_shapes=[pltpu.VMEM(s, jnp.float32) for s in scratch],
        compiler_params=pltpu.CompilerParams(vmem_limit_bytes=24 << 20),
        name=getattr(kernel, "func", kernel).__name__,
    )(*args)


FULL, PART = REACH, REACH - 1
PLANES = 3 * FULL + 3 * PART


def band_kernel(rows, levels, *refs):
    sources, (second, first), copies, sems = refs[:8], refs[8:10], refs[10:18], refs[18]
    moves = [pltpu.make_async_copy(x, y, sems.at[k]) for k, (x, y) in enumerate(zip(sources, copies))]
    for move in moves:
        move.start()
    for move in moves:
        move.wait()
    noise, kappa2, conduct, land = copies[:4]
    odd = lax.axis_index("lat") % 2
    top = rows - REACH
    loads = (
        lambda at: noise[at, :],
        lambda at: land[at, :].astype(jnp.float32),
        lambda at: conduct[1, at, :],
        lambda at: kappa2[at, :],
        lambda at: conduct[0, at, :],
        lambda at: conduct[2, at, :],
    )
    for out, side in ((first, odd), (second, 1 - odd)):
        k = 0
        for kind, load in enumerate(loads):
            count = FULL if kind < 3 else PART
            start = (1 - side) * (rows - count)
            for j in range(count):
                out[k] = load(pl.ds(start + j, levels, stride=rows))
                k += 1


def turned(planes, rows_of_planes):
    blocks = [jnp.concatenate(planes[j : j + REACH], axis=0) for j in range(0, rows_of_planes, REACH)]
    return jnp.concatenate([b.T for b in blocks], axis=1)


def coefficients(levels, band, kappa, east, north, upper, ocean):
    columns, lanes = kappa.shape
    lane = lax.broadcasted_iota(jnp.int32, (1, lanes), 1)
    row = lax.broadcasted_iota(jnp.int32, (columns, 1), 0)
    upper = jnp.where(lane % levels == levels - 1, 0.0, upper)
    south = jnp.where(lane % band < levels, 0.0, lane_roll(north, levels))
    west = jnp.where(row == 0, 0.0, pltpu.roll(east, 1, 0))
    ocean_east = jnp.where(row == columns - 1, 1.0, pltpu.roll(ocean, columns - 1, 0))
    diagonal = ocean * (kappa + east + west + north + south + upper + lane_roll(upper, 1))
    return diagonal, east * ocean * ocean_east, upper * ocean * lane_roll(ocean, -1)


def own_kernel(
    rows, levels, columns,
    noise, kappa2, conduct, land, weights,
    field, statics, edge, to_first, to_second,
):
    last_band = lax.axis_index("lat") == lax.axis_size("lat") - 1
    lon_odd = lax.axis_index("lon") % 2
    lanes = rows * levels

    def own(load):
        return turned([load(pl.ds(j, levels, stride=rows)) for j in range(rows)], rows)

    r = own(lambda at: noise[at, :])
    field[...] = r
    ocean = own(lambda at: land[at, :].astype(jnp.float32))
    north = own(lambda at: conduct[1, at, :])
    kappa = own(lambda at: kappa2[at, :])
    east = own(lambda at: conduct[0, at, :])
    upper = own(lambda at: conduct[2, at, :])
    lane = lax.broadcasted_iota(jnp.int32, (1, lanes), 1)
    north = jnp.where(last_band & (lane >= lanes - levels), 0.0, north)
    diagonal, to_east, to_upper = coefficients(levels, lanes, kappa, east, north, upper, ocean)
    for k, x in enumerate((diagonal, to_east, north, to_upper, ocean)):
        statics[k] = x
    edge[0:1] = east[columns - 1 :]
    m = dot(weights[...], r)[:4]
    end = columns - 1
    blank = jnp.zeros((5, lanes), jnp.float32)
    for_east = [m, r[end:], diagonal[end:], to_east[end - 1 : end], east[end:], ocean[end:], north[end:], to_upper[end:], blank]
    for_west = [m, r[:1], diagonal[:1], to_east[:1], east[:1], ocean[:1], north[:1], to_upper[:1], blank]
    for_east = jnp.concatenate(for_east, axis=0)
    for_west = jnp.concatenate(for_west, axis=0)
    to_first[...] = jnp.where(lon_odd == 0, for_east, for_west)
    to_second[...] = jnp.where(lon_odd == 0, for_west, for_east)


def ghost_kernel(levels, columns, got_second, got_first, near, made, own, spread, ghosts, patches, edge):
    lat_odd = lax.axis_index("lat") % 2
    group = REACH * levels

    def ghost(kind, north):
        count = FULL if kind < 3 else PART
        k = kind * FULL if kind < 3 else 3 * FULL + (kind - 3) * PART
        a = got_first[pl.ds(k, count)].reshape(count * levels, columns)
        b = jnp.where(inner_band(), got_second[pl.ds(k, count)], 0.0).reshape(count * levels, columns)
        from_first = (lat_odd == 0) if north else (lat_odd == 1)
        planes = jnp.where(from_first, a, b)
        if count == REACH:
            return planes.T
        blank = jnp.zeros((group - count * levels, columns), jnp.float32)
        return jnp.concatenate([planes, blank] if north else [blank, planes], axis=0).T

    r, ocean, north, kappa, east, upper = (
        jnp.concatenate([ghost(kind, False), ghost(kind, True)], axis=1) for kind in range(6)
    )
    spread[...] = dot(near[...], r)
    diagonal, to_east, to_upper = coefficients(levels, group, kappa, east, north, upper, ocean)
    edge[0:1] = east[columns - 1 :]
    last = made.shape[2] - group
    low, high = slice(0, group), slice(group, 2 * group)
    lane = lax.broadcasted_iota(jnp.int32, (1, group), 1)
    first_one, last_one = lane < levels, lane >= group - levels
    up = lambda x: pltpu.roll(x, levels, 1)
    down = lambda x: pltpu.roll(x, group - levels, 1)
    own_low, own_high = pl.ds(0, group), pl.ds(last, group)
    ocean_low, ocean_high = made[4, :, own_low], made[4, :, own_high]
    north_high = own[3, :, own_high]
    north_high = jnp.where(last_one, north_high * down(ocean[:, high]), north_high)
    north_of = lambda x, o, above: x * o * jnp.where(last_one, down(above), down(o))
    ghost_low = north_of(north[:, low], ocean[:, low], ocean_low)
    ghost_high = north_of(north[:, high], ocean[:, high], ocean[:, high])
    patches[0] = own[0, :, own_low] + jnp.where(first_one, ocean_low * up(north[:, low]), 0.0)
    patches[1] = jnp.where(first_one, up(ghost_low), own[4, :, own_low])
    patches[2] = north_high
    row = lax.broadcasted_iota(jnp.int32, (columns, 1), 0)
    for part, n, below in ((low, ghost_low, ghost_low), (high, ghost_high, north_high)):
        d, e, u, o = (x[:, part] for x in (diagonal, to_east, to_upper, ocean))
        if part is high:
            d = d + jnp.where(first_one, o * up(made[2, :, own_high]), 0.0)
        w = jnp.where(row == 0, 0.0, pltpu.roll(e, 1, 0))
        for k, x in enumerate((d, e, w, n, jnp.where(first_one, up(below), up(n)), u, pltpu.roll(u, 1, 1), o)):
            ghosts[k, :, part] = x


def coefficient(statics, k, at):
    own, ghosts, patches = statics
    group = ghosts.shape[2] // 2
    tile = pl.ds(at, TILE)
    x = own[k, tile]
    parts = [x[:, j : j + group] for j in range(0, x.shape[1], group)]
    if k in (0, 4):
        parts[0] = patches[0 if k == 0 else 1, tile]
    if k == 3:
        parts[-1] = patches[2, tile]
    g = ghosts[k, tile]
    return jnp.concatenate([g[:, :group]] + parts + [g[:, group:]], axis=1)


def forward_kernel(group, *refs):
    lists, (second, first) = refs[:-2], refs[-2:]
    odd = lax.axis_index("lat") % 2
    k = 0
    for x in lists:
        count, lanes = x.shape
        low, high = x[:, 0:group], x[:, lanes - group :]
        first[pl.ds(k, count)] = jnp.where(odd == 0, high, low)
        second[pl.ds(k, count)] = jnp.where(odd == 0, low, high)
        k += count


def joint_moments(left, right, rho, width):
    c = rho**width
    return jnp.concatenate(
        [
            left[0:1] + c * right[0:1],
            left[1:2] + c * (right[1:2] + width * right[0:1]),
            right[2:3] + c * left[2:3],
            right[3:4] + c * (left[3:4] + width * left[2:3]),
        ],
        axis=0,
    )


def chip_kernel(rho, columns, own, got, out):
    even = lax.axis_index("lon") % 2 == 0
    mine, its = own[0:4], got[0:4]
    out[...] = own[...]
    out[0:4] = joint_moments(jnp.where(even, mine, its), jnp.where(even, its, mine), rho, columns)


def quad_kernel(rho, columns, mine, got, out):
    even = lax.axis_index("lon") % 2 == 0
    a, b = mine[0:4], got[0:4]
    m = joint_moments(jnp.where(even, b, a), jnp.where(even, a, b), rho, 2 * columns)
    out[...] = jnp.concatenate([m, jnp.zeros_like(m)], axis=0)


def near_kernel(levels, near, field, made, spread, statics):
    spread[...] = dot(near[...], field[...])
    columns = field.shape[0]
    lanes = field.shape[1]
    lane = lax.broadcasted_iota(jnp.int32, (1, lanes), 1)
    row = lax.broadcasted_iota(jnp.int32, (TILE, 1), 0)
    for at in range(0, columns, TILE):
        tile = pl.ds(at, TILE)
        d, e, n, u, o = (made[k, tile] for k in range(5))
        w = pltpu.roll(e, 1, 0)
        w = jnp.where(row == 0, carried, w) if at else w
        carried = e[TILE - 1 :]
        n = n * o * jnp.where(lane >= lanes - levels, 1.0, lane_roll(o, -levels))
        for k, x in enumerate((d, e, w, n, lane_roll(n, levels), u, lane_roll(u, 1), o)):
            statics[k, tile] = x


def told(far, lists):
    x = jnp.concatenate([t[0:8] for t in lists], axis=0)
    if x.shape[0] % 16:
        x = jnp.concatenate([x, jnp.zeros((8, x.shape[1]), jnp.float32)], axis=0)
    high, middle, low = thirds(x, lambda p: p.astype(jnp.float32))
    stacked = jnp.concatenate([high, middle, high, low, middle, high], axis=0)
    return jnp.dot(far[lax.axis_index("lon") % 2], stacked, preferred_element_type=jnp.float32)


def faces(v, n, s, u, low, levels):
    return n * lane_roll(v, -levels) + s * lane_roll(v, levels) + u * lane_roll(v, -1) + low * lane_roll(v, 1)


def apply_tile(levels, v, statics, ends, at):
    own = statics[0]
    if at == 0:
        faces_of = lambda k: ends[k, 0:TILE]
    elif at + TILE == own.shape[1]:
        faces_of = lambda k: ends[k, TILE : 2 * TILE]
    else:
        faces_of = lambda k: coefficient(statics, k, at)
    d, e, w, n, s, u, low = (faces_of(k) for k in range(7))
    i = at + EDGE
    here = v[pl.ds(i, TILE)]
    out = d * here - e * v[pl.ds(i + 1, TILE)] - w * v[pl.ds(i - 1, TILE)]
    return here, out - faces(here, n, s, u, low, levels)


def apply_rim(levels, columns, v, f, rim):
    end = EDGE + columns
    pick = lambda a, b: jnp.concatenate([v[a : a + 1], v[b : b + 1], jnp.zeros((6, v.shape[1]), jnp.float32)], axis=0)
    here = pick(EDGE - 1, end)
    g = rim[0] * here - rim[1] * pick(EDGE, end + 1) - rim[2] * pick(EDGE - 2, end - 1)
    g = g - faces(here, rim[3], rim[4], rim[5], rim[6], levels)
    f[EDGE - 1 : EDGE] = g[0:1]
    f[end : end + 1] = g[1:2]


def joined(own, ghost):
    group = ghost.shape[1] // 2
    return jnp.concatenate([ghost[:, :group], own, ghost[:, group:]], axis=1)


def completed(levels, group, diagonal, north, ocean):
    lanes = ocean.shape[1]
    lane = lax.broadcasted_iota(jnp.int32, (1, lanes), 1)
    first_of_band = ((lane >= group) & (lane < group + levels)) | ((lane >= lanes - group) & (lane < lanes - group + levels))
    diagonal = diagonal + jnp.where(first_of_band, ocean * lane_roll(north, levels), 0.0)
    return diagonal, north * ocean * lane_roll(ocean, -levels)


def first_kernel(
    rows, levels, columns, others,
    own_spread, own_edge, ghost_spread, own_part, ghost_part, patches, edge, far, weights, side_second, side_first, *rest,
):
    statics = own_part, ghost_part, patches
    received = rest[: 1 + others]
    v, image, ends, rim, to_first, to_second, f = rest[1 + others :]
    lat_odd = lax.axis_index("lat") % 2
    even = lax.axis_index("lon") % 2 == 0
    group = REACH * levels
    lanes = rows * levels + 2 * group
    lists, k = [], 0
    for x in received:
        count = x.shape[0]
        a = side_first[pl.ds(k, count)]
        b = jnp.where(inner_band(), side_second[pl.ds(k, count)], 0.0)
        lists.append(jnp.concatenate([jnp.where(lat_odd == 1, a, b), x[...], jnp.where(lat_odd == 1, b, a)], axis=1))
        k += count
    v[...] = joined(own_spread[...], ghost_spread[...]) + told(far, lists)

    one, two = lists[0], lists[1]
    east_list, west_list = jnp.where(even, one, two), jnp.where(even, two, one)
    end = columns - 1
    for k in range(7):
        ends[k, 0:TILE] = coefficient(statics, k, 0)
        ends[k, TILE : 2 * TILE] = coefficient(statics, k, columns - TILE)
    ocean = coefficient(statics, 7, 0)[0:1]
    face_west = west_list[7:8] * west_list[8:9] * ocean
    last_east = ends[1, 2 * TILE - 1 :] * east_list[8:9]
    ends[0, 0:1] = ends[0, 0:1] + ocean * west_list[7:8]
    ends[2, 0:1] = face_west
    ends[1, 2 * TILE - 1 : 2 * TILE] = last_east
    blank = jnp.zeros((6, lanes), jnp.float32)
    stack = lambda p, q: jnp.concatenate([p, q, blank], axis=0)
    last_face = joined(own_edge[0:1], edge[0:1])
    rim_diagonal, rim_north = completed(
        levels, group,
        stack(west_list[5:6], east_list[5:6] + east_list[8:9] * last_face),
        stack(west_list[9:10], east_list[9:10]),
        stack(west_list[8:9], east_list[8:9]),
    )
    rim_upper = stack(west_list[10:11], east_list[10:11])
    rim[0] = rim_diagonal
    rim[1] = stack(face_west, east_list[6:7])
    rim[2] = stack(west_list[6:7], last_east)
    rim[3] = rim_north
    rim[4] = lane_roll(rim_north, levels)
    rim[5] = rim_upper
    rim[6] = lane_roll(rim_upper, 1)

    for at in range(0, columns, TILE):
        f[pl.ds(EDGE + at, TILE)] = apply_tile(levels, v, statics, ends, at)[1]
    apply_rim(levels, columns, v, f, rim)
    m = [0.0] * 4
    for at in range(0, columns, TILE):
        tile = pl.ds(at, TILE)
        second = apply_tile(levels, f, statics, ends, at)[1]
        w = jnp.where(coefficient(statics, 7, at) > 0.5, second, v[pl.ds(EDGE + at, TILE)])
        image[tile] = w
        for k in range(4):
            spread = weights[k, tile]
            m[k] = m[k] + w * jnp.concatenate([spread] * (lanes // 128), axis=1)
    m = [jnp.sum(x, axis=0, keepdims=True) * SCALE for x in m]
    pad = jnp.zeros((3, lanes), jnp.float32)
    for_east = jnp.concatenate(m + [image[end:] * SCALE, pad], axis=0)
    for_west = jnp.concatenate(m + [image[:1] * SCALE, pad], axis=0)
    to_first[...] = jnp.where(even, for_east, for_west)
    to_second[...] = jnp.where(even, for_west, for_east)


def lane_sums(tiles):
    total = functools.reduce(lambda a, b: a + b, tiles)
    s = jnp.sum(total, axis=0, keepdims=True)
    return functools.reduce(lambda a, b: a + b, [s[:, k : k + 128] for k in range(0, s.shape[1], 128)])


def own_lanes(rows, levels):
    return slice(REACH * levels, (REACH + rows) * levels)


def between_kernel(rows, levels, columns, near, field, precond, image, spread, sums):
    own = own_lanes(rows, levels)
    spread[...] = dot(near[...], image[...] * SCALE)
    energy, curve = [], []
    for at in range(0, columns, TILE):
        tile = pl.ds(at, TILE)
        p = precond[pl.ds(EDGE + at, TILE), own]
        energy.append(field[tile] * p)
        curve.append(p * image[tile, own])
    sums[...] = jnp.concatenate([lane_sums(energy), lane_sums(curve), jnp.zeros((6, 128), jnp.float32)], axis=0)


def second_kernel(
    levels, columns, rows, others, spread, early, image, own_part, ghost_part, patches, ends, far, rim, *rest
):
    statics = own_part, ghost_part, patches
    received = rest[: 1 + others]
    v, f, sums = rest[1 + others :]
    v[...] = spread[...] + told(far, received)
    own = own_lanes(rows, levels)
    mixed, last = [], []
    for at in range(0, columns, TILE):
        tile = pl.ds(at, TILE)
        q, b = apply_tile(levels, v, statics, ends, at)
        f[pl.ds(EDGE + at, TILE)] = b
        q, b, ocean = q[:, own], b[:, own], own_part[7, tile]
        mixed.append(image[tile, own] * q)
        still = jnp.where(ocean > 0.5, b, q)
        last.append(still * still)
    apply_rim(levels, columns, v, f, rim)
    sums[...] = jnp.concatenate([early[0:2], lane_sums(mixed), lane_sums(last), early[4:8]], axis=0)


def turn_kernel(rows, levels, columns, precond, image, again, f, own_part, ghost_part, patches, ends, *outs):
    statics = own_part, ghost_part, patches
    z = outs[4]
    own = own_lanes(rows, levels)
    for at in range(0, columns, TILE):
        second = apply_tile(levels, f, statics, ends, at)[1]
        tile = pl.ds(at, TILE)
        z[tile] = jnp.where(coefficient(statics, 7, at) > 0.5, second, again[pl.ds(EDGE + at, TILE)])
    group = REACH * levels
    slab = pl.ds(EDGE, columns)
    for j in range(0, rows, REACH):
        at = slice(own.start + j * levels, own.start + j * levels + group)
        for out, x in zip(outs, (precond[slab, at], image[:, at], again[slab, at], z[:, at])):
            t = x.T
            for i in range(REACH):
                out[pl.ds(j + i, levels, stride=rows), :] = t[i * levels : (i + 1) * levels]


PIECES = 4


def combine_kernel(sums, noise, precond, image, again, along, answer, left, x, y, sems):
    total = jnp.sum(sums[...], axis=1, keepdims=True)
    energy, curve, mixed, last = total[0:1], total[1:2], total[2:3], total[3:4]
    alpha = energy / curve
    beta = alpha / SCALE
    growth = alpha * beta * mixed / energy
    step = energy * (growth - 1.0) / (beta * beta * last - growth * growth * curve)
    keep = alpha + step * growth
    back = step * beta
    size = noise.shape[0] // PIECES
    moves = []
    for k in range(PIECES):
        part = pl.ds(k * size, size)
        x[part] = keep * precond[part] - back * again[part]
        moves.append(pltpu.make_async_copy(x.at[part], answer.at[part], sems.at[0, k]))
        moves[-1].start()
        y[part] = noise[part] - (keep * image[part] - back * along[part])
        moves.append(pltpu.make_async_copy(y.at[part], left.at[part], sems.at[1, k]))
        moves[-1].start()
    for move in moves:
        move.wait()


def doubling(count):
    steps = []
    while 2 ** len(steps) < count:
        steps.append(2 ** len(steps))
    return steps


def summed(x):
    count, bands = lax.axis_size("lon"), lax.axis_size("lat")
    x = x + lax.ppermute(x, "lon", [(i, i ^ 1) for i in range(count)])
    for step in doubling(count)[1:]:
        x = x + lax.ppermute(x, "lon", [(i, i ^ step ^ 1) for i in range(count)])
    for step in doubling(bands):
        pairs = [(i * bands + j, (i ^ 1) * bands + (j ^ step)) for i in range(count) for j in range(bands)]
        x = x + lax.ppermute(x, ("lon", "lat"), pairs)
    return x


def body(near, far, weights, columns_of, noise, kappa2, conduct, land):
    levels, rows, columns = noise.shape
    count = lax.axis_size("lon")
    others = count // 4
    flat = levels * rows
    group = REACH * levels
    lanes = flat + 2 * group
    tall = columns + 2 * EDGE
    rho = circle_kernel(count * columns)[0]
    noise = noise.reshape(flat, columns)
    kappa2 = kappa2.reshape(flat, columns)
    land = land.reshape(flat, columns)
    conduct = conduct.reshape(3, flat, columns)

    sources = (noise, kappa2, conduct, land, near, far, weights, columns_of)
    planes = (PLANES, levels, columns)
    second, first, noise, kappa2, conduct, land, near, far, weights, columns_of = pl.pallas_call(
        functools.partial(band_kernel, rows, levels),
        out_shape=[pltpu.VMEM(planes, jnp.float32)] * 2 + [pltpu.VMEM(x.shape, x.dtype) for x in sources],
        in_specs=[pl.BlockSpec(memory_space=pltpu.HBM)] * len(sources),
        out_specs=whole(2 + len(sources)),
        scratch_shapes=[pltpu.SemaphoreType.DMA((len(sources),))],
        compiler_params=pltpu.CompilerParams(vmem_limit_bytes=8 << 20),
        name="band_kernel",
    )(*[pltpu.with_memory_space_constraint(x, pltpu.HBM) for x in sources])
    lat_a, lat_b = lat_perms(count, lax.axis_size("lat"))
    to_band = lambda x, pairs: lax.ppermute(x, ("lon", "lat"), pairs)
    got_second, got_first = to_band(second, lat_b), to_band(first, lat_a)

    own_field, made, own_edge, to_first, to_second = call(
        functools.partial(own_kernel, rows, levels, columns),
        [(columns, flat), (5, columns, flat), (8, flat), (16, flat), (16, flat)],
        noise, kappa2, conduct, land, weights,
    )
    lon_a, lon_b = lon_perms(count)

    def exchange(one, two):
        wide = two.shape[1]
        got_one = lax.ppermute(one, "lon", lon_a)
        (two,) = call(functools.partial(chip_kernel, rho, columns), [two.shape], two, got_one)
        got_two = lax.ppermute(two, "lon", lon_b)
        if count == 4:
            return [got_one, got_two]
        (four,) = call(functools.partial(quad_kernel, rho, columns), [(8, wide)], two, got_two)
        return [got_one, got_two] + [
            lax.ppermute(four, "lon", [(i, (i + d) % count) for i in range(count)]) for d in range(4, count, 4)
        ]

    lists = exchange(to_first, to_second)
    own_spread, own_part = call(
        functools.partial(near_kernel, levels), [(tall, flat), (8, columns, flat)], near, own_field, made
    )
    heights = sum(x.shape[0] for x in lists)
    side_second, side_first = call(functools.partial(forward_kernel, group), [(heights, group)] * 2, *lists)
    side_second, side_first = to_band(side_second, lat_b), to_band(side_first, lat_a)
    ghost_spread, ghost_part, patches, edge = call(
        functools.partial(ghost_kernel, levels, columns),
        [(tall, 2 * group), (8, columns, 2 * group), (3, columns, group), (8, 2 * group)],
        got_second, got_first, near, made, own_part,
    )
    precond, image, ends, rim, to_first, to_second = call(
        functools.partial(first_kernel, rows, levels, columns, others),
        [(tall, lanes), (columns, lanes), (7, 2 * TILE, lanes), (7, 8, lanes), (8, lanes), (8, lanes)],
        own_spread, own_edge, ghost_spread, own_part, ghost_part, patches, edge, far, columns_of, side_second, side_first, *lists,
        scratch=[(tall, lanes)],
    )
    lists = exchange(to_first, to_second)
    spread, sums = call(
        functools.partial(between_kernel, rows, levels, columns),
        [(tall, lanes), (8, 128)],
        near, own_field, precond, image,
    )
    again, half, sums = call(
        functools.partial(second_kernel, levels, columns, rows, others),
        [(tall, lanes), (tall, lanes), (8, 128)],
        spread, sums, image, own_part, ghost_part, patches, ends, far, rim, *lists,
    )
    sums = summed(sums)
    turned_back = call(
        functools.partial(turn_kernel, rows, levels, columns),
        [(flat, columns)] * 4 + [(columns, lanes)],
        precond, image, again, half, own_part, ghost_part, patches, ends,
    )[:4]
    operands = [pltpu.with_memory_space_constraint(x, pltpu.VMEM) for x in (sums, noise, *turned_back)]
    answer, left = pl.pallas_call(
        combine_kernel,
        out_shape=[jax.ShapeDtypeStruct((flat, columns), jnp.float32)] * 2,
        in_specs=whole(len(operands)),
        out_specs=[pl.BlockSpec(memory_space=pltpu.HBM)] * 2,
        scratch_shapes=[pltpu.VMEM((flat, columns), jnp.float32)] * 2 + [pltpu.SemaphoreType.DMA((2, PIECES))],
        compiler_params=pltpu.CompilerParams(vmem_limit_bytes=8 << 20),
        name="combine_kernel",
    )(*operands)
    return answer.reshape(levels, rows, columns), left.reshape(levels, rows, columns)


def solution(mesh):
    def run(noise, kappa2, conduct, land):
        count = mesh.shape["lon"]
        matrices = circle_matrices(count, noise.shape[2] // count)
        return jax.shard_map(
            functools.partial(body, *matrices),
            mesh=mesh,
            in_specs=(
                P("ens", "lat", "lon"),
                P(None, "lat", "lon"),
                P(None, None, "lat", "lon"),
                P(None, "lat", "lon"),
            ),
            out_specs=(P("ens", "lat", "lon"), P("ens", "lat", "lon")),
            check_vma=False,
        )(noise, kappa2, conduct, land)

    return run
```

```python
import functools
import math

import jax
import jax.numpy as jnp
import numpy as np
from jax import lax
from jax.experimental import pallas as pl
from jax.experimental.pallas import tpu as pltpu
from jax.sharding import PartitionSpec as P

base_kappa = 0.001
base_conduct = 1.0

SCALE = 2.0**-31
REACH = 4
TILE = 8
EDGE = 8

HIGHEST = lax.Precision.HIGHEST


def dot(a, b):
    return jnp.dot(a, b, precision=HIGHEST, preferred_element_type=jnp.float32)


def circle_kernel(total):
    middle = 2.0 + base_kappa / base_conduct
    rho = (middle - math.sqrt(middle * middle - 4.0)) / 2.0
    height = 1.0 / (1.0 / rho - rho) / base_conduct
    wrap = rho**total
    shift = (1.0 + rho * rho) / (1.0 - rho * rho) + total * wrap / (1.0 - wrap)
    front = height * height / (1.0 - wrap)
    return rho, front, shift


def circle_matrices(count, columns):
    total = count * columns
    rho, front, shift = circle_kernel(total)

    def one_side(n):
        return front * rho**n * (n + shift)

    def both_sides(n):
        return one_side(n) + one_side(total - n)

    place = np.arange(columns)
    rows = columns + 2 * EDGE
    x = np.arange(rows) - EDGE
    used = (x >= -2) & (x < columns + 2)
    near = both_sides(np.abs(x[:, None] - place[None, :])) * used[:, None]
    back = columns - 1 - place
    moments = np.zeros((8, columns))
    moments[0] = rho**place
    moments[1] = place * rho**place
    moments[2] = rho**back
    moments[3] = back * rho**back

    def block(start, size, neighbour):
        start = start % count * columns
        a = start - x
        b = total - start + x - (size * columns - 1)
        out = np.zeros((rows, 8))
        out[:, 0] = front * rho**a * (a + shift)
        out[:, 1] = front * rho**a
        out[:, 2] = front * rho**b * (b + shift)
        out[:, 3] = front * rho**b
        amend = both_sides(1) - both_sides(-1)
        if neighbour == "east":
            out[EDGE + columns + 1, 4] = amend
        if neighbour == "west":
            out[EDGE - 2, 4] = amend
        return out * used[:, None]

    fours = range(4, count, 4)
    even = [block(1, 1, "east"), block(-2, 2, "west")] + [block(-2 - d, 4, "") for d in fours]
    odd = [block(-1, 1, "west"), block(1, 2, "east")] + [block(-1 - d, 4, "") for d in fours]
    far = np.stack([np.concatenate(even, axis=1), np.concatenate(odd, axis=1)])
    far = np.pad(far, ((0, 0), (0, 0), (0, -far.shape[2] % 16))).astype(np.float32)
    high, middle, low = thirds(far, lambda x: x.astype(np.float32))
    far = np.concatenate([high, high, middle, high, middle, low], axis=2)
    columns_of = np.broadcast_to(moments[:4, :, None], (4, columns, 128))
    as_f32 = lambda m: np.asarray(m, np.float32)
    return as_f32(near), far, as_f32(moments), as_f32(columns_of)


def lon_perms(count):
    first = [(i, i ^ 1) for i in range(count)]
    return first, [(i, (i - 1 + 2 * (i % 2)) % count) for i in range(count)]


def lat_perms(count, bands):
    first, second = [], []
    for i in range(count):
        for j in range(bands):
            k = j - 1 + 2 * (j % 2)
            first.append((i * bands + j, i * bands + (j ^ 1)))
            second.append((i * bands + j, i * bands + k if 0 <= k < bands else (i ^ 1) * bands + j))
    return first, second


def inner_band():
    return (lax.axis_index("lat") > 0) & (lax.axis_index("lat") < lax.axis_size("lat") - 1)


def lane_roll(x, by):
    count = x.shape[1] // 128
    skip, by = divmod(by % x.shape[1], 128)
    parts = [x[:, k * 128 : (k + 1) * 128] for k in range(count)]
    if by:
        turned = [pltpu.roll(p, by, 1) for p in parts]
        lane = lax.broadcasted_iota(jnp.int32, (1, 128), 1)
        parts = [jnp.where(lane < by, turned[k - 1], turned[k]) for k in range(count)]
    return jnp.concatenate([parts[(k - skip) % count] for k in range(count)], axis=1)


def thirds(x, cast):
    high = x.astype(jnp.bfloat16)
    rest = x - cast(high)
    middle = rest.astype(jnp.bfloat16)
    return high, middle, (rest - cast(middle)).astype(jnp.bfloat16)


def whole(n):
    return [pl.BlockSpec(memory_space=pltpu.VMEM)] * n


def call(kernel, outs, *args, scratch=()):
    args = [pltpu.with_memory_space_constraint(a, pltpu.VMEM) for a in args]
    return pl.pallas_call(
        kernel,
        out_shape=[pltpu.VMEM(s, jnp.float32) for s in outs],
        in_specs=whole(len(args)),
        out_specs=whole(len(outs)),
        scratch_shapes=[pltpu.VMEM(s, jnp.float32) for s in scratch],
        compiler_params=pltpu.CompilerParams(vmem_limit_bytes=24 << 20),
        name=getattr(kernel, "func", kernel).__name__,
    )(*args)


FULL, PART = REACH, REACH - 1
PLANES = 2 * FULL + 3 * PART


def band_kernel(rows, levels, *refs):
    sources, (second, first), copies, sems = refs[:8], refs[8:10], refs[10:18], refs[18]
    order = (0, 3, 2, 1, 4, 5, 6, 7)
    moves = [pltpu.make_async_copy(sources[k], copies[k], sems.at[k]) for k in order]
    for move in moves:
        move.start()
    noise, kappa2, conduct, land = copies[:4]
    odd = lax.axis_index("lat") % 2
    sides = ((first, odd), (second, 1 - odd))
    plane = lambda lat: pl.ds(lat, levels, stride=rows)
    moves[0].wait()
    for out, side in sides:
        for j in range(FULL):
            out[j] = noise[plane((1 - side) * (rows - FULL) + j), :]
    for move in moves[1:4]:
        move.wait()
    columns = noise.shape[1]
    lane = lax.broadcasted_iota(jnp.int32, (1, columns), 1)
    level = lax.broadcasted_iota(jnp.int32, (levels, 1), 0)
    for out, side in sides:
        base = (1 - side) * (rows - FULL)
        ocean = [land[plane(base + j), :].astype(jnp.float32) for j in range(FULL)]
        north = [conduct[1, plane(base + j), :] for j in range(FULL)]
        for j in range(PART):
            out[FULL + 3 * PART + j] = north[j] * ocean[j] * ocean[j + 1]
        out[FULL + 4 * PART] = north[PART]
        near = lambda x, j: jnp.where(side == 0, x[j + 1], x[j])
        for j in range(PART):
            at = plane(base + 1 - side + j)
            o, n = near(ocean, j), near(north, j)
            below = north[j] if j == 0 else jnp.where(side == 0, north[j], north[j - 1])
            south = jnp.where(side == 0, below, 0.0) if j == 0 else below
            e, k = conduct[0, at, :], kappa2[at, :]
            u = jnp.where(level == levels - 1, 0.0, conduct[2, at, :])
            west = jnp.where(lane == 0, 0.0, pltpu.roll(e, 1, 1))
            ocean_east = jnp.where(lane == columns - 1, 1.0, pltpu.roll(o, columns - 1, 1))
            out[FULL + j] = o * (k + e + west + n + south + u + pltpu.roll(u, 1, 0))
            out[FULL + PART + j] = e * o * ocean_east
            out[FULL + 2 * PART + j] = u * o * pltpu.roll(o, levels - 1, 0)
    for move in moves[4:]:
        move.wait()


def turned(planes, rows_of_planes):
    blocks = [jnp.concatenate(planes[j : j + REACH], axis=0) for j in range(0, rows_of_planes, REACH)]
    return jnp.concatenate([b.T for b in blocks], axis=1)


def coefficients(levels, band, kappa, east, north, upper, ocean):
    columns, lanes = kappa.shape
    lane = lax.broadcasted_iota(jnp.int32, (1, lanes), 1)
    row = lax.broadcasted_iota(jnp.int32, (columns, 1), 0)
    upper = jnp.where(lane % levels == levels - 1, 0.0, upper)
    south = jnp.where(lane % band < levels, 0.0, lane_roll(north, levels))
    west = jnp.where(row == 0, 0.0, pltpu.roll(east, 1, 0))
    ocean_east = jnp.where(row == columns - 1, 1.0, pltpu.roll(ocean, columns - 1, 0))
    diagonal = ocean * (kappa + east + west + north + south + upper + lane_roll(upper, 1))
    return diagonal, east * ocean * ocean_east, upper * ocean * lane_roll(ocean, -1)


def field_kernel(rows, levels, noise, weights, field, sums):
    r = turned([noise[pl.ds(j, levels, stride=rows), :] for j in range(rows)], rows)
    field[...] = r
    sums[...] = dot(weights[...], r)


def own_kernel(
    rows, levels, columns,
    kappa2, conduct, land, field,
    statics, edge, to_first, to_second,
):
    last_band = lax.axis_index("lat") == lax.axis_size("lat") - 1
    lon_odd = lax.axis_index("lon") % 2
    lanes = rows * levels

    def own(load):
        return turned([load(pl.ds(j, levels, stride=rows)) for j in range(rows)], rows)

    ocean = own(lambda at: land[at, :].astype(jnp.float32))
    north = own(lambda at: conduct[1, at, :])
    kappa = own(lambda at: kappa2[at, :])
    east = own(lambda at: conduct[0, at, :])
    upper = own(lambda at: conduct[2, at, :])
    lane = lax.broadcasted_iota(jnp.int32, (1, lanes), 1)
    north = jnp.where(last_band & (lane >= lanes - levels), 0.0, north)
    diagonal, to_east, to_upper = coefficients(levels, lanes, kappa, east, north, upper, ocean)
    for k, x in enumerate((diagonal, to_east, north, to_upper, ocean)):
        statics[k] = x
    end = columns - 1
    edge[...] = jnp.concatenate([east[end:], jnp.zeros((7, lanes), jnp.float32)], axis=0)
    blank = jnp.zeros((1, lanes), jnp.float32)
    for_east = [field[end:], diagonal[end:], to_east[end - 1 : end], east[end:], ocean[end:], north[end:], to_upper[end:], blank]
    for_west = [field[:1], diagonal[:1], to_east[:1], east[:1], ocean[:1], north[:1], to_upper[:1], blank]
    for_east = jnp.concatenate(for_east, axis=0)
    for_west = jnp.concatenate(for_west, axis=0)
    to_first[...] = jnp.where(lon_odd == 0, for_east, for_west)
    to_second[...] = jnp.where(lon_odd == 0, for_west, for_east)


MOMENTS, LIST = 4, 11


def list_kernel(moments, edges, out):
    out[...] = jnp.concatenate([moments[0:MOMENTS], edges[...], jnp.zeros((4, edges.shape[1]), jnp.float32)], axis=0)


def ghost_kernel(levels, columns, got_second, got_first, near, made, own, spread, ghosts, patches):
    lat_odd = lax.axis_index("lat") % 2
    group = REACH * levels

    def ghost(k, count, north):
        a = got_first[pl.ds(k, count)].reshape(count * levels, columns)
        b = jnp.where(inner_band(), got_second[pl.ds(k, count)], 0.0).reshape(count * levels, columns)
        from_first = (lat_odd == 0) if north else (lat_odd == 1)
        planes = jnp.where(from_first, a, b)
        if count == REACH:
            return planes.T
        blank = jnp.zeros((group - count * levels, columns), jnp.float32)
        return jnp.concatenate([planes, blank] if north else [blank, planes], axis=0).T

    pieces = ((0, FULL), (FULL, PART), (FULL + PART, PART), (FULL + 2 * PART, PART), (FULL + 3 * PART, FULL))
    r, diagonal, to_east, to_upper, north = (
        jnp.concatenate([ghost(k, count, False), ghost(k, count, True)], axis=1) for k, count in pieces
    )
    spread[...] = dot(near[...], r)
    ocean = jnp.where(diagonal > 0.0, 1.0, 0.0)
    last = made.shape[2] - group
    low, high = slice(0, group), slice(group, 2 * group)
    lane = lax.broadcasted_iota(jnp.int32, (1, group), 1)
    first_one, last_one = lane < levels, lane >= group - levels
    up = lambda x: pltpu.roll(x, levels, 1)
    down = lambda x: pltpu.roll(x, group - levels, 1)
    own_low, own_high = pl.ds(0, group), pl.ds(last, group)
    ocean_low, ocean_high = made[4, :, own_low], made[4, :, own_high]
    north_high = own[3, :, own_high]
    north_high = jnp.where(last_one, north_high * down(ocean[:, high]), north_high)
    ghost_low = north[:, low]
    ghost_low = jnp.where(last_one, ghost_low * ocean[:, low] * down(ocean_low), ghost_low)
    ghost_high = north[:, high]
    patches[0] = own[0, :, own_low] + jnp.where(first_one, ocean_low * up(north[:, low]), 0.0)
    patches[1] = jnp.where(first_one, up(ghost_low), own[4, :, own_low])
    patches[2] = north_high
    row = lax.broadcasted_iota(jnp.int32, (columns, 1), 0)
    for part, n, below in ((low, ghost_low, ghost_low), (high, ghost_high, north_high)):
        d, e, u, o = (x[:, part] for x in (diagonal, to_east, to_upper, ocean))
        if part is high:
            d = d + jnp.where(first_one, o * up(made[2, :, own_high]), 0.0)
        w = jnp.where(row == 0, 0.0, pltpu.roll(e, 1, 0))
        for k, x in enumerate((d, e, w, n, jnp.where(first_one, up(below), up(n)), u, pltpu.roll(u, 1, 1), o)):
            ghosts[k, :, part] = x


def coefficient(statics, k, at):
    own, ghosts, patches = statics
    group = ghosts.shape[2] // 2
    tile = pl.ds(at, TILE)
    x = own[k, tile]
    parts = [x[:, j : j + group] for j in range(0, x.shape[1], group)]
    if k in (0, 4):
        parts[0] = patches[0 if k == 0 else 1, tile]
    if k == 3:
        parts[-1] = patches[2, tile]
    g = ghosts[k, tile]
    return jnp.concatenate([g[:, :group]] + parts + [g[:, group:]], axis=1)


def forward_kernel(group, *refs):
    (one, two, edge), more, (second, first) = refs[:3], refs[3:-2], refs[-2:]
    odd = lax.axis_index("lat") % 2
    whole_rows = [one[0:LIST], two[0:LIST], edge[0:2]] + [x[...] for x in more]
    x = jnp.concatenate(whole_rows, axis=0)
    low, high = x[:, 0:group], x[:, x.shape[1] - group :]
    first[...] = jnp.where(odd == 0, high, low)
    second[...] = jnp.where(odd == 0, low, high)


def joint_moments(left, right, rho, width):
    c = rho**width
    return jnp.concatenate(
        [
            left[0:1] + c * right[0:1],
            left[1:2] + c * (right[1:2] + width * right[0:1]),
            right[2:3] + c * left[2:3],
            right[3:4] + c * (left[3:4] + width * left[2:3]),
        ],
        axis=0,
    )


def chip_kernel(rho, columns, own, edges, got, out):
    even = lax.axis_index("lon") % 2 == 0
    mine, its = own[0:MOMENTS], got[0:MOMENTS]
    m = joint_moments(jnp.where(even, mine, its), jnp.where(even, its, mine), rho, columns)
    blank = jnp.zeros((out.shape[0] - MOMENTS - edges.shape[0], m.shape[1]), jnp.float32)
    out[...] = jnp.concatenate([m, edges[...], blank], axis=0)


def again_kernel(rho, columns, own, got, out):
    even = lax.axis_index("lon") % 2 == 0
    mine, its = own[0:MOMENTS], got[0:MOMENTS]
    out[...] = own[...]
    out[0:MOMENTS] = joint_moments(jnp.where(even, mine, its), jnp.where(even, its, mine), rho, columns)


def quad_kernel(rho, columns, mine, got, out):
    even = lax.axis_index("lon") % 2 == 0
    a, b = mine[0:4], got[0:4]
    m = joint_moments(jnp.where(even, b, a), jnp.where(even, a, b), rho, 2 * columns)
    out[...] = jnp.concatenate([m, jnp.zeros_like(m)], axis=0)


def near_kernel(levels, near, field, made, spread, statics):
    spread[...] = dot(near[...], field[...])
    columns = field.shape[0]
    lanes = field.shape[1]
    lane = lax.broadcasted_iota(jnp.int32, (1, lanes), 1)
    row = lax.broadcasted_iota(jnp.int32, (TILE, 1), 0)
    for at in range(0, columns, TILE):
        tile = pl.ds(at, TILE)
        d, e, n, u, o = (made[k, tile] for k in range(5))
        w = pltpu.roll(e, 1, 0)
        w = jnp.where(row == 0, carried, w) if at else w
        carried = e[TILE - 1 :]
        n = n * o * jnp.where(lane >= lanes - levels, 1.0, lane_roll(o, -levels))
        for k, x in enumerate((d, e, w, n, lane_roll(n, levels), u, lane_roll(u, 1), o)):
            statics[k, tile] = x


def told(far, lists):
    x = jnp.concatenate([t[0:8] for t in lists], axis=0)
    if x.shape[0] % 16:
        x = jnp.concatenate([x, jnp.zeros((8, x.shape[1]), jnp.float32)], axis=0)
    high, middle, low = thirds(x, lambda p: p.astype(jnp.float32))
    stacked = jnp.concatenate([high, middle, high, low, middle, high], axis=0)
    return jnp.dot(far[lax.axis_index("lon") % 2], stacked, preferred_element_type=jnp.float32)


def faces(v, n, s, u, low, levels):
    return n * lane_roll(v, -levels) + s * lane_roll(v, levels) + u * lane_roll(v, -1) + low * lane_roll(v, 1)


def shifts(v, at, kept):
    def turned_rows(i):
        if i not in kept:
            x = v[pl.ds(i, TILE)]
            kept[i] = x, pltpu.roll(x, TILE - 1, 0), pltpu.roll(x, 1, 0)
        return kept[i]

    i = at + EDGE
    row = lax.broadcasted_iota(jnp.int32, (TILE, 1), 0)
    x, east_v, west_v = turned_rows(i)
    east_v = jnp.where(row == TILE - 1, turned_rows(i + TILE)[1], east_v)
    west_v = jnp.where(row == 0, turned_rows(i - TILE)[2], west_v)
    return x, east_v, west_v


def apply_tile(levels, v, statics, ends, at, kept):
    own = statics[0]
    if at == 0:
        faces_of = lambda k: ends[k, 0:TILE]
    elif at + TILE == own.shape[1]:
        faces_of = lambda k: ends[k, TILE : 2 * TILE]
    else:
        faces_of = lambda k: coefficient(statics, k, at)
    d, e, w, n, s, u, low = (faces_of(k) for k in range(7))
    here, east_v, west_v = shifts(v, at, kept)
    return here, d * here - e * east_v - w * west_v - faces(here, n, s, u, low, levels)


def apply_rim(levels, columns, v, f, rim):
    end = EDGE + columns
    pick = lambda a, b: jnp.concatenate([v[a : a + 1], v[b : b + 1], jnp.zeros((6, v.shape[1]), jnp.float32)], axis=0)
    here = pick(EDGE - 1, end)
    g = rim[0] * here - rim[1] * pick(EDGE, end + 1) - rim[2] * pick(EDGE - 2, end - 1)
    g = g - faces(here, rim[3], rim[4], rim[5], rim[6], levels)
    f[EDGE - 1 : EDGE] = g[0:1]
    f[end : end + 1] = g[1:2]


def joined(own, ghost):
    group = ghost.shape[1] // 2
    return jnp.concatenate([ghost[:, :group], own, ghost[:, group:]], axis=1)


def completed(levels, group, diagonal, north, ocean):
    lanes = ocean.shape[1]
    lane = lax.broadcasted_iota(jnp.int32, (1, lanes), 1)
    first_of_band = ((lane >= group) & (lane < group + levels)) | ((lane >= lanes - group) & (lane < lanes - group + levels))
    diagonal = diagonal + jnp.where(first_of_band, ocean * lane_roll(north, levels), 0.0)
    return diagonal, north * ocean * lane_roll(ocean, -levels)


def first_kernel(
    rows, levels, columns, others,
    own_spread, own_edge, ghost_spread, own_part, ghost_part, patches, far, weights, side_second, side_first, *rest,
):
    statics = own_part, ghost_part, patches
    received = rest[: 1 + others]
    v, image, ends, rim, to_first, to_second, f = rest[1 + others :]
    lat_odd = lax.axis_index("lat") % 2
    even = lax.axis_index("lon") % 2 == 0
    group = REACH * levels
    lanes = rows * levels + 2 * group
    a, b = side_first[...], jnp.where(inner_band(), side_second[...], 0.0)
    south, north = jnp.where(lat_odd == 1, a, b), jnp.where(lat_odd == 1, b, a)
    lists, k = [], 0
    for x in (received[0][0:LIST], received[1][0:LIST], own_edge[0:2], *[x[...] for x in received[2:]]):
        at = slice(k, k + x.shape[0])
        lists.append(jnp.concatenate([south[at], x, north[at]], axis=1))
        k += x.shape[0]
    last_face = lists.pop(2)[0:1]
    v[...] = joined(own_spread[...], ghost_spread[...]) + told(far, lists)

    one, two = lists[0], lists[1]
    east_list, west_list = jnp.where(even, one, two), jnp.where(even, two, one)
    end = columns - 1
    for k in range(7):
        ends[k, 0:TILE] = coefficient(statics, k, 0)
        ends[k, TILE : 2 * TILE] = coefficient(statics, k, columns - TILE)
    ocean = coefficient(statics, 7, 0)[0:1]
    face_west = west_list[7:8] * west_list[8:9] * ocean
    last_east = ends[1, 2 * TILE - 1 :] * east_list[8:9]
    ends[0, 0:1] = ends[0, 0:1] + ocean * west_list[7:8]
    ends[2, 0:1] = face_west
    ends[1, 2 * TILE - 1 : 2 * TILE] = last_east
    blank = jnp.zeros((6, lanes), jnp.float32)
    stack = lambda p, q: jnp.concatenate([p, q, blank], axis=0)
    rim_diagonal, rim_north = completed(
        levels, group,
        stack(west_list[5:6], east_list[5:6] + east_list[8:9] * last_face),
        stack(west_list[9:10], east_list[9:10]),
        stack(west_list[8:9], east_list[8:9]),
    )
    rim_upper = stack(west_list[10:11], east_list[10:11])
    rim[0] = rim_diagonal
    rim[1] = stack(face_west, east_list[6:7])
    rim[2] = stack(west_list[6:7], last_east)
    rim[3] = rim_north
    rim[4] = lane_roll(rim_north, levels)
    rim[5] = rim_upper
    rim[6] = lane_roll(rim_upper, 1)

    kept = {}
    for at in range(0, columns, TILE):
        f[pl.ds(EDGE + at, TILE)] = apply_tile(levels, v, statics, ends, at, kept)[1]
    apply_rim(levels, columns, v, f, rim)
    m, kept = [0.0] * 4, {}
    for at in range(0, columns, TILE):
        tile = pl.ds(at, TILE)
        second = apply_tile(levels, f, statics, ends, at, kept)[1]
        w = jnp.where(coefficient(statics, 7, at) > 0.5, second, v[pl.ds(EDGE + at, TILE)])
        image[tile] = w
        for k in range(4):
            spread = weights[k, tile]
            m[k] = m[k] + w * jnp.concatenate([spread] * (lanes // 128), axis=1)
    m = [jnp.sum(x, axis=0, keepdims=True) * SCALE for x in m]
    pad = jnp.zeros((3, lanes), jnp.float32)
    for_east = jnp.concatenate(m + [image[end:] * SCALE, pad], axis=0)
    for_west = jnp.concatenate(m + [image[:1] * SCALE, pad], axis=0)
    to_first[...] = jnp.where(even, for_east, for_west)
    to_second[...] = jnp.where(even, for_west, for_east)


def lane_sums(tiles):
    total = functools.reduce(lambda a, b: a + b, tiles)
    s = jnp.sum(total, axis=0, keepdims=True)
    return functools.reduce(lambda a, b: a + b, [s[:, k : k + 128] for k in range(0, s.shape[1], 128)])


def own_lanes(rows, levels):
    return slice(REACH * levels, (REACH + rows) * levels)


def between_kernel(rows, levels, columns, near, field, precond, image, spread, sums):
    own = own_lanes(rows, levels)
    spread[...] = dot(near[...], image[...] * SCALE)
    energy, curve = [], []
    for at in range(0, columns, TILE):
        tile = pl.ds(at, TILE)
        p = precond[pl.ds(EDGE + at, TILE), own]
        energy.append(field[tile] * p)
        curve.append(p * image[tile, own])
    sums[...] = jnp.concatenate([lane_sums(energy), lane_sums(curve), jnp.zeros((6, 128), jnp.float32)], axis=0)


def second_kernel(
    levels, columns, rows, others, spread, early, image, own_part, ghost_part, patches, ends, far, rim, *rest
):
    statics = own_part, ghost_part, patches
    received = rest[: 1 + others]
    v, f, sums = rest[1 + others :]
    v[...] = spread[...] + told(far, received)
    own = own_lanes(rows, levels)
    mixed, last, kept = [], [], {}
    for at in range(0, columns, TILE):
        tile = pl.ds(at, TILE)
        q, b = apply_tile(levels, v, statics, ends, at, kept)
        f[pl.ds(EDGE + at, TILE)] = b
        q, b, ocean = q[:, own], b[:, own], own_part[7, tile]
        mixed.append(image[tile, own] * q)
        still = jnp.where(ocean > 0.5, b, q)
        last.append(still * still)
    apply_rim(levels, columns, v, f, rim)
    sums[...] = jnp.concatenate([early[0:2], lane_sums(mixed), lane_sums(last), early[4:8]], axis=0)


def turn_kernel(rows, levels, columns, precond, image, again, f, own_part, ghost_part, patches, ends, *outs):
    statics = own_part, ghost_part, patches
    z = outs[4]
    own = own_lanes(rows, levels)
    kept = {}
    for at in range(0, columns, TILE):
        second = apply_tile(levels, f, statics, ends, at, kept)[1]
        tile = pl.ds(at, TILE)
        z[tile] = jnp.where(coefficient(statics, 7, at) > 0.5, second, again[pl.ds(EDGE + at, TILE)])
    group = REACH * levels
    slab = pl.ds(EDGE, columns)
    for j in range(0, rows, REACH):
        at = slice(own.start + j * levels, own.start + j * levels + group)
        for out, x in zip(outs, (precond[slab, at], image[:, at], again[slab, at], z[:, at])):
            t = x.T
            for i in range(REACH):
                out[pl.ds(j + i, levels, stride=rows), :] = t[i * levels : (i + 1) * levels]


PIECES = 4


def combine_kernel(sums, noise, precond, image, again, along, answer, left, x, y, sems):
    total = jnp.sum(sums[...], axis=1, keepdims=True)
    energy, curve, mixed, last = total[0:1], total[1:2], total[2:3], total[3:4]
    alpha = energy / curve
    beta = alpha / SCALE
    growth = alpha * beta * mixed / energy
    step = energy * (growth - 1.0) / (beta * beta * last - growth * growth * curve)
    keep = alpha + step * growth
    back = step * beta
    size = noise.shape[0] // PIECES
    moves = []
    for k in range(PIECES):
        part = pl.ds(k * size, size)
        x[part] = keep * precond[part] - back * again[part]
        moves.append(pltpu.make_async_copy(x.at[part], answer.at[part], sems.at[0, k]))
        moves[-1].start()
        y[part] = noise[part] - (keep * image[part] - back * along[part])
        moves.append(pltpu.make_async_copy(y.at[part], left.at[part], sems.at[1, k]))
        moves[-1].start()
    for move in moves:
        move.wait()


def doubling(count):
    steps = []
    while 2 ** len(steps) < count:
        steps.append(2 ** len(steps))
    return steps


def summed(x):
    count, bands = lax.axis_size("lon"), lax.axis_size("lat")
    x = x + lax.ppermute(x, "lon", [(i, i ^ 1) for i in range(count)])
    for step in doubling(count)[1:]:
        x = x + lax.ppermute(x, "lon", [(i, i ^ step ^ 1) for i in range(count)])
    for step in doubling(bands):
        pairs = [(i * bands + j, (i ^ 1) * bands + (j ^ step)) for i in range(count) for j in range(bands)]
        x = x + lax.ppermute(x, ("lon", "lat"), pairs)
    return x


def body(near, far, weights, columns_of, noise, kappa2, conduct, land):
    levels, rows, columns = noise.shape
    count = lax.axis_size("lon")
    others = count // 4
    flat = levels * rows
    group = REACH * levels
    lanes = flat + 2 * group
    tall = columns + 2 * EDGE
    rho = circle_kernel(count * columns)[0]
    noise = noise.reshape(flat, columns)
    kappa2 = kappa2.reshape(flat, columns)
    land = land.reshape(flat, columns)
    conduct = conduct.reshape(3, flat, columns)

    sources = (noise, kappa2, conduct, land, near, far, weights, columns_of)
    planes = (PLANES, levels, columns)
    second, first, noise, kappa2, conduct, land, near, far, weights, columns_of = pl.pallas_call(
        functools.partial(band_kernel, rows, levels),
        out_shape=[pltpu.VMEM(planes, jnp.float32)] * 2 + [pltpu.VMEM(x.shape, x.dtype) for x in sources],
        in_specs=[pl.BlockSpec(memory_space=pltpu.HBM)] * len(sources),
        out_specs=whole(2 + len(sources)),
        scratch_shapes=[pltpu.SemaphoreType.DMA((len(sources),))],
        compiler_params=pltpu.CompilerParams(vmem_limit_bytes=8 << 20),
        name="band_kernel",
    )(*[pltpu.with_memory_space_constraint(x, pltpu.HBM) for x in sources])
    lat_a, lat_b = lat_perms(count, lax.axis_size("lat"))
    to_band = lambda x, pairs: lax.ppermute(x, ("lon", "lat"), pairs)
    got_second, got_first = to_band(second, lat_b), to_band(first, lat_a)

    own_field, mine = call(
        functools.partial(field_kernel, rows, levels), [(columns, flat), (8, flat)], noise, weights
    )
    made, own_edge, to_first, to_second = call(
        functools.partial(own_kernel, rows, levels, columns),
        [(5, columns, flat), (8, flat), (8, flat), (8, flat)],
        kappa2, conduct, land, own_field,
    )
    lon_a, lon_b = lon_perms(count)

    def farther(two, got_two):
        if count == 4:
            return []
        (four,) = call(functools.partial(quad_kernel, rho, columns), [(8, two.shape[1])], two, got_two)
        return [lax.ppermute(four, "lon", [(i, (i + d) % count) for i in range(count)]) for d in range(4, count, 4)]

    got = lax.ppermute(mine, "lon", lon_a)
    (two,) = call(functools.partial(chip_kernel, rho, columns), [(16, flat)], mine, to_second, got)
    got_two = lax.ppermute(two, "lon", lon_b)
    (got_one,) = call(list_kernel, [(16, flat)], got, lax.ppermute(to_first, "lon", lon_a))
    lists = [got_one, got_two] + farther(two, got_two)
    own_spread, own_part = call(
        functools.partial(near_kernel, levels), [(tall, flat), (8, columns, flat)], near, own_field, made
    )
    sent = (*lists[:2], own_edge, *lists[2:])
    heights = 2 * LIST + 2 + sum(x.shape[0] for x in lists[2:])
    side_second, side_first = call(functools.partial(forward_kernel, group), [(heights, group)] * 2, *sent)
    side_second, side_first = to_band(side_second, lat_b), to_band(side_first, lat_a)
    ghost_spread, ghost_part, patches = call(
        functools.partial(ghost_kernel, levels, columns),
        [(tall, 2 * group), (8, columns, 2 * group), (3, columns, group)],
        got_second, got_first, near, made, own_part,
    )
    precond, image, ends, rim, to_first, to_second = call(
        functools.partial(first_kernel, rows, levels, columns, others),
        [(tall, lanes), (columns, lanes), (7, 2 * TILE, lanes), (7, 8, lanes), (8, lanes), (8, lanes)],
        own_spread, own_edge, ghost_spread, own_part, ghost_part, patches, far, columns_of, side_second, side_first, *lists,
        scratch=[(tall, lanes)],
    )
    got_one = lax.ppermute(to_first, "lon", lon_a)
    (two,) = call(functools.partial(again_kernel, rho, columns), [(8, lanes)], to_second, got_one)
    got_two = lax.ppermute(two, "lon", lon_b)
    lists = [got_one, got_two] + farther(two, got_two)
    spread, sums = call(
        functools.partial(between_kernel, rows, levels, columns),
        [(tall, lanes), (8, 128)],
        near, own_field, precond, image,
    )
    again, half, sums = call(
        functools.partial(second_kernel, levels, columns, rows, others),
        [(tall, lanes), (tall, lanes), (8, 128)],
        spread, sums, image, own_part, ghost_part, patches, ends, far, rim, *lists,
    )
    sums = summed(sums)
    turned_back = call(
        functools.partial(turn_kernel, rows, levels, columns),
        [(flat, columns)] * 4 + [(columns, lanes)],
        precond, image, again, half, own_part, ghost_part, patches, ends,
    )[:4]
    operands = [pltpu.with_memory_space_constraint(x, pltpu.VMEM) for x in (sums, noise, *turned_back)]
    answer, left = pl.pallas_call(
        combine_kernel,
        out_shape=[jax.ShapeDtypeStruct((flat, columns), jnp.float32)] * 2,
        in_specs=whole(len(operands)),
        out_specs=[pl.BlockSpec(memory_space=pltpu.HBM)] * 2,
        scratch_shapes=[pltpu.VMEM((flat, columns), jnp.float32)] * 2 + [pltpu.SemaphoreType.DMA((2, PIECES))],
        compiler_params=pltpu.CompilerParams(vmem_limit_bytes=8 << 20),
        name="combine_kernel",
    )(*operands)
    return answer.reshape(levels, rows, columns), left.reshape(levels, rows, columns)


def solution(mesh):
    def run(noise, kappa2, conduct, land):
        count = mesh.shape["lon"]
        matrices = circle_matrices(count, noise.shape[2] // count)
        return jax.shard_map(
            functools.partial(body, *matrices),
            mesh=mesh,
            in_specs=(
                P("ens", "lat", "lon"),
                P(None, "lat", "lon"),
                P(None, None, "lat", "lon"),
                P(None, "lat", "lon"),
            ),
            out_specs=(P("ens", "lat", "lon"), P("ens", "lat", "lon")),
            check_vma=False,
        )(noise, kappa2, conduct, land)

    return run
```

```python
import functools
import math

import jax
import jax.numpy as jnp
import numpy as np
from jax import lax
from jax.experimental import pallas as pl
from jax.experimental.pallas import tpu as pltpu
from jax.sharding import PartitionSpec as P

base_kappa = 0.001
base_conduct = 1.0

SCALE = 2.0**-31
REACH = 4
TILE = 8
EDGE = 8

HIGHEST = lax.Precision.HIGHEST


def dot(a, b):
    return jnp.dot(a, b, precision=HIGHEST, preferred_element_type=jnp.float32)


def circle_kernel(total):
    middle = 2.0 + base_kappa / base_conduct
    rho = (middle - math.sqrt(middle * middle - 4.0)) / 2.0
    height = 1.0 / (1.0 / rho - rho) / base_conduct
    wrap = rho**total
    shift = (1.0 + rho * rho) / (1.0 - rho * rho) + total * wrap / (1.0 - wrap)
    front = height * height / (1.0 - wrap)
    return rho, front, shift


def circle_matrices(count, columns):
    total = count * columns
    rho, front, shift = circle_kernel(total)

    def one_side(n):
        return front * rho**n * (n + shift)

    def both_sides(n):
        return one_side(n) + one_side(total - n)

    place = np.arange(columns)
    rows = columns + 2 * EDGE
    x = np.arange(rows) - EDGE
    used = (x >= -2) & (x < columns + 2)
    near = both_sides(np.abs(x[:, None] - place[None, :])) * used[:, None]
    back = columns - 1 - place
    moments = np.zeros((8, columns))
    moments[0] = rho**place
    moments[1] = place * rho**place
    moments[2] = rho**back
    moments[3] = back * rho**back

    def block(start, size, neighbour):
        start = start % count * columns
        a = start - x
        b = total - start + x - (size * columns - 1)
        out = np.zeros((rows, 8))
        out[:, 0] = front * rho**a * (a + shift)
        out[:, 1] = front * rho**a
        out[:, 2] = front * rho**b * (b + shift)
        out[:, 3] = front * rho**b
        amend = both_sides(1) - both_sides(-1)
        if neighbour == "east":
            out[EDGE + columns + 1, 4] = amend
        if neighbour == "west":
            out[EDGE - 2, 4] = amend
        return out * used[:, None]

    fours = range(4, count, 4)
    even = [block(1, 1, "east"), block(-2, 2, "west")] + [block(-2 - d, 4, "") for d in fours]
    odd = [block(-1, 1, "west"), block(1, 2, "east")] + [block(-1 - d, 4, "") for d in fours]
    far = np.stack([np.concatenate(even, axis=1), np.concatenate(odd, axis=1)])
    far = np.pad(far, ((0, 0), (0, 0), (0, -far.shape[2] % 16))).astype(np.float32)
    high, middle, low = thirds(far, lambda x: x.astype(np.float32))
    far = np.concatenate([high, high, middle, high, middle, low], axis=2)
    columns_of = np.broadcast_to(moments[:4, :, None], (4, columns, 128))
    as_f32 = lambda m: np.asarray(m, np.float32)
    return as_f32(near), far, as_f32(moments), as_f32(columns_of)


def lon_perms(count):
    first = [(i, i ^ 1) for i in range(count)]
    return first, [(i, (i - 1 + 2 * (i % 2)) % count) for i in range(count)]


def lat_perms(count, bands):
    first, second = [], []
    for i in range(count):
        for j in range(bands):
            k = j - 1 + 2 * (j % 2)
            first.append((i * bands + j, i * bands + (j ^ 1)))
            second.append((i * bands + j, i * bands + k if 0 <= k < bands else (i ^ 1) * bands + j))
    return first, second


def inner_band():
    return (lax.axis_index("lat") > 0) & (lax.axis_index("lat") < lax.axis_size("lat") - 1)


def lane_roll(x, by):
    count = x.shape[1] // 128
    skip, by = divmod(by % x.shape[1], 128)
    parts = [x[:, k * 128 : (k + 1) * 128] for k in range(count)]
    if by:
        turned = [pltpu.roll(p, by, 1) for p in parts]
        lane = lax.broadcasted_iota(jnp.int32, (1, 128), 1)
        parts = [jnp.where(lane < by, turned[k - 1], turned[k]) for k in range(count)]
    return jnp.concatenate([parts[(k - skip) % count] for k in range(count)], axis=1)


def thirds(x, cast):
    high = x.astype(jnp.bfloat16)
    rest = x - cast(high)
    middle = rest.astype(jnp.bfloat16)
    return high, middle, (rest - cast(middle)).astype(jnp.bfloat16)


def whole(n):
    return [pl.BlockSpec(memory_space=pltpu.VMEM)] * n


def call(kernel, outs, *args, scratch=()):
    args = [pltpu.with_memory_space_constraint(a, pltpu.VMEM) for a in args]
    return pl.pallas_call(
        kernel,
        out_shape=[pltpu.VMEM(s, jnp.float32) for s in outs],
        in_specs=whole(len(args)),
        out_specs=whole(len(outs)),
        scratch_shapes=[pltpu.VMEM(s, jnp.float32) for s in scratch],
        compiler_params=pltpu.CompilerParams(vmem_limit_bytes=24 << 20),
        name=getattr(kernel, "func", kernel).__name__,
    )(*args)


FULL, PART = REACH, REACH - 1
PLANES = 2 * FULL + 3 * PART


def band_kernel(rows, levels, *refs):
    sources, (first, second), copies, sems = refs[:8], refs[8:10], refs[10:18], refs[18]
    order = (0, 3, 2, 1, 4, 5, 6, 7)
    moves = [pltpu.make_async_copy(sources[k], copies[k], sems.at[k]) for k in order]
    for move in moves:
        move.start()
    noise, kappa2, conduct, land = copies[:4]
    odd = lax.axis_index("lat") % 2
    sides = ((first, odd), (second, 1 - odd))
    plane = lambda lat: pl.ds(lat, levels, stride=rows)
    moves[0].wait()
    for out, side in sides:
        for j in range(FULL):
            out[j] = noise[plane((1 - side) * (rows - FULL) + j), :]
    for move in moves[1:4]:
        move.wait()
    columns = noise.shape[1]
    lane = lax.broadcasted_iota(jnp.int32, (1, columns), 1)
    level = lax.broadcasted_iota(jnp.int32, (levels, 1), 0)
    for out, side in sides:
        base = (1 - side) * (rows - FULL)
        ocean = [land[plane(base + j), :].astype(jnp.float32) for j in range(FULL)]
        north = [conduct[1, plane(base + j), :] for j in range(FULL)]
        for j in range(PART):
            out[FULL + 3 * PART + j] = north[j] * ocean[j] * ocean[j + 1]
        out[FULL + 4 * PART] = north[PART]
        near = lambda x, j: jnp.where(side == 0, x[j + 1], x[j])
        for j in range(PART):
            at = plane(base + 1 - side + j)
            o, n = near(ocean, j), near(north, j)
            below = north[j] if j == 0 else jnp.where(side == 0, north[j], north[j - 1])
            south = jnp.where(side == 0, below, 0.0) if j == 0 else below
            e, k = conduct[0, at, :], kappa2[at, :]
            u = jnp.where(level == levels - 1, 0.0, conduct[2, at, :])
            west = jnp.where(lane == 0, 0.0, pltpu.roll(e, 1, 1))
            ocean_east = jnp.where(lane == columns - 1, 1.0, pltpu.roll(o, columns - 1, 1))
            out[FULL + j] = o * (k + e + west + n + south + u + pltpu.roll(u, 1, 0))
            out[FULL + PART + j] = e * o * ocean_east
            out[FULL + 2 * PART + j] = u * o * pltpu.roll(o, levels - 1, 0)
    for move in moves[4:]:
        move.wait()


def turned(planes, rows_of_planes):
    blocks = [jnp.concatenate(planes[j : j + REACH], axis=0) for j in range(0, rows_of_planes, REACH)]
    return jnp.concatenate([b.T for b in blocks], axis=1)


def coefficients(levels, band, kappa, east, north, upper, ocean):
    columns, lanes = kappa.shape
    lane = lax.broadcasted_iota(jnp.int32, (1, lanes), 1)
    row = lax.broadcasted_iota(jnp.int32, (columns, 1), 0)
    upper = jnp.where(lane % levels == levels - 1, 0.0, upper)
    south = jnp.where(lane % band < levels, 0.0, lane_roll(north, levels))
    west = jnp.where(row == 0, 0.0, pltpu.roll(east, 1, 0))
    ocean_east = jnp.where(row == columns - 1, 1.0, pltpu.roll(ocean, columns - 1, 0))
    diagonal = ocean * (kappa + east + west + north + south + upper + lane_roll(upper, 1))
    return diagonal, east * ocean * ocean_east, upper * ocean * lane_roll(ocean, -1)


def field_kernel(rows, levels, noise, weights, field, sums):
    r = turned([noise[pl.ds(j, levels, stride=rows), :] for j in range(rows)], rows)
    field[...] = r
    sums[...] = dot(weights[...], r)


def own_kernel(
    rows, levels, columns,
    kappa2, conduct, land, field,
    statics, edge, to_first, to_second,
):
    last_band = lax.axis_index("lat") == lax.axis_size("lat") - 1
    lon_odd = lax.axis_index("lon") % 2
    lanes = rows * levels

    def own(load):
        return turned([load(pl.ds(j, levels, stride=rows)) for j in range(rows)], rows)

    ocean = own(lambda at: land[at, :].astype(jnp.float32))
    north = own(lambda at: conduct[1, at, :])
    kappa = own(lambda at: kappa2[at, :])
    east = own(lambda at: conduct[0, at, :])
    upper = own(lambda at: conduct[2, at, :])
    lane = lax.broadcasted_iota(jnp.int32, (1, lanes), 1)
    north = jnp.where(last_band & (lane >= lanes - levels), 0.0, north)
    diagonal, to_east, to_upper = coefficients(levels, lanes, kappa, east, north, upper, ocean)
    for k, x in enumerate((diagonal, to_east, north, to_upper, ocean)):
        statics[k] = x
    end = columns - 1
    edge[...] = jnp.concatenate([east[end:], jnp.zeros((7, lanes), jnp.float32)], axis=0)
    blank = jnp.zeros((1, lanes), jnp.float32)
    for_east = [field[end:], diagonal[end:], to_east[end - 1 : end], east[end:], ocean[end:], north[end:], to_upper[end:], blank]
    for_west = [field[:1], diagonal[:1], to_east[:1], east[:1], ocean[:1], north[:1], to_upper[:1], blank]
    for_east = jnp.concatenate(for_east, axis=0)
    for_west = jnp.concatenate(for_west, axis=0)
    to_first[...] = jnp.where(lon_odd == 0, for_east, for_west)
    to_second[...] = jnp.where(lon_odd == 0, for_west, for_east)


MOMENTS, LIST = 4, 11


def list_kernel(moments, edges, out):
    out[...] = jnp.concatenate([moments[0:MOMENTS], edges[...], jnp.zeros((4, edges.shape[1]), jnp.float32)], axis=0)


def ghost_kernel(levels, columns, got_first, got_second, near, made, own, spread, ghosts, patches):
    lat_odd = lax.axis_index("lat") % 2
    group = REACH * levels

    def ghost(k, count, north):
        a = got_first[pl.ds(k, count)].reshape(count * levels, columns)
        b = jnp.where(inner_band(), got_second[pl.ds(k, count)], 0.0).reshape(count * levels, columns)
        from_first = (lat_odd == 0) if north else (lat_odd == 1)
        planes = jnp.where(from_first, a, b)
        if count == REACH:
            return planes.T
        blank = jnp.zeros((group - count * levels, columns), jnp.float32)
        return jnp.concatenate([planes, blank] if north else [blank, planes], axis=0).T

    pieces = ((0, FULL), (FULL, PART), (FULL + PART, PART), (FULL + 2 * PART, PART), (FULL + 3 * PART, FULL))
    r, diagonal, to_east, to_upper, north = (
        jnp.concatenate([ghost(k, count, False), ghost(k, count, True)], axis=1) for k, count in pieces
    )
    spread[...] = dot(near[...], r)
    ocean = jnp.where(diagonal > 0.0, 1.0, 0.0)
    last = made.shape[2] - group
    low, high = slice(0, group), slice(group, 2 * group)
    lane = lax.broadcasted_iota(jnp.int32, (1, group), 1)
    first_one, last_one = lane < levels, lane >= group - levels
    up = lambda x: pltpu.roll(x, levels, 1)
    down = lambda x: pltpu.roll(x, group - levels, 1)
    own_low, own_high = pl.ds(0, group), pl.ds(last, group)
    ocean_low, ocean_high = made[4, :, own_low], made[4, :, own_high]
    north_high = own[3, :, own_high]
    north_high = jnp.where(last_one, north_high * down(ocean[:, high]), north_high)
    ghost_low = north[:, low]
    ghost_low = jnp.where(last_one, ghost_low * ocean[:, low] * down(ocean_low), ghost_low)
    ghost_high = north[:, high]
    patches[0] = own[0, :, own_low] + jnp.where(first_one, ocean_low * up(north[:, low]), 0.0)
    patches[1] = jnp.where(first_one, up(ghost_low), own[4, :, own_low])
    patches[2] = north_high
    row = lax.broadcasted_iota(jnp.int32, (columns, 1), 0)
    for part, n, below in ((low, ghost_low, ghost_low), (high, ghost_high, north_high)):
        d, e, u, o = (x[:, part] for x in (diagonal, to_east, to_upper, ocean))
        if part is high:
            d = d + jnp.where(first_one, o * up(made[2, :, own_high]), 0.0)
        w = jnp.where(row == 0, 0.0, pltpu.roll(e, 1, 0))
        for k, x in enumerate((d, e, w, n, jnp.where(first_one, up(below), up(n)), u, pltpu.roll(u, 1, 1), o)):
            ghosts[k, :, part] = x


def coefficient(statics, k, at):
    own, ghosts, patches = statics
    group = ghosts.shape[2] // 2
    tile = pl.ds(at, TILE)
    x = own[k, tile]
    parts = [x[:, j : j + group] for j in range(0, x.shape[1], group)]
    if k in (0, 4):
        parts[0] = patches[0 if k == 0 else 1, tile]
    if k == 3:
        parts[-1] = patches[2, tile]
    g = ghosts[k, tile]
    return jnp.concatenate([g[:, :group]] + parts + [g[:, group:]], axis=1)


def forward_kernel(group, *refs):
    (one, two, edge), more, (first, second) = refs[:3], refs[3:-2], refs[-2:]
    odd = lax.axis_index("lat") % 2
    whole_rows = [one[0:LIST], two[0:LIST], edge[0:2]] + [x[...] for x in more]
    x = jnp.concatenate(whole_rows, axis=0)
    low, high = x[:, 0:group], x[:, x.shape[1] - group :]
    first[...] = jnp.where(odd == 0, high, low)
    second[...] = jnp.where(odd == 0, low, high)


def joint_moments(left, right, rho, width):
    c = rho**width
    return jnp.concatenate(
        [
            left[0:1] + c * right[0:1],
            left[1:2] + c * (right[1:2] + width * right[0:1]),
            right[2:3] + c * left[2:3],
            right[3:4] + c * (left[3:4] + width * left[2:3]),
        ],
        axis=0,
    )


def chip_kernel(rho, columns, own, edges, got, out):
    even = lax.axis_index("lon") % 2 == 0
    mine, its = own[0:MOMENTS], got[0:MOMENTS]
    m = joint_moments(jnp.where(even, mine, its), jnp.where(even, its, mine), rho, columns)
    blank = jnp.zeros((out.shape[0] - MOMENTS - edges.shape[0], m.shape[1]), jnp.float32)
    out[...] = jnp.concatenate([m, edges[...], blank], axis=0)


def again_kernel(rho, columns, own, got, out):
    even = lax.axis_index("lon") % 2 == 0
    mine, its = own[0:MOMENTS], got[0:MOMENTS]
    out[...] = own[...]
    out[0:MOMENTS] = joint_moments(jnp.where(even, mine, its), jnp.where(even, its, mine), rho, columns)


def quad_kernel(rho, columns, mine, got, out):
    even = lax.axis_index("lon") % 2 == 0
    a, b = mine[0:4], got[0:4]
    m = joint_moments(jnp.where(even, b, a), jnp.where(even, a, b), rho, 2 * columns)
    out[...] = jnp.concatenate([m, jnp.zeros_like(m)], axis=0)


def near_kernel(levels, near, field, made, spread, statics):
    spread[...] = dot(near[...], field[...])
    columns = field.shape[0]
    lanes = field.shape[1]
    lane = lax.broadcasted_iota(jnp.int32, (1, lanes), 1)
    row = lax.broadcasted_iota(jnp.int32, (TILE, 1), 0)
    for at in range(0, columns, TILE):
        tile = pl.ds(at, TILE)
        d, e, n, u, o = (made[k, tile] for k in range(5))
        w = pltpu.roll(e, 1, 0)
        w = jnp.where(row == 0, carried, w) if at else w
        carried = e[TILE - 1 :]
        n = n * o * jnp.where(lane >= lanes - levels, 1.0, lane_roll(o, -levels))
        for k, x in enumerate((d, e, w, n, lane_roll(n, levels), u, lane_roll(u, 1), o)):
            statics[k, tile] = x


def told(far, lists):
    x = jnp.concatenate([t[0:8] for t in lists], axis=0)
    if x.shape[0] % 16:
        x = jnp.concatenate([x, jnp.zeros((8, x.shape[1]), jnp.float32)], axis=0)
    high, middle, low = thirds(x, lambda p: p.astype(jnp.float32))
    stacked = jnp.concatenate([high, middle, high, low, middle, high], axis=0)
    return jnp.dot(far[lax.axis_index("lon") % 2], stacked, preferred_element_type=jnp.float32)


def faces(v, n, s, u, low, levels):
    return n * lane_roll(v, -levels) + s * lane_roll(v, levels) + u * lane_roll(v, -1) + low * lane_roll(v, 1)


def shifts(v, at, kept):
    def turned_rows(i):
        if i not in kept:
            x = v[pl.ds(i, TILE)]
            kept[i] = x, pltpu.roll(x, TILE - 1, 0), pltpu.roll(x, 1, 0)
        return kept[i]

    i = at + EDGE
    row = lax.broadcasted_iota(jnp.int32, (TILE, 1), 0)
    x, east_v, west_v = turned_rows(i)
    east_v = jnp.where(row == TILE - 1, turned_rows(i + TILE)[1], east_v)
    west_v = jnp.where(row == 0, turned_rows(i - TILE)[2], west_v)
    return x, east_v, west_v


def apply_tile(levels, v, statics, ends, at, kept):
    own = statics[0]
    if at == 0:
        faces_of = lambda k: ends[k, 0:TILE]
    elif at + TILE == own.shape[1]:
        faces_of = lambda k: ends[k, TILE : 2 * TILE]
    else:
        faces_of = lambda k: coefficient(statics, k, at)
    d, e, w, n, s, u, low = (faces_of(k) for k in range(7))
    here, east_v, west_v = shifts(v, at, kept)
    return here, d * here - e * east_v - w * west_v - faces(here, n, s, u, low, levels)


def apply_rim(levels, columns, v, f, rim):
    end = EDGE + columns
    pick = lambda a, b: jnp.concatenate([v[a : a + 1], v[b : b + 1], jnp.zeros((6, v.shape[1]), jnp.float32)], axis=0)
    here = pick(EDGE - 1, end)
    g = rim[0] * here - rim[1] * pick(EDGE, end + 1) - rim[2] * pick(EDGE - 2, end - 1)
    g = g - faces(here, rim[3], rim[4], rim[5], rim[6], levels)
    f[EDGE - 1 : EDGE] = g[0:1]
    f[end : end + 1] = g[1:2]


def joined(own, ghost):
    group = ghost.shape[1] // 2
    return jnp.concatenate([ghost[:, :group], own, ghost[:, group:]], axis=1)


def completed(levels, group, diagonal, north, ocean):
    lanes = ocean.shape[1]
    lane = lax.broadcasted_iota(jnp.int32, (1, lanes), 1)
    first_of_band = ((lane >= group) & (lane < group + levels)) | ((lane >= lanes - group) & (lane < lanes - group + levels))
    diagonal = diagonal + jnp.where(first_of_band, ocean * lane_roll(north, levels), 0.0)
    return diagonal, north * ocean * lane_roll(ocean, -levels)


def first_kernel(
    rows, levels, columns, others,
    own_spread, own_edge, ghost_spread, own_part, ghost_part, patches, far, weights, side_first, side_second, *rest,
):
    statics = own_part, ghost_part, patches
    received = rest[: 1 + others]
    v, image, ends, rim, to_first, to_second, f = rest[1 + others :]
    lat_odd = lax.axis_index("lat") % 2
    even = lax.axis_index("lon") % 2 == 0
    group = REACH * levels
    lanes = rows * levels + 2 * group
    a, b = side_first[...], jnp.where(inner_band(), side_second[...], 0.0)
    south, north = jnp.where(lat_odd == 1, a, b), jnp.where(lat_odd == 1, b, a)
    lists, k = [], 0
    for x in (received[0][0:LIST], received[1][0:LIST], own_edge[0:2], *[x[...] for x in received[2:]]):
        at = slice(k, k + x.shape[0])
        lists.append(jnp.concatenate([south[at], x, north[at]], axis=1))
        k += x.shape[0]
    last_face = lists.pop(2)[0:1]
    v[...] = joined(own_spread[...], ghost_spread[...]) + told(far, lists)

    one, two = lists[0], lists[1]
    east_list, west_list = jnp.where(even, one, two), jnp.where(even, two, one)
    end = columns - 1
    for k in range(7):
        ends[k, 0:TILE] = coefficient(statics, k, 0)
        ends[k, TILE : 2 * TILE] = coefficient(statics, k, columns - TILE)
    ocean = coefficient(statics, 7, 0)[0:1]
    face_west = west_list[7:8] * west_list[8:9] * ocean
    last_east = ends[1, 2 * TILE - 1 :] * east_list[8:9]
    ends[0, 0:1] = ends[0, 0:1] + ocean * west_list[7:8]
    ends[2, 0:1] = face_west
    ends[1, 2 * TILE - 1 : 2 * TILE] = last_east
    blank = jnp.zeros((6, lanes), jnp.float32)
    stack = lambda p, q: jnp.concatenate([p, q, blank], axis=0)
    rim_diagonal, rim_north = completed(
        levels, group,
        stack(west_list[5:6], east_list[5:6] + east_list[8:9] * last_face),
        stack(west_list[9:10], east_list[9:10]),
        stack(west_list[8:9], east_list[8:9]),
    )
    rim_upper = stack(west_list[10:11], east_list[10:11])
    rim[0] = rim_diagonal
    rim[1] = stack(face_west, east_list[6:7])
    rim[2] = stack(west_list[6:7], last_east)
    rim[3] = rim_north
    rim[4] = lane_roll(rim_north, levels)
    rim[5] = rim_upper
    rim[6] = lane_roll(rim_upper, 1)

    kept = {}
    for at in range(0, columns, TILE):
        f[pl.ds(EDGE + at, TILE)] = apply_tile(levels, v, statics, ends, at, kept)[1]
    apply_rim(levels, columns, v, f, rim)
    m, kept = [0.0] * 4, {}
    for at in range(0, columns, TILE):
        tile = pl.ds(at, TILE)
        second = apply_tile(levels, f, statics, ends, at, kept)[1]
        w = jnp.where(coefficient(statics, 7, at) > 0.5, second, v[pl.ds(EDGE + at, TILE)])
        image[tile] = w
        for k in range(4):
            spread = weights[k, tile]
            m[k] = m[k] + w * jnp.concatenate([spread] * (lanes // 128), axis=1)
    m = [jnp.sum(x, axis=0, keepdims=True) * SCALE for x in m]
    pad = jnp.zeros((3, lanes), jnp.float32)
    for_east = jnp.concatenate(m + [image[end:] * SCALE, pad], axis=0)
    for_west = jnp.concatenate(m + [image[:1] * SCALE, pad], axis=0)
    to_first[...] = jnp.where(even, for_east, for_west)
    to_second[...] = jnp.where(even, for_west, for_east)


def lane_sums(tiles):
    total = functools.reduce(lambda a, b: a + b, tiles)
    s = jnp.sum(total, axis=0, keepdims=True)
    return functools.reduce(lambda a, b: a + b, [s[:, k : k + 128] for k in range(0, s.shape[1], 128)])


def own_lanes(rows, levels):
    return slice(REACH * levels, (REACH + rows) * levels)


def between_kernel(rows, levels, columns, near, field, precond, image, spread, sums):
    own = own_lanes(rows, levels)
    spread[...] = dot(near[...], image[...] * SCALE)
    energy, curve = [], []
    for at in range(0, columns, TILE):
        tile = pl.ds(at, TILE)
        p = precond[pl.ds(EDGE + at, TILE), own]
        energy.append(field[tile] * p)
        curve.append(p * image[tile, own])
    sums[...] = jnp.concatenate([lane_sums(energy), lane_sums(curve), jnp.zeros((6, 128), jnp.float32)], axis=0)


def second_kernel(
    levels, columns, rows, others, spread, early, image, own_part, ghost_part, patches, ends, far, rim, *rest
):
    statics = own_part, ghost_part, patches
    received = rest[: 1 + others]
    v, f, sums = rest[1 + others :]
    v[...] = spread[...] + told(far, received)
    own = own_lanes(rows, levels)
    mixed, last, kept = [], [], {}
    for at in range(0, columns, TILE):
        tile = pl.ds(at, TILE)
        q, b = apply_tile(levels, v, statics, ends, at, kept)
        f[pl.ds(EDGE + at, TILE)] = b
        q, b, ocean = q[:, own], b[:, own], own_part[7, tile]
        mixed.append(image[tile, own] * q)
        still = jnp.where(ocean > 0.5, b, q)
        last.append(still * still)
    apply_rim(levels, columns, v, f, rim)
    sums[...] = jnp.concatenate([early[0:2], lane_sums(mixed), lane_sums(last), early[4:8]], axis=0)


def turn_kernel(rows, levels, columns, precond, image, again, f, own_part, ghost_part, patches, ends, *outs):
    statics = own_part, ghost_part, patches
    z = outs[4]
    own = own_lanes(rows, levels)
    kept = {}
    for at in range(0, columns, TILE):
        second = apply_tile(levels, f, statics, ends, at, kept)[1]
        tile = pl.ds(at, TILE)
        z[tile] = jnp.where(coefficient(statics, 7, at) > 0.5, second, again[pl.ds(EDGE + at, TILE)])
    group = REACH * levels
    slab = pl.ds(EDGE, columns)
    for j in range(0, rows, REACH):
        at = slice(own.start + j * levels, own.start + j * levels + group)
        for out, x in zip(outs, (precond[slab, at], image[:, at], again[slab, at], z[:, at])):
            t = x.T
            for i in range(REACH):
                out[pl.ds(j + i, levels, stride=rows), :] = t[i * levels : (i + 1) * levels]


PIECES = 4


def combine_kernel(sums, noise, precond, image, again, along, answer, left, x, y, sems):
    total = jnp.sum(sums[...], axis=1, keepdims=True)
    energy, curve, mixed, last = total[0:1], total[1:2], total[2:3], total[3:4]
    alpha = energy / curve
    beta = alpha / SCALE
    growth = alpha * beta * mixed / energy
    step = energy * (growth - 1.0) / (beta * beta * last - growth * growth * curve)
    keep = alpha + step * growth
    back = step * beta
    size = noise.shape[0] // PIECES
    moves = []
    for k in range(PIECES):
        part = pl.ds(k * size, size)
        x[part] = keep * precond[part] - back * again[part]
        moves.append(pltpu.make_async_copy(x.at[part], answer.at[part], sems.at[0, k]))
        moves[-1].start()
        y[part] = noise[part] - (keep * image[part] - back * along[part])
        moves.append(pltpu.make_async_copy(y.at[part], left.at[part], sems.at[1, k]))
        moves[-1].start()
    for move in moves:
        move.wait()


def doubling(count):
    steps = []
    while 2 ** len(steps) < count:
        steps.append(2 ** len(steps))
    return steps


def summed(x):
    count, bands = lax.axis_size("lon"), lax.axis_size("lat")
    x = x + lax.ppermute(x, "lon", [(i, i ^ 1) for i in range(count)])
    for step in doubling(count)[1:]:
        x = x + lax.ppermute(x, "lon", [(i, i ^ step ^ 1) for i in range(count)])
    for step in doubling(bands):
        pairs = [(i * bands + j, (i ^ 1) * bands + (j ^ step)) for i in range(count) for j in range(bands)]
        x = x + lax.ppermute(x, ("lon", "lat"), pairs)
    return x


def body(near, far, weights, columns_of, noise, kappa2, conduct, land):
    levels, rows, columns = noise.shape
    count = lax.axis_size("lon")
    others = count // 4
    flat = levels * rows
    group = REACH * levels
    lanes = flat + 2 * group
    tall = columns + 2 * EDGE
    rho = circle_kernel(count * columns)[0]
    noise = noise.reshape(flat, columns)
    kappa2 = kappa2.reshape(flat, columns)
    land = land.reshape(flat, columns)
    conduct = conduct.reshape(3, flat, columns)

    sources = (noise, kappa2, conduct, land, near, far, weights, columns_of)
    planes = (PLANES, levels, columns)
    first, second, noise, kappa2, conduct, land, near, far, weights, columns_of = pl.pallas_call(
        functools.partial(band_kernel, rows, levels),
        out_shape=[pltpu.VMEM(planes, jnp.float32)] * 2 + [pltpu.VMEM(x.shape, x.dtype) for x in sources],
        in_specs=[pl.BlockSpec(memory_space=pltpu.HBM)] * len(sources),
        out_specs=whole(2 + len(sources)),
        scratch_shapes=[pltpu.SemaphoreType.DMA((len(sources),))],
        compiler_params=pltpu.CompilerParams(vmem_limit_bytes=8 << 20),
        name="band_kernel",
    )(*[pltpu.with_memory_space_constraint(x, pltpu.HBM) for x in sources])
    lat_a, lat_b = lat_perms(count, lax.axis_size("lat"))
    to_band = lambda x, pairs: lax.ppermute(x, ("lon", "lat"), pairs)
    got_second, got_first = to_band(second, lat_b), to_band(first, lat_a)

    own_field, mine = call(
        functools.partial(field_kernel, rows, levels), [(columns, flat), (8, flat)], noise, weights
    )
    made, own_edge, to_first, to_second = call(
        functools.partial(own_kernel, rows, levels, columns),
        [(5, columns, flat), (8, flat), (8, flat), (8, flat)],
        kappa2, conduct, land, own_field,
    )
    lon_a, lon_b = lon_perms(count)

    def farther(two, got_two):
        if count == 4:
            return []
        (four,) = call(functools.partial(quad_kernel, rho, columns), [(8, two.shape[1])], two, got_two)
        return [lax.ppermute(four, "lon", [(i, (i + d) % count) for i in range(count)]) for d in range(4, count, 4)]

    got = lax.ppermute(mine, "lon", lon_a)
    (two,) = call(functools.partial(chip_kernel, rho, columns), [(16, flat)], mine, to_second, got)
    got_two = lax.ppermute(two, "lon", lon_b)
    (got_one,) = call(list_kernel, [(16, flat)], got, lax.ppermute(to_first, "lon", lon_a))
    lists = [got_one, got_two] + farther(two, got_two)
    own_spread, own_part = call(
        functools.partial(near_kernel, levels), [(tall, flat), (8, columns, flat)], near, own_field, made
    )
    sent = (*lists[:2], own_edge, *lists[2:])
    heights = 2 * LIST + 2 + sum(x.shape[0] for x in lists[2:])
    side_first, side_second = call(functools.partial(forward_kernel, group), [(heights, group)] * 2, *sent)
    side_second, side_first = to_band(side_second, lat_b), to_band(side_first, lat_a)
    ghost_spread, ghost_part, patches = call(
        functools.partial(ghost_kernel, levels, columns),
        [(tall, 2 * group), (8, columns, 2 * group), (3, columns, group)],
        got_first, got_second, near, made, own_part,
    )
    precond, image, ends, rim, to_first, to_second = call(
        functools.partial(first_kernel, rows, levels, columns, others),
        [(tall, lanes), (columns, lanes), (7, 2 * TILE, lanes), (7, 8, lanes), (8, lanes), (8, lanes)],
        own_spread, own_edge, ghost_spread, own_part, ghost_part, patches, far, columns_of, side_first, side_second, *lists,
        scratch=[(tall, lanes)],
    )
    got_one = lax.ppermute(to_first, "lon", lon_a)
    (two,) = call(functools.partial(again_kernel, rho, columns), [(8, lanes)], to_second, got_one)
    got_two = lax.ppermute(two, "lon", lon_b)
    lists = [got_one, got_two] + farther(two, got_two)
    spread, sums = call(
        functools.partial(between_kernel, rows, levels, columns),
        [(tall, lanes), (8, 128)],
        near, own_field, precond, image,
    )
    again, half, sums = call(
        functools.partial(second_kernel, levels, columns, rows, others),
        [(tall, lanes), (tall, lanes), (8, 128)],
        spread, sums, image, own_part, ghost_part, patches, ends, far, rim, *lists,
    )
    sums = summed(sums)
    turned_back = call(
        functools.partial(turn_kernel, rows, levels, columns),
        [(flat, columns)] * 4 + [(columns, lanes)],
        precond, image, again, half, own_part, ghost_part, patches, ends,
    )[:4]
    operands = [pltpu.with_memory_space_constraint(x, pltpu.VMEM) for x in (sums, noise, *turned_back)]
    answer, left = pl.pallas_call(
        combine_kernel,
        out_shape=[jax.ShapeDtypeStruct((flat, columns), jnp.float32)] * 2,
        in_specs=whole(len(operands)),
        out_specs=[pl.BlockSpec(memory_space=pltpu.HBM)] * 2,
        scratch_shapes=[pltpu.VMEM((flat, columns), jnp.float32)] * 2 + [pltpu.SemaphoreType.DMA((2, PIECES))],
        compiler_params=pltpu.CompilerParams(vmem_limit_bytes=8 << 20),
        name="combine_kernel",
    )(*operands)
    return answer.reshape(levels, rows, columns), left.reshape(levels, rows, columns)


def solution(mesh):
    def run(noise, kappa2, conduct, land):
        count = mesh.shape["lon"]
        matrices = circle_matrices(count, noise.shape[2] // count)
        return jax.shard_map(
            functools.partial(body, *matrices),
            mesh=mesh,
            in_specs=(
                P("ens", "lat", "lon"),
                P(None, "lat", "lon"),
                P(None, None, "lat", "lon"),
                P(None, "lat", "lon"),
            ),
            out_specs=(P("ens", "lat", "lon"), P("ens", "lat", "lon")),
            check_vma=False,
        )(noise, kappa2, conduct, land)

    return run
```

```python
import functools
import math

import jax
import jax.numpy as jnp
import numpy as np
from jax import lax
from jax.experimental import pallas as pl
from jax.experimental.pallas import tpu as pltpu
from jax.sharding import PartitionSpec as P

base_kappa = 0.001
base_conduct = 1.0

SCALE = 2.0**-31
REACH = 4
TILE = 8
EDGE = 8

HIGHEST = lax.Precision.HIGHEST


def dot(a, b):
    return jnp.dot(a, b, precision=HIGHEST, preferred_element_type=jnp.float32)


def circle_kernel(total):
    middle = 2.0 + base_kappa / base_conduct
    rho = (middle - math.sqrt(middle * middle - 4.0)) / 2.0
    height = 1.0 / (1.0 / rho - rho) / base_conduct
    wrap = rho**total
    shift = (1.0 + rho * rho) / (1.0 - rho * rho) + total * wrap / (1.0 - wrap)
    front = height * height / (1.0 - wrap)
    return rho, front, shift


def circle_matrices(count, columns):
    total = count * columns
    rho, front, shift = circle_kernel(total)

    def one_side(n):
        return front * rho**n * (n + shift)

    def both_sides(n):
        return one_side(n) + one_side(total - n)

    place = np.arange(columns)
    rows = columns + 2 * EDGE
    x = np.arange(rows) - EDGE
    used = (x >= -2) & (x < columns + 2)
    near = both_sides(np.abs(x[:, None] - place[None, :])) * used[:, None]
    back = columns - 1 - place
    moments = np.zeros((8, columns))
    moments[0] = rho**place
    moments[1] = place * rho**place
    moments[2] = rho**back
    moments[3] = back * rho**back

    def block(start, size, neighbour):
        start = start % count * columns
        a = start - x
        b = total - start + x - (size * columns - 1)
        out = np.zeros((rows, 8))
        out[:, 0] = front * rho**a * (a + shift)
        out[:, 1] = front * rho**a
        out[:, 2] = front * rho**b * (b + shift)
        out[:, 3] = front * rho**b
        amend = both_sides(1) - both_sides(-1)
        if neighbour == "east":
            out[EDGE + columns + 1, 4] = amend
        if neighbour == "west":
            out[EDGE - 2, 4] = amend
        return out * used[:, None]

    fours = range(4, count, 4)
    even = [block(1, 1, "east"), block(-2, 2, "west")] + [block(-2 - d, 4, "") for d in fours]
    odd = [block(-1, 1, "west"), block(1, 2, "east")] + [block(-1 - d, 4, "") for d in fours]
    far = np.stack([np.concatenate(even, axis=1), np.concatenate(odd, axis=1)])
    far = np.pad(far, ((0, 0), (0, 0), (0, -far.shape[2] % 16))).astype(np.float32)
    high, middle, low = thirds(far, lambda x: x.astype(np.float32))
    far = np.concatenate([high, high, middle, high, middle, low], axis=2)
    columns_of = np.broadcast_to(moments[:4, :, None], (4, columns, 128))
    as_f32 = lambda m: np.asarray(m, np.float32)
    return as_f32(near), far, as_f32(moments), as_f32(columns_of)


def lon_perms(count):
    first = [(i, i ^ 1) for i in range(count)]
    return first, [(i, (i - 1 + 2 * (i % 2)) % count) for i in range(count)]


def lat_perms(count, bands):
    first, second = [], []
    for i in range(count):
        for j in range(bands):
            k = j - 1 + 2 * (j % 2)
            first.append((i * bands + j, i * bands + (j ^ 1)))
            second.append((i * bands + j, i * bands + k if 0 <= k < bands else (i ^ 1) * bands + j))
    return first, second


def inner_band():
    return (lax.axis_index("lat") > 0) & (lax.axis_index("lat") < lax.axis_size("lat") - 1)


def lane_roll(x, by):
    count = x.shape[1] // 128
    skip, by = divmod(by % x.shape[1], 128)
    parts = [x[:, k * 128 : (k + 1) * 128] for k in range(count)]
    if by:
        turned = [pltpu.roll(p, by, 1) for p in parts]
        lane = lax.broadcasted_iota(jnp.int32, (1, 128), 1)
        parts = [jnp.where(lane < by, turned[k - 1], turned[k]) for k in range(count)]
    return jnp.concatenate([parts[(k - skip) % count] for k in range(count)], axis=1)


def thirds(x, cast):
    high = x.astype(jnp.bfloat16)
    rest = x - cast(high)
    middle = rest.astype(jnp.bfloat16)
    return high, middle, (rest - cast(middle)).astype(jnp.bfloat16)


def whole(n):
    return [pl.BlockSpec(memory_space=pltpu.VMEM)] * n


def call(kernel, outs, *args, scratch=()):
    args = [pltpu.with_memory_space_constraint(a, pltpu.VMEM) for a in args]
    return pl.pallas_call(
        kernel,
        out_shape=[pltpu.VMEM(s, jnp.float32) for s in outs],
        in_specs=whole(len(args)),
        out_specs=whole(len(outs)),
        scratch_shapes=[pltpu.VMEM(s, jnp.float32) for s in scratch],
        compiler_params=pltpu.CompilerParams(vmem_limit_bytes=24 << 20),
        name=getattr(kernel, "func", kernel).__name__,
    )(*args)


FULL, PART = REACH, REACH - 1
PLANES = 2 * FULL + 3 * PART


def band_kernel(rows, levels, *refs):
    sources, (first, second), copies, sems = refs[:8], refs[8:10], refs[10:18], refs[18]
    pairs = [(sources[0], copies[0]), (sources[3], copies[3])]
    pairs += [(sources[2].at[k], copies[2].at[k]) for k in (1, 0, 2)]
    pairs += [(sources[k], copies[k]) for k in (1, 6, 4, 5, 7)]
    moves = [pltpu.make_async_copy(x, y, sems.at[k]) for k, (x, y) in enumerate(pairs)]
    for move in moves:
        move.start()
    noise, kappa2, conduct, land = copies[:4]
    columns = noise.shape[1]
    odd = lax.axis_index("lat") % 2
    lane = lax.broadcasted_iota(jnp.int32, (1, columns), 1)
    level = lax.broadcasted_iota(jnp.int32, (levels, 1), 0)
    plane = lambda lat: pl.ds(lat, levels, stride=rows)
    sides = ((first, odd), (second, 1 - odd))
    moves[0].wait()
    for out, side in sides:
        for j in range(FULL):
            out[j] = noise[plane((1 - side) * (rows - FULL) + j), :]
    moves[1].wait()
    moves[2].wait()
    oceans, totals = [], []
    for out, side in sides:
        base = (1 - side) * (rows - FULL)
        ocean = [land[plane(base + j), :].astype(jnp.float32) for j in range(FULL)]
        north = [conduct[1, plane(base + j), :] for j in range(FULL)]
        for j in range(PART):
            out[FULL + 3 * PART + j] = north[j] * ocean[j] * ocean[j + 1]
        out[FULL + 4 * PART] = north[PART]
        near = lambda x, j: jnp.where(side == 0, x[j + 1], x[j])
        below = [north[0]] + [near([north[j - 1], north[j]], 0) for j in range(1, PART)]
        below[0] = jnp.where(side == 0, north[0], 0.0)
        oceans.append([near(ocean, j) for j in range(PART)])
        totals.append([near(north, j) + below[j] for j in range(PART)])
    at = lambda side, j: plane((1 - side) * (rows - PART) + j)
    moves[3].wait()
    for (out, side), ocean, total in zip(sides, oceans, totals):
        for j in range(PART):
            e, o = conduct[0, at(side, j), :], ocean[j]
            ocean_east = jnp.where(lane == columns - 1, 1.0, pltpu.roll(o, columns - 1, 1))
            out[FULL + PART + j] = e * o * ocean_east
            total[j] = total[j] + (e + jnp.where(lane == 0, 0.0, pltpu.roll(e, 1, 1)))
    moves[4].wait()
    for (out, side), ocean, total in zip(sides, oceans, totals):
        for j in range(PART):
            u, o = jnp.where(level == levels - 1, 0.0, conduct[2, at(side, j), :]), ocean[j]
            out[FULL + 2 * PART + j] = u * o * pltpu.roll(o, levels - 1, 0)
            total[j] = total[j] + (u + pltpu.roll(u, 1, 0))
    moves[5].wait()
    for (out, side), ocean, total in zip(sides, oceans, totals):
        for j in range(PART):
            out[FULL + j] = ocean[j] * (kappa2[at(side, j), :] + total[j])
    for move in moves[6:]:
        move.wait()


def turned(planes, rows_of_planes):
    blocks = [jnp.concatenate(planes[j : j + REACH], axis=0) for j in range(0, rows_of_planes, REACH)]
    return jnp.concatenate([b.T for b in blocks], axis=1)


def coefficients(levels, band, kappa, east, north, upper, ocean):
    columns, lanes = kappa.shape
    lane = lax.broadcasted_iota(jnp.int32, (1, lanes), 1)
    row = lax.broadcasted_iota(jnp.int32, (columns, 1), 0)
    upper = jnp.where(lane % levels == levels - 1, 0.0, upper)
    south = jnp.where(lane % band < levels, 0.0, lane_roll(north, levels))
    west = jnp.where(row == 0, 0.0, pltpu.roll(east, 1, 0))
    ocean_east = jnp.where(row == columns - 1, 1.0, pltpu.roll(ocean, columns - 1, 0))
    diagonal = ocean * (kappa + east + west + north + south + upper + lane_roll(upper, 1))
    return diagonal, east * ocean * ocean_east, upper * ocean * lane_roll(ocean, -1)


def field_kernel(rows, levels, noise, weights, field, sums):
    r = turned([noise[pl.ds(j, levels, stride=rows), :] for j in range(rows)], rows)
    field[...] = r
    sums[...] = dot(weights[...], r)


def own_kernel(
    rows, levels, columns,
    kappa2, conduct, land, field,
    statics, edge, to_first, to_second,
):
    last_band = lax.axis_index("lat") == lax.axis_size("lat") - 1
    lon_odd = lax.axis_index("lon") % 2
    lanes = rows * levels

    def own(load):
        return turned([load(pl.ds(j, levels, stride=rows)) for j in range(rows)], rows)

    ocean = own(lambda at: land[at, :].astype(jnp.float32))
    north = own(lambda at: conduct[1, at, :])
    kappa = own(lambda at: kappa2[at, :])
    east = own(lambda at: conduct[0, at, :])
    upper = own(lambda at: conduct[2, at, :])
    lane = lax.broadcasted_iota(jnp.int32, (1, lanes), 1)
    north = jnp.where(last_band & (lane >= lanes - levels), 0.0, north)
    diagonal, to_east, to_upper = coefficients(levels, lanes, kappa, east, north, upper, ocean)
    for k, x in enumerate((diagonal, to_east, north, to_upper, ocean)):
        statics[k] = x
    end = columns - 1
    edge[...] = jnp.concatenate([east[end:], jnp.zeros((7, lanes), jnp.float32)], axis=0)
    blank = jnp.zeros((1, lanes), jnp.float32)
    for_east = [field[end:], diagonal[end:], to_east[end - 1 : end], east[end:], ocean[end:], north[end:], to_upper[end:], blank]
    for_west = [field[:1], diagonal[:1], to_east[:1], east[:1], ocean[:1], north[:1], to_upper[:1], blank]
    for_east = jnp.concatenate(for_east, axis=0)
    for_west = jnp.concatenate(for_west, axis=0)
    to_first[...] = jnp.where(lon_odd == 0, for_east, for_west)
    to_second[...] = jnp.where(lon_odd == 0, for_west, for_east)


MOMENTS, LIST = 4, 11


def list_kernel(moments, edges, out):
    out[...] = jnp.concatenate([moments[0:MOMENTS], edges[...], jnp.zeros((4, edges.shape[1]), jnp.float32)], axis=0)


def ghost_kernel(levels, columns, got_first, got_second, near, made, own, spread, ghosts, patches):
    lat_odd = lax.axis_index("lat") % 2
    group = REACH * levels

    def ghost(k, count, north):
        a = got_first[pl.ds(k, count)].reshape(count * levels, columns)
        b = jnp.where(inner_band(), got_second[pl.ds(k, count)], 0.0).reshape(count * levels, columns)
        from_first = (lat_odd == 0) if north else (lat_odd == 1)
        planes = jnp.where(from_first, a, b)
        if count == REACH:
            return planes.T
        blank = jnp.zeros((group - count * levels, columns), jnp.float32)
        return jnp.concatenate([planes, blank] if north else [blank, planes], axis=0).T

    pieces = ((0, FULL), (FULL, PART), (FULL + PART, PART), (FULL + 2 * PART, PART), (FULL + 3 * PART, FULL))
    r, diagonal, to_east, to_upper, north = (
        jnp.concatenate([ghost(k, count, False), ghost(k, count, True)], axis=1) for k, count in pieces
    )
    spread[...] = dot(near[...], r)
    ocean = jnp.where(diagonal > 0.0, 1.0, 0.0)
    last = made.shape[2] - group
    low, high = slice(0, group), slice(group, 2 * group)
    lane = lax.broadcasted_iota(jnp.int32, (1, group), 1)
    first_one, last_one = lane < levels, lane >= group - levels
    up = lambda x: pltpu.roll(x, levels, 1)
    down = lambda x: pltpu.roll(x, group - levels, 1)
    own_low, own_high = pl.ds(0, group), pl.ds(last, group)
    ocean_low, ocean_high = made[4, :, own_low], made[4, :, own_high]
    north_high = own[3, :, own_high]
    north_high = jnp.where(last_one, north_high * down(ocean[:, high]), north_high)
    ghost_low = north[:, low]
    ghost_low = jnp.where(last_one, ghost_low * ocean[:, low] * down(ocean_low), ghost_low)
    ghost_high = north[:, high]
    patches[0] = own[0, :, own_low] + jnp.where(first_one, ocean_low * up(north[:, low]), 0.0)
    patches[1] = jnp.where(first_one, up(ghost_low), own[4, :, own_low])
    patches[2] = north_high
    row = lax.broadcasted_iota(jnp.int32, (columns, 1), 0)
    for part, n, below in ((low, ghost_low, ghost_low), (high, ghost_high, north_high)):
        d, e, u, o = (x[:, part] for x in (diagonal, to_east, to_upper, ocean))
        if part is high:
            d = d + jnp.where(first_one, o * up(made[2, :, own_high]), 0.0)
        w = jnp.where(row == 0, 0.0, pltpu.roll(e, 1, 0))
        for k, x in enumerate((d, e, w, n, jnp.where(first_one, up(below), up(n)), u, pltpu.roll(u, 1, 1), o)):
            ghosts[k, :, part] = x


def coefficient(statics, k, at):
    own, ghosts, patches = statics
    group = ghosts.shape[2] // 2
    tile = pl.ds(at, TILE)
    x = own[k, tile]
    parts = [x[:, j : j + group] for j in range(0, x.shape[1], group)]
    if k in (0, 4):
        parts[0] = patches[0 if k == 0 else 1, tile]
    if k == 3:
        parts[-1] = patches[2, tile]
    g = ghosts[k, tile]
    return jnp.concatenate([g[:, :group]] + parts + [g[:, group:]], axis=1)


def forward_kernel(group, *refs):
    (one, two, edge), more, (first, second) = refs[1:4], refs[4:-2], refs[-2:]
    odd = lax.axis_index("lat") % 2
    whole_rows = [one[0:LIST], two[0:LIST], edge[0:2]] + [x[...] for x in more]
    x = jnp.concatenate(whole_rows, axis=0)
    low, high = x[:, 0:group], x[:, x.shape[1] - group :]
    first[...] = jnp.where(odd == 0, high, low)
    second[...] = jnp.where(odd == 0, low, high)


def joint_moments(left, right, rho, width):
    c = rho**width
    return jnp.concatenate(
        [
            left[0:1] + c * right[0:1],
            left[1:2] + c * (right[1:2] + width * right[0:1]),
            right[2:3] + c * left[2:3],
            right[3:4] + c * (left[3:4] + width * left[2:3]),
        ],
        axis=0,
    )


def chip_kernel(rho, columns, own, edges, got, out):
    even = lax.axis_index("lon") % 2 == 0
    mine, its = own[0:MOMENTS], got[0:MOMENTS]
    m = joint_moments(jnp.where(even, mine, its), jnp.where(even, its, mine), rho, columns)
    blank = jnp.zeros((out.shape[0] - MOMENTS - edges.shape[0], m.shape[1]), jnp.float32)
    out[...] = jnp.concatenate([m, edges[...], blank], axis=0)


def again_kernel(rho, columns, own, got, out):
    even = lax.axis_index("lon") % 2 == 0
    mine, its = own[0:MOMENTS], got[0:MOMENTS]
    out[...] = own[...]
    out[0:MOMENTS] = joint_moments(jnp.where(even, mine, its), jnp.where(even, its, mine), rho, columns)


def quad_kernel(rho, columns, mine, got, out):
    even = lax.axis_index("lon") % 2 == 0
    a, b = mine[0:4], got[0:4]
    m = joint_moments(jnp.where(even, b, a), jnp.where(even, a, b), rho, 2 * columns)
    out[...] = jnp.concatenate([m, jnp.zeros_like(m)], axis=0)


def near_kernel(levels, near, field, made, spread, statics):
    spread[...] = dot(near[...], field[...])
    columns = field.shape[0]
    lanes = field.shape[1]
    lane = lax.broadcasted_iota(jnp.int32, (1, lanes), 1)
    row = lax.broadcasted_iota(jnp.int32, (TILE, 1), 0)
    for at in range(0, columns, TILE):
        tile = pl.ds(at, TILE)
        d, e, n, u, o = (made[k, tile] for k in range(5))
        w = pltpu.roll(e, 1, 0)
        w = jnp.where(row == 0, carried, w) if at else w
        carried = e[TILE - 1 :]
        n = n * o * jnp.where(lane >= lanes - levels, 1.0, lane_roll(o, -levels))
        for k, x in enumerate((d, e, w, n, lane_roll(n, levels), u, lane_roll(u, 1), o)):
            statics[k, tile] = x


def told(far, lists):
    x = jnp.concatenate([t[0:8] for t in lists], axis=0)
    if x.shape[0] % 16:
        x = jnp.concatenate([x, jnp.zeros((8, x.shape[1]), jnp.float32)], axis=0)
    high, middle, low = thirds(x, lambda p: p.astype(jnp.float32))
    stacked = jnp.concatenate([high, middle, high, low, middle, high], axis=0)
    return jnp.dot(far[lax.axis_index("lon") % 2], stacked, preferred_element_type=jnp.float32)


def faces(v, n, s, u, low, levels):
    return n * lane_roll(v, -levels) + s * lane_roll(v, levels) + u * lane_roll(v, -1) + low * lane_roll(v, 1)


def shifts(v, at, kept):
    def turned_rows(i):
        if i not in kept:
            x = v[pl.ds(i, TILE)]
            kept[i] = x, pltpu.roll(x, TILE - 1, 0), pltpu.roll(x, 1, 0)
        return kept[i]

    i = at + EDGE
    row = lax.broadcasted_iota(jnp.int32, (TILE, 1), 0)
    x, east_v, west_v = turned_rows(i)
    east_v = jnp.where(row == TILE - 1, turned_rows(i + TILE)[1], east_v)
    west_v = jnp.where(row == 0, turned_rows(i - TILE)[2], west_v)
    return x, east_v, west_v


def apply_tile(levels, v, statics, ends, at, kept):
    own = statics[0]
    if at == 0:
        faces_of = lambda k: ends[k, 0:TILE]
    elif at + TILE == own.shape[1]:
        faces_of = lambda k: ends[k, TILE : 2 * TILE]
    else:
        faces_of = lambda k: coefficient(statics, k, at)
    d, e, w, n, s, u, low = (faces_of(k) for k in range(7))
    here, east_v, west_v = shifts(v, at, kept)
    return here, d * here - e * east_v - w * west_v - faces(here, n, s, u, low, levels)


def apply_rim(levels, columns, v, f, rim):
    end = EDGE + columns
    pick = lambda a, b: jnp.concatenate([v[a : a + 1], v[b : b + 1], jnp.zeros((6, v.shape[1]), jnp.float32)], axis=0)
    here = pick(EDGE - 1, end)
    g = rim[0] * here - rim[1] * pick(EDGE, end + 1) - rim[2] * pick(EDGE - 2, end - 1)
    g = g - faces(here, rim[3], rim[4], rim[5], rim[6], levels)
    f[EDGE - 1 : EDGE] = g[0:1]
    f[end : end + 1] = g[1:2]


def joined(own, ghost):
    group = ghost.shape[1] // 2
    return jnp.concatenate([ghost[:, :group], own, ghost[:, group:]], axis=1)


def completed(levels, group, diagonal, north, ocean):
    lanes = ocean.shape[1]
    lane = lax.broadcasted_iota(jnp.int32, (1, lanes), 1)
    first_of_band = ((lane >= group) & (lane < group + levels)) | ((lane >= lanes - group) & (lane < lanes - group + levels))
    diagonal = diagonal + jnp.where(first_of_band, ocean * lane_roll(north, levels), 0.0)
    return diagonal, north * ocean * lane_roll(ocean, -levels)


def first_kernel(
    rows, levels, columns, others,
    own_spread, own_edge, ghost_spread, own_part, ghost_part, patches, far, weights, side_first, side_second, *rest,
):
    statics = own_part, ghost_part, patches
    received = rest[: 1 + others]
    v, image, ends, rim, to_first, to_second, f = rest[1 + others :]
    lat_odd = lax.axis_index("lat") % 2
    even = lax.axis_index("lon") % 2 == 0
    group = REACH * levels
    lanes = rows * levels + 2 * group
    a, b = side_first[...], jnp.where(inner_band(), side_second[...], 0.0)
    south, north = jnp.where(lat_odd == 1, a, b), jnp.where(lat_odd == 1, b, a)
    lists, k = [], 0
    for x in (received[0][0:LIST], received[1][0:LIST], own_edge[0:2], *[x[...] for x in received[2:]]):
        at = slice(k, k + x.shape[0])
        lists.append(jnp.concatenate([south[at], x, north[at]], axis=1))
        k += x.shape[0]
    last_face = lists.pop(2)[0:1]
    v[...] = joined(own_spread[...], ghost_spread[...]) + told(far, lists)

    one, two = lists[0], lists[1]
    east_list, west_list = jnp.where(even, one, two), jnp.where(even, two, one)
    end = columns - 1
    for k in range(7):
        ends[k, 0:TILE] = coefficient(statics, k, 0)
        ends[k, TILE : 2 * TILE] = coefficient(statics, k, columns - TILE)
    ocean = coefficient(statics, 7, 0)[0:1]
    face_west = west_list[7:8] * west_list[8:9] * ocean
    last_east = ends[1, 2 * TILE - 1 :] * east_list[8:9]
    ends[0, 0:1] = ends[0, 0:1] + ocean * west_list[7:8]
    ends[2, 0:1] = face_west
    ends[1, 2 * TILE - 1 : 2 * TILE] = last_east
    blank = jnp.zeros((6, lanes), jnp.float32)
    stack = lambda p, q: jnp.concatenate([p, q, blank], axis=0)
    rim_diagonal, rim_north = completed(
        levels, group,
        stack(west_list[5:6], east_list[5:6] + east_list[8:9] * last_face),
        stack(west_list[9:10], east_list[9:10]),
        stack(west_list[8:9], east_list[8:9]),
    )
    rim_upper = stack(west_list[10:11], east_list[10:11])
    rim[0] = rim_diagonal
    rim[1] = stack(face_west, east_list[6:7])
    rim[2] = stack(west_list[6:7], last_east)
    rim[3] = rim_north
    rim[4] = lane_roll(rim_north, levels)
    rim[5] = rim_upper
    rim[6] = lane_roll(rim_upper, 1)

    kept = {}
    for at in range(0, columns, TILE):
        f[pl.ds(EDGE + at, TILE)] = apply_tile(levels, v, statics, ends, at, kept)[1]
    apply_rim(levels, columns, v, f, rim)
    m, kept = [0.0] * 4, {}
    for at in range(0, columns, TILE):
        tile = pl.ds(at, TILE)
        second = apply_tile(levels, f, statics, ends, at, kept)[1]
        w = jnp.where(coefficient(statics, 7, at) > 0.5, second, v[pl.ds(EDGE + at, TILE)])
        image[tile] = w
        for k in range(4):
            spread = weights[k, tile]
            m[k] = m[k] + w * jnp.concatenate([spread] * (lanes // 128), axis=1)
    m = [jnp.sum(x, axis=0, keepdims=True) * SCALE for x in m]
    pad = jnp.zeros((3, lanes), jnp.float32)
    for_east = jnp.concatenate(m + [image[end:] * SCALE, pad], axis=0)
    for_west = jnp.concatenate(m + [image[:1] * SCALE, pad], axis=0)
    to_first[...] = jnp.where(even, for_east, for_west)
    to_second[...] = jnp.where(even, for_west, for_east)


def lane_sums(tiles):
    total = functools.reduce(lambda a, b: a + b, tiles)
    s = jnp.sum(total, axis=0, keepdims=True)
    return functools.reduce(lambda a, b: a + b, [s[:, k : k + 128] for k in range(0, s.shape[1], 128)])


def own_lanes(rows, levels):
    return slice(REACH * levels, (REACH + rows) * levels)


def between_kernel(rows, levels, columns, near, field, precond, image, spread, sums):
    own = own_lanes(rows, levels)
    spread[...] = dot(near[...], image[...] * SCALE)
    energy, curve = [], []
    for at in range(0, columns, TILE):
        tile = pl.ds(at, TILE)
        p = precond[pl.ds(EDGE + at, TILE), own]
        energy.append(field[tile] * p)
        curve.append(p * image[tile, own])
    sums[...] = jnp.concatenate([lane_sums(energy), lane_sums(curve), jnp.zeros((6, 128), jnp.float32)], axis=0)


def second_kernel(
    levels, columns, rows, others, spread, early, image, own_part, ghost_part, patches, ends, far, rim, *rest
):
    statics = own_part, ghost_part, patches
    received = rest[: 1 + others]
    v, f, sums = rest[1 + others :]
    v[...] = spread[...] + told(far, received)
    own = own_lanes(rows, levels)
    mixed, last, kept = [], [], {}
    for at in range(0, columns, TILE):
        tile = pl.ds(at, TILE)
        q, b = apply_tile(levels, v, statics, ends, at, kept)
        f[pl.ds(EDGE + at, TILE)] = b
        q, b, ocean = q[:, own], b[:, own], own_part[7, tile]
        mixed.append(image[tile, own] * q)
        still = jnp.where(ocean > 0.5, b, q)
        last.append(still * still)
    apply_rim(levels, columns, v, f, rim)
    sums[...] = jnp.concatenate([early[0:2], lane_sums(mixed), lane_sums(last), early[4:8]], axis=0)


def turn_kernel(rows, levels, columns, precond, image, again, f, own_part, ghost_part, patches, ends, *outs):
    statics = own_part, ghost_part, patches
    z = outs[4]
    own = own_lanes(rows, levels)
    kept = {}
    for at in range(0, columns, TILE):
        second = apply_tile(levels, f, statics, ends, at, kept)[1]
        tile = pl.ds(at, TILE)
        z[tile] = jnp.where(coefficient(statics, 7, at) > 0.5, second, again[pl.ds(EDGE + at, TILE)])
    group = REACH * levels
    slab = pl.ds(EDGE, columns)
    for j in range(0, rows, REACH):
        at = slice(own.start + j * levels, own.start + j * levels + group)
        for out, x in zip(outs, (precond[slab, at], image[:, at], again[slab, at], z[:, at])):
            t = x.T
            for i in range(REACH):
                out[pl.ds(j + i, levels, stride=rows), :] = t[i * levels : (i + 1) * levels]


PIECES = 4


def combine_kernel(sums, noise, precond, image, again, along, answer, left, x, y, sems):
    total = jnp.sum(sums[...], axis=1, keepdims=True)
    energy, curve, mixed, last = total[0:1], total[1:2], total[2:3], total[3:4]
    alpha = energy / curve
    beta = alpha / SCALE
    growth = alpha * beta * mixed / energy
    step = energy * (growth - 1.0) / (beta * beta * last - growth * growth * curve)
    keep = alpha + step * growth
    back = step * beta
    size = noise.shape[0] // PIECES
    moves = []
    for k in range(PIECES):
        part = pl.ds(k * size, size)
        x[part] = keep * precond[part] - back * again[part]
        moves.append(pltpu.make_async_copy(x.at[part], answer.at[part], sems.at[0, k]))
        moves[-1].start()
        y[part] = noise[part] - (keep * image[part] - back * along[part])
        moves.append(pltpu.make_async_copy(y.at[part], left.at[part], sems.at[1, k]))
        moves[-1].start()
    for move in moves:
        move.wait()


def doubling(count):
    steps = []
    while 2 ** len(steps) < count:
        steps.append(2 ** len(steps))
    return steps


def summed(x):
    count, bands = lax.axis_size("lon"), lax.axis_size("lat")
    x = x + lax.ppermute(x, "lon", [(i, i ^ 1) for i in range(count)])
    for step in doubling(bands)[::-1]:
        pairs = [(i * bands + j, (i ^ 1) * bands + (j ^ step)) for i in range(count) for j in range(bands)]
        x = x + lax.ppermute(x, ("lon", "lat"), pairs)
    for step in doubling(count)[1:]:
        x = x + lax.ppermute(x, "lon", [(i, i ^ step ^ 1) for i in range(count)])
    return x


def body(near, far, weights, columns_of, noise, kappa2, conduct, land):
    levels, rows, columns = noise.shape
    count = lax.axis_size("lon")
    others = count // 4
    flat = levels * rows
    group = REACH * levels
    lanes = flat + 2 * group
    tall = columns + 2 * EDGE
    rho = circle_kernel(count * columns)[0]
    noise = noise.reshape(flat, columns)
    kappa2 = kappa2.reshape(flat, columns)
    land = land.reshape(flat, columns)
    conduct = conduct.reshape(3, flat, columns)

    sources = (noise, kappa2, conduct, land, near, far, weights, columns_of)
    planes = (PLANES, levels, columns)
    first, second, noise, kappa2, conduct, land, near, far, weights, columns_of = pl.pallas_call(
        functools.partial(band_kernel, rows, levels),
        out_shape=[pltpu.VMEM(planes, jnp.float32)] * 2 + [pltpu.VMEM(x.shape, x.dtype) for x in sources],
        in_specs=[pl.BlockSpec(memory_space=pltpu.HBM)] * len(sources),
        out_specs=whole(2 + len(sources)),
        scratch_shapes=[pltpu.SemaphoreType.DMA((len(sources) + 2,))],
        compiler_params=pltpu.CompilerParams(vmem_limit_bytes=8 << 20),
        name="band_kernel",
    )(*[pltpu.with_memory_space_constraint(x, pltpu.HBM) for x in sources])
    lat_a, lat_b = lat_perms(count, lax.axis_size("lat"))
    to_band = lambda x, pairs: lax.ppermute(x, ("lon", "lat"), pairs)
    got_second, got_first = to_band(second, lat_b), to_band(first, lat_a)

    own_field, mine = call(
        functools.partial(field_kernel, rows, levels), [(columns, flat), (8, flat)], noise, weights
    )
    made, own_edge, to_first, to_second = call(
        functools.partial(own_kernel, rows, levels, columns),
        [(5, columns, flat), (8, flat), (8, flat), (8, flat)],
        kappa2, conduct, land, own_field,
    )
    lon_a, lon_b = lon_perms(count)

    def farther(two, got_two):
        if count == 4:
            return []
        (four,) = call(functools.partial(quad_kernel, rho, columns), [(8, two.shape[1])], two, got_two)
        return [lax.ppermute(four, "lon", [(i, (i + d) % count) for i in range(count)]) for d in range(4, count, 4)]

    got = lax.ppermute(mine, "lon", lon_a)
    (two,) = call(functools.partial(chip_kernel, rho, columns), [(16, flat)], mine, to_second, got)
    got_two = lax.ppermute(two, "lon", lon_b)
    (got_one,) = call(list_kernel, [(16, flat)], got, lax.ppermute(to_first, "lon", lon_a))
    lists = [got_one, got_two] + farther(two, got_two)
    own_spread, own_part = call(
        functools.partial(near_kernel, levels), [(tall, flat), (8, columns, flat)], near, own_field, made
    )
    sent = (*lists[:2], own_edge, *lists[2:])
    heights = 2 * LIST + 2 + sum(x.shape[0] for x in lists[2:])
    side_first, side_second = call(functools.partial(forward_kernel, group), [(heights, group)] * 2, own_spread, *sent)
    side_second, side_first = to_band(side_second, lat_b), to_band(side_first, lat_a)
    ghost_spread, ghost_part, patches = call(
        functools.partial(ghost_kernel, levels, columns),
        [(tall, 2 * group), (8, columns, 2 * group), (3, columns, group)],
        got_first, got_second, near, made, own_part,
    )
    precond, image, ends, rim, to_first, to_second = call(
        functools.partial(first_kernel, rows, levels, columns, others),
        [(tall, lanes), (columns, lanes), (7, 2 * TILE, lanes), (7, 8, lanes), (8, lanes), (8, lanes)],
        own_spread, own_edge, ghost_spread, own_part, ghost_part, patches, far, columns_of, side_first, side_second, *lists,
        scratch=[(tall, lanes)],
    )
    got_one = lax.ppermute(to_first, "lon", lon_a)
    (two,) = call(functools.partial(again_kernel, rho, columns), [(8, lanes)], to_second, got_one)
    got_two = lax.ppermute(two, "lon", lon_b)
    lists = [got_one, got_two] + farther(two, got_two)
    spread, sums = call(
        functools.partial(between_kernel, rows, levels, columns),
        [(tall, lanes), (8, 128)],
        near, own_field, precond, image,
    )
    again, half, sums = call(
        functools.partial(second_kernel, levels, columns, rows, others),
        [(tall, lanes), (tall, lanes), (8, 128)],
        spread, sums, image, own_part, ghost_part, patches, ends, far, rim, *lists,
    )
    sums = summed(sums)
    turned_back = call(
        functools.partial(turn_kernel, rows, levels, columns),
        [(flat, columns)] * 4 + [(columns, lanes)],
        precond, image, again, half, own_part, ghost_part, patches, ends,
    )[:4]
    operands = [pltpu.with_memory_space_constraint(x, pltpu.VMEM) for x in (sums, noise, *turned_back)]
    answer, left = pl.pallas_call(
        combine_kernel,
        out_shape=[jax.ShapeDtypeStruct((flat, columns), jnp.float32)] * 2,
        in_specs=whole(len(operands)),
        out_specs=[pl.BlockSpec(memory_space=pltpu.HBM)] * 2,
        scratch_shapes=[pltpu.VMEM((flat, columns), jnp.float32)] * 2 + [pltpu.SemaphoreType.DMA((2, PIECES))],
        compiler_params=pltpu.CompilerParams(vmem_limit_bytes=8 << 20),
        name="combine_kernel",
    )(*operands)
    return answer.reshape(levels, rows, columns), left.reshape(levels, rows, columns)


def solution(mesh):
    def run(noise, kappa2, conduct, land):
        count = mesh.shape["lon"]
        matrices = circle_matrices(count, noise.shape[2] // count)
        return jax.shard_map(
            functools.partial(body, *matrices),
            mesh=mesh,
            in_specs=(
                P("ens", "lat", "lon"),
                P(None, "lat", "lon"),
                P(None, None, "lat", "lon"),
                P(None, "lat", "lon"),
            ),
            out_specs=(P("ens", "lat", "lon"), P("ens", "lat", "lon")),
            check_vma=False,
        )(noise, kappa2, conduct, land)

    return run
```

```python
import functools
import math

import jax
import jax.numpy as jnp
import numpy as np
from jax import lax
from jax.experimental import pallas as pl
from jax.experimental.pallas import tpu as pltpu
from jax.sharding import PartitionSpec as P

base_kappa = 0.001
base_conduct = 1.0

SCALE = 2.0**-31
REACH = 4
TILE = 8
EDGE = 8

HIGHEST = lax.Precision.HIGHEST


def dot(a, b):
    return jnp.dot(a, b, precision=HIGHEST, preferred_element_type=jnp.float32)


def circle_kernel(total):
    middle = 2.0 + base_kappa / base_conduct
    rho = (middle - math.sqrt(middle * middle - 4.0)) / 2.0
    height = 1.0 / (1.0 / rho - rho) / base_conduct
    wrap = rho**total
    shift = (1.0 + rho * rho) / (1.0 - rho * rho) + total * wrap / (1.0 - wrap)
    front = height * height / (1.0 - wrap)
    return rho, front, shift


def circle_matrices(count, columns):
    total = count * columns
    rho, front, shift = circle_kernel(total)

    def one_side(n):
        return front * rho**n * (n + shift)

    def both_sides(n):
        return one_side(n) + one_side(total - n)

    place = np.arange(columns)
    rows = columns + 2 * EDGE
    x = np.arange(rows) - EDGE
    used = (x >= -2) & (x < columns + 2)
    near = both_sides(np.abs(x[:, None] - place[None, :])) * used[:, None]
    back = columns - 1 - place
    moments = np.zeros((8, columns))
    moments[0] = rho**place
    moments[1] = place * rho**place
    moments[2] = rho**back
    moments[3] = back * rho**back

    def block(start, size, neighbour):
        start = start % count * columns
        a = start - x
        b = total - start + x - (size * columns - 1)
        out = np.zeros((rows, 8))
        out[:, 0] = front * rho**a * (a + shift)
        out[:, 1] = front * rho**a
        out[:, 2] = front * rho**b * (b + shift)
        out[:, 3] = front * rho**b
        amend = both_sides(1) - both_sides(-1)
        if neighbour == "east":
            out[EDGE + columns + 1, 4] = amend
        if neighbour == "west":
            out[EDGE - 2, 4] = amend
        return out * used[:, None]

    fours = range(4, count, 4)
    even = [block(1, 1, "east"), block(-2, 2, "west")] + [block(-2 - d, 4, "") for d in fours]
    odd = [block(-1, 1, "west"), block(1, 2, "east")] + [block(-1 - d, 4, "") for d in fours]
    far = np.stack([np.concatenate(even, axis=1), np.concatenate(odd, axis=1)])
    far = np.pad(far, ((0, 0), (0, 0), (0, -far.shape[2] % 16))).astype(np.float32)
    high, middle, low = thirds(far, lambda x: x.astype(np.float32))
    far = np.concatenate([high, high, middle, high, middle, low], axis=2)
    columns_of = np.broadcast_to(moments[:4, :, None], (4, columns, 128))
    as_f32 = lambda m: np.asarray(m, np.float32)
    return as_f32(near), far, as_f32(moments), as_f32(columns_of)


def lon_perms(count):
    first = [(i, i ^ 1) for i in range(count)]
    return first, [(i, (i - 1 + 2 * (i % 2)) % count) for i in range(count)]


def lat_perms(count, bands):
    first, second = [], []
    for i in range(count):
        for j in range(bands):
            k = j - 1 + 2 * (j % 2)
            first.append((i * bands + j, i * bands + (j ^ 1)))
            second.append((i * bands + j, i * bands + k if 0 <= k < bands else (i ^ 1) * bands + j))
    return first, second


def inner_band():
    return (lax.axis_index("lat") > 0) & (lax.axis_index("lat") < lax.axis_size("lat") - 1)


def lane_roll(x, by):
    count = x.shape[1] // 128
    skip, by = divmod(by % x.shape[1], 128)
    parts = [x[:, k * 128 : (k + 1) * 128] for k in range(count)]
    if by:
        turned = [pltpu.roll(p, by, 1) for p in parts]
        lane = lax.broadcasted_iota(jnp.int32, (1, 128), 1)
        parts = [jnp.where(lane < by, turned[k - 1], turned[k]) for k in range(count)]
    return jnp.concatenate([parts[(k - skip) % count] for k in range(count)], axis=1)


def thirds(x, cast):
    high = x.astype(jnp.bfloat16)
    rest = x - cast(high)
    middle = rest.astype(jnp.bfloat16)
    return high, middle, (rest - cast(middle)).astype(jnp.bfloat16)


def whole(n):
    return [pl.BlockSpec(memory_space=pltpu.VMEM)] * n


def call(kernel, outs, *args, scratch=()):
    args = [pltpu.with_memory_space_constraint(a, pltpu.VMEM) for a in args]
    return pl.pallas_call(
        kernel,
        out_shape=[pltpu.VMEM(s, jnp.float32) for s in outs],
        in_specs=whole(len(args)),
        out_specs=whole(len(outs)),
        scratch_shapes=[pltpu.VMEM(s, jnp.float32) for s in scratch],
        compiler_params=pltpu.CompilerParams(vmem_limit_bytes=24 << 20),
        name=getattr(kernel, "func", kernel).__name__,
    )(*args)


FULL, PART = REACH, REACH - 1
PLANES = 2 * FULL + 3 * PART


def band_kernel(rows, levels, *refs):
    sources, (first, second), copies, sems = refs[:8], refs[8:10], refs[10:18], refs[18]
    pairs = [(sources[0], copies[0]), (sources[3], copies[3])]
    pairs += [(sources[2].at[k], copies[2].at[k]) for k in (1, 0, 2)]
    pairs += [(sources[k], copies[k]) for k in (1, 6, 4, 5, 7)]
    moves = [pltpu.make_async_copy(x, y, sems.at[k]) for k, (x, y) in enumerate(pairs)]
    for move in moves:
        move.start()
    noise, kappa2, conduct, land = copies[:4]
    columns = noise.shape[1]
    odd = lax.axis_index("lat") % 2
    lane = lax.broadcasted_iota(jnp.int32, (1, columns), 1)
    level = lax.broadcasted_iota(jnp.int32, (levels, 1), 0)
    plane = lambda lat: pl.ds(lat, levels, stride=rows)
    sides = ((first, odd), (second, 1 - odd))
    moves[0].wait()
    for out, side in sides:
        for j in range(FULL):
            out[j] = noise[plane((1 - side) * (rows - FULL) + j), :]
    moves[1].wait()
    moves[2].wait()
    oceans, totals = [], []
    for out, side in sides:
        base = (1 - side) * (rows - FULL)
        ocean = [land[plane(base + j), :].astype(jnp.float32) for j in range(FULL)]
        north = [conduct[1, plane(base + j), :] for j in range(FULL)]
        for j in range(PART):
            out[FULL + 3 * PART + j] = north[j] * ocean[j] * ocean[j + 1]
        out[FULL + 4 * PART] = north[PART]
        near = lambda x, j: jnp.where(side == 0, x[j + 1], x[j])
        below = [north[0]] + [near([north[j - 1], north[j]], 0) for j in range(1, PART)]
        below[0] = jnp.where(side == 0, north[0], 0.0)
        oceans.append([near(ocean, j) for j in range(PART)])
        totals.append([near(north, j) + below[j] for j in range(PART)])
    at = lambda side, j: plane((1 - side) * (rows - PART) + j)
    moves[3].wait()
    for (out, side), ocean, total in zip(sides, oceans, totals):
        for j in range(PART):
            e, o = conduct[0, at(side, j), :], ocean[j]
            ocean_east = jnp.where(lane == columns - 1, 1.0, pltpu.roll(o, columns - 1, 1))
            out[FULL + PART + j] = e * o * ocean_east
            total[j] = total[j] + (e + jnp.where(lane == 0, 0.0, pltpu.roll(e, 1, 1)))
    moves[4].wait()
    for (out, side), ocean, total in zip(sides, oceans, totals):
        for j in range(PART):
            u, o = jnp.where(level == levels - 1, 0.0, conduct[2, at(side, j), :]), ocean[j]
            out[FULL + 2 * PART + j] = u * o * pltpu.roll(o, levels - 1, 0)
            total[j] = total[j] + (u + pltpu.roll(u, 1, 0))
    moves[5].wait()
    for (out, side), ocean, total in zip(sides, oceans, totals):
        for j in range(PART):
            out[FULL + j] = ocean[j] * (kappa2[at(side, j), :] + total[j])
    for move in moves[6:]:
        move.wait()


def turned(planes, rows_of_planes):
    blocks = [jnp.concatenate(planes[j : j + REACH], axis=0) for j in range(0, rows_of_planes, REACH)]
    return jnp.concatenate([b.T for b in blocks], axis=1)


def coefficients(levels, band, kappa, east, north, upper, ocean):
    columns, lanes = kappa.shape
    lane = lax.broadcasted_iota(jnp.int32, (1, lanes), 1)
    row = lax.broadcasted_iota(jnp.int32, (columns, 1), 0)
    upper = jnp.where(lane % levels == levels - 1, 0.0, upper)
    south = jnp.where(lane % band < levels, 0.0, lane_roll(north, levels))
    west = jnp.where(row == 0, 0.0, pltpu.roll(east, 1, 0))
    ocean_east = jnp.where(row == columns - 1, 1.0, pltpu.roll(ocean, columns - 1, 0))
    diagonal = ocean * (kappa + east + west + north + south + upper + lane_roll(upper, 1))
    return diagonal, east * ocean * ocean_east, upper * ocean * lane_roll(ocean, -1)


def field_kernel(rows, levels, noise, weights, field, sums):
    r = turned([noise[pl.ds(j, levels, stride=rows), :] for j in range(rows)], rows)
    field[...] = r
    sums[...] = dot(weights[...], r)


def own_kernel(
    rows, levels, columns,
    kappa2, conduct, land, field,
    statics, edge, to_first, to_second,
):
    last_band = lax.axis_index("lat") == lax.axis_size("lat") - 1
    lon_odd = lax.axis_index("lon") % 2
    lanes = rows * levels

    def own(load):
        return turned([load(pl.ds(j, levels, stride=rows)) for j in range(rows)], rows)

    ocean = own(lambda at: land[at, :].astype(jnp.float32))
    north = own(lambda at: conduct[1, at, :])
    kappa = own(lambda at: kappa2[at, :])
    east = own(lambda at: conduct[0, at, :])
    upper = own(lambda at: conduct[2, at, :])
    lane = lax.broadcasted_iota(jnp.int32, (1, lanes), 1)
    north = jnp.where(last_band & (lane >= lanes - levels), 0.0, north)
    diagonal, to_east, to_upper = coefficients(levels, lanes, kappa, east, north, upper, ocean)
    for k, x in enumerate((diagonal, to_east, north, to_upper, ocean)):
        statics[k] = x
    end = columns - 1
    edge[...] = jnp.concatenate([east[end:], jnp.zeros((7, lanes), jnp.float32)], axis=0)
    blank = jnp.zeros((1, lanes), jnp.float32)
    for_east = [field[end:], diagonal[end:], to_east[end - 1 : end], east[end:], ocean[end:], north[end:], to_upper[end:], blank]
    for_west = [field[:1], diagonal[:1], to_east[:1], east[:1], ocean[:1], north[:1], to_upper[:1], blank]
    for_east = jnp.concatenate(for_east, axis=0)
    for_west = jnp.concatenate(for_west, axis=0)
    to_first[...] = jnp.where(lon_odd == 0, for_east, for_west)
    to_second[...] = jnp.where(lon_odd == 0, for_west, for_east)


MOMENTS, LIST = 4, 11


def list_kernel(moments, edges, out):
    out[...] = jnp.concatenate([moments[0:MOMENTS], edges[...], jnp.zeros((4, edges.shape[1]), jnp.float32)], axis=0)


def ghost_kernel(levels, columns, got_first, got_second, near, made, own, spread, ghosts, patches):
    lat_odd = lax.axis_index("lat") % 2
    group = REACH * levels

    def ghost(k, count, north):
        a = got_first[pl.ds(k, count)].reshape(count * levels, columns)
        b = jnp.where(inner_band(), got_second[pl.ds(k, count)], 0.0).reshape(count * levels, columns)
        from_first = (lat_odd == 0) if north else (lat_odd == 1)
        planes = jnp.where(from_first, a, b)
        if count == REACH:
            return planes.T
        blank = jnp.zeros((group - count * levels, columns), jnp.float32)
        return jnp.concatenate([planes, blank] if north else [blank, planes], axis=0).T

    pieces = ((0, FULL), (FULL, PART), (FULL + PART, PART), (FULL + 2 * PART, PART), (FULL + 3 * PART, FULL))
    r, diagonal, to_east, to_upper, north = (
        jnp.concatenate([ghost(k, count, False), ghost(k, count, True)], axis=1) for k, count in pieces
    )
    spread[...] = dot(near[...], r)
    ocean = jnp.where(diagonal > 0.0, 1.0, 0.0)
    last = made.shape[2] - group
    low, high = slice(0, group), slice(group, 2 * group)
    lane = lax.broadcasted_iota(jnp.int32, (1, group), 1)
    first_one, last_one = lane < levels, lane >= group - levels
    up = lambda x: pltpu.roll(x, levels, 1)
    down = lambda x: pltpu.roll(x, group - levels, 1)
    own_low, own_high = pl.ds(0, group), pl.ds(last, group)
    ocean_low, ocean_high = made[4, :, own_low], made[4, :, own_high]
    north_high = own[3, :, own_high]
    north_high = jnp.where(last_one, north_high * down(ocean[:, high]), north_high)
    ghost_low = north[:, low]
    ghost_low = jnp.where(last_one, ghost_low * ocean[:, low] * down(ocean_low), ghost_low)
    ghost_high = north[:, high]
    patches[0] = own[0, :, own_low] + jnp.where(first_one, ocean_low * up(north[:, low]), 0.0)
    patches[1] = jnp.where(first_one, up(ghost_low), own[4, :, own_low])
    patches[2] = north_high
    row = lax.broadcasted_iota(jnp.int32, (columns, 1), 0)
    for part, n, below in ((low, ghost_low, ghost_low), (high, ghost_high, north_high)):
        d, e, u, o = (x[:, part] for x in (diagonal, to_east, to_upper, ocean))
        if part is high:
            d = d + jnp.where(first_one, o * up(made[2, :, own_high]), 0.0)
        w = jnp.where(row == 0, 0.0, pltpu.roll(e, 1, 0))
        for k, x in enumerate((d, e, w, n, jnp.where(first_one, up(below), up(n)), u, pltpu.roll(u, 1, 1), o)):
            ghosts[k, :, part] = x


def coefficient(statics, k, at):
    own, ghosts, patches = statics
    group = ghosts.shape[2] // 2
    tile = pl.ds(at, TILE)
    x = own[k, tile]
    parts = [x[:, j : j + group] for j in range(0, x.shape[1], group)]
    if k in (0, 4):
        parts[0] = patches[0 if k == 0 else 1, tile]
    if k == 3:
        parts[-1] = patches[2, tile]
    g = ghosts[k, tile]
    return jnp.concatenate([g[:, :group]] + parts + [g[:, group:]], axis=1)


def forward_kernel(group, *refs):
    (one, two, edge), more, (first, second) = refs[1:4], refs[4:-2], refs[-2:]
    odd = lax.axis_index("lat") % 2
    whole_rows = [one[0:LIST], two[0:LIST], edge[0:2]] + [x[...] for x in more]
    x = jnp.concatenate(whole_rows, axis=0)
    low, high = x[:, 0:group], x[:, x.shape[1] - group :]
    first[...] = jnp.where(odd == 0, high, low)
    second[...] = jnp.where(odd == 0, low, high)


def joint_moments(left, right, rho, width):
    c = rho**width
    return jnp.concatenate(
        [
            left[0:1] + c * right[0:1],
            left[1:2] + c * (right[1:2] + width * right[0:1]),
            right[2:3] + c * left[2:3],
            right[3:4] + c * (left[3:4] + width * left[2:3]),
        ],
        axis=0,
    )


def chip_kernel(rho, columns, own, edges, got, out):
    even = lax.axis_index("lon") % 2 == 0
    mine, its = own[0:MOMENTS], got[0:MOMENTS]
    m = joint_moments(jnp.where(even, mine, its), jnp.where(even, its, mine), rho, columns)
    blank = jnp.zeros((out.shape[0] - MOMENTS - edges.shape[0], m.shape[1]), jnp.float32)
    out[...] = jnp.concatenate([m, edges[...], blank], axis=0)


def again_kernel(rho, columns, own, got, out):
    even = lax.axis_index("lon") % 2 == 0
    mine, its = own[0:MOMENTS], got[0:MOMENTS]
    out[...] = own[...]
    out[0:MOMENTS] = joint_moments(jnp.where(even, mine, its), jnp.where(even, its, mine), rho, columns)


def quad_kernel(rho, columns, mine, got, out):
    even = lax.axis_index("lon") % 2 == 0
    a, b = mine[0:4], got[0:4]
    m = joint_moments(jnp.where(even, b, a), jnp.where(even, a, b), rho, 2 * columns)
    out[...] = jnp.concatenate([m, jnp.zeros_like(m)], axis=0)


def near_kernel(levels, near, field, made, spread, statics):
    spread[...] = dot(near[...], field[...])
    columns = field.shape[0]
    lanes = field.shape[1]
    lane = lax.broadcasted_iota(jnp.int32, (1, lanes), 1)
    row = lax.broadcasted_iota(jnp.int32, (TILE, 1), 0)
    for at in range(0, columns, TILE):
        tile = pl.ds(at, TILE)
        d, e, n, u, o = (made[k, tile] for k in range(5))
        w = pltpu.roll(e, 1, 0)
        w = jnp.where(row == 0, carried, w) if at else w
        carried = e[TILE - 1 :]
        n = n * o * jnp.where(lane >= lanes - levels, 1.0, lane_roll(o, -levels))
        for k, x in enumerate((d, e, w, n, lane_roll(n, levels), u, lane_roll(u, 1), o)):
            statics[k, tile] = x


def told(far, lists):
    x = jnp.concatenate([t[0:8] for t in lists], axis=0)
    if x.shape[0] % 16:
        x = jnp.concatenate([x, jnp.zeros((8, x.shape[1]), jnp.float32)], axis=0)
    high, middle, low = thirds(x, lambda p: p.astype(jnp.float32))
    stacked = jnp.concatenate([high, middle, high, low, middle, high], axis=0)
    return jnp.dot(far[lax.axis_index("lon") % 2], stacked, preferred_element_type=jnp.float32)


def faces(v, n, s, u, low, levels):
    return n * lane_roll(v, -levels) + s * lane_roll(v, levels) + u * lane_roll(v, -1) + low * lane_roll(v, 1)


def shifts(v, at, kept):
    def turned_rows(i):
        if i not in kept:
            x = v[pl.ds(i, TILE)]
            kept[i] = x, pltpu.roll(x, TILE - 1, 0), pltpu.roll(x, 1, 0)
        return kept[i]

    i = at + EDGE
    row = lax.broadcasted_iota(jnp.int32, (TILE, 1), 0)
    x, east_v, west_v = turned_rows(i)
    east_v = jnp.where(row == TILE - 1, turned_rows(i + TILE)[1], east_v)
    west_v = jnp.where(row == 0, turned_rows(i - TILE)[2], west_v)
    return x, east_v, west_v


def apply_tile(levels, v, statics, ends, at, kept):
    own = statics[0]
    if at == 0:
        faces_of = lambda k: ends[k, 0:TILE]
    elif at + TILE == own.shape[1]:
        faces_of = lambda k: ends[k, TILE : 2 * TILE]
    else:
        faces_of = lambda k: coefficient(statics, k, at)
    d, e, w, n, s, u, low = (faces_of(k) for k in range(7))
    here, east_v, west_v = shifts(v, at, kept)
    return here, d * here - e * east_v - w * west_v - faces(here, n, s, u, low, levels)


def apply_rim(levels, columns, v, f, rim):
    end = EDGE + columns
    pick = lambda a, b: jnp.concatenate([v[a : a + 1], v[b : b + 1], jnp.zeros((6, v.shape[1]), jnp.float32)], axis=0)
    here = pick(EDGE - 1, end)
    g = rim[0] * here - rim[1] * pick(EDGE, end + 1) - rim[2] * pick(EDGE - 2, end - 1)
    g = g - faces(here, rim[3], rim[4], rim[5], rim[6], levels)
    f[EDGE - 1 : EDGE] = g[0:1]
    f[end : end + 1] = g[1:2]


def joined(own, ghost):
    group = ghost.shape[1] // 2
    return jnp.concatenate([ghost[:, :group], own, ghost[:, group:]], axis=1)


def completed(levels, group, diagonal, north, ocean):
    lanes = ocean.shape[1]
    lane = lax.broadcasted_iota(jnp.int32, (1, lanes), 1)
    first_of_band = ((lane >= group) & (lane < group + levels)) | ((lane >= lanes - group) & (lane < lanes - group + levels))
    diagonal = diagonal + jnp.where(first_of_band, ocean * lane_roll(north, levels), 0.0)
    return diagonal, north * ocean * lane_roll(ocean, -levels)


def first_kernel(
    rows, levels, columns, others,
    own_spread, own_edge, ghost_spread, own_part, ghost_part, patches, far, weights, side_first, side_second, *rest,
):
    statics = own_part, ghost_part, patches
    received = rest[: 1 + others]
    v, image, ends, rim, to_first, to_second, f = rest[1 + others :]
    lat_odd = lax.axis_index("lat") % 2
    even = lax.axis_index("lon") % 2 == 0
    group = REACH * levels
    lanes = rows * levels + 2 * group
    a, b = side_first[...], jnp.where(inner_band(), side_second[...], 0.0)
    south, north = jnp.where(lat_odd == 1, a, b), jnp.where(lat_odd == 1, b, a)
    lists, k = [], 0
    for x in (received[0][0:LIST], received[1][0:LIST], own_edge[0:2], *[x[...] for x in received[2:]]):
        at = slice(k, k + x.shape[0])
        lists.append(jnp.concatenate([south[at], x, north[at]], axis=1))
        k += x.shape[0]
    last_face = lists.pop(2)[0:1]
    v[...] = joined(own_spread[...], ghost_spread[...]) + told(far, lists)

    one, two = lists[0], lists[1]
    east_list, west_list = jnp.where(even, one, two), jnp.where(even, two, one)
    end = columns - 1
    for k in range(7):
        ends[k, 0:TILE] = coefficient(statics, k, 0)
        ends[k, TILE : 2 * TILE] = coefficient(statics, k, columns - TILE)
    ocean = coefficient(statics, 7, 0)[0:1]
    face_west = west_list[7:8] * west_list[8:9] * ocean
    last_east = ends[1, 2 * TILE - 1 :] * east_list[8:9]
    ends[0, 0:1] = ends[0, 0:1] + ocean * west_list[7:8]
    ends[2, 0:1] = face_west
    ends[1, 2 * TILE - 1 : 2 * TILE] = last_east
    blank = jnp.zeros((6, lanes), jnp.float32)
    stack = lambda p, q: jnp.concatenate([p, q, blank], axis=0)
    rim_diagonal, rim_north = completed(
        levels, group,
        stack(west_list[5:6], east_list[5:6] + east_list[8:9] * last_face),
        stack(west_list[9:10], east_list[9:10]),
        stack(west_list[8:9], east_list[8:9]),
    )
    rim_upper = stack(west_list[10:11], east_list[10:11])
    rim[0] = rim_diagonal
    rim[1] = stack(face_west, east_list[6:7])
    rim[2] = stack(west_list[6:7], last_east)
    rim[3] = rim_north
    rim[4] = lane_roll(rim_north, levels)
    rim[5] = rim_upper
    rim[6] = lane_roll(rim_upper, 1)

    kept = {}
    for at in range(0, columns, TILE):
        f[pl.ds(EDGE + at, TILE)] = apply_tile(levels, v, statics, ends, at, kept)[1]
    apply_rim(levels, columns, v, f, rim)
    m, kept = [0.0] * 4, {}
    for at in range(0, columns, TILE):
        tile = pl.ds(at, TILE)
        second = apply_tile(levels, f, statics, ends, at, kept)[1]
        w = jnp.where(coefficient(statics, 7, at) > 0.5, second, v[pl.ds(EDGE + at, TILE)])
        image[tile] = w
        for k in range(4):
            spread = weights[k, tile]
            m[k] = m[k] + w * jnp.concatenate([spread] * (lanes // 128), axis=1)
    m = [jnp.sum(x, axis=0, keepdims=True) * SCALE for x in m]
    pad = jnp.zeros((3, lanes), jnp.float32)
    for_east = jnp.concatenate(m + [image[end:] * SCALE, pad], axis=0)
    for_west = jnp.concatenate(m + [image[:1] * SCALE, pad], axis=0)
    to_first[...] = jnp.where(even, for_east, for_west)
    to_second[...] = jnp.where(even, for_west, for_east)


def lane_sums(tiles):
    total = functools.reduce(lambda a, b: a + b, tiles)
    s = jnp.sum(total, axis=0, keepdims=True)
    return functools.reduce(lambda a, b: a + b, [s[:, k : k + 128] for k in range(0, s.shape[1], 128)])


def own_lanes(rows, levels):
    return slice(REACH * levels, (REACH + rows) * levels)


def between_kernel(rows, levels, columns, near, field, precond, image, spread, sums):
    own = own_lanes(rows, levels)
    spread[...] = dot(near[...], image[...] * SCALE)
    energy, curve = [], []
    for at in range(0, columns, TILE):
        tile = pl.ds(at, TILE)
        p = precond[pl.ds(EDGE + at, TILE), own]
        energy.append(field[tile] * p)
        curve.append(p * image[tile, own])
    sums[...] = jnp.concatenate([lane_sums(energy), lane_sums(curve), jnp.zeros((6, 128), jnp.float32)], axis=0)


def second_kernel(
    levels, columns, rows, others, spread, early, image, own_part, ghost_part, patches, ends, far, rim, *rest
):
    statics = own_part, ghost_part, patches
    received = rest[: 1 + others]
    v, f, sums = rest[1 + others :]
    v[...] = spread[...] + told(far, received)
    own = own_lanes(rows, levels)
    mixed, last, kept = [], [], {}
    for at in range(0, columns, TILE):
        tile = pl.ds(at, TILE)
        q, b = apply_tile(levels, v, statics, ends, at, kept)
        f[pl.ds(EDGE + at, TILE)] = b
        q, b, ocean = q[:, own], b[:, own], own_part[7, tile]
        mixed.append(image[tile, own] * q)
        still = jnp.where(ocean > 0.5, b, q)
        last.append(still * still)
    apply_rim(levels, columns, v, f, rim)
    sums[...] = jnp.concatenate([early[0:2], lane_sums(mixed), lane_sums(last), early[4:8]], axis=0)


def turn_kernel(rows, levels, columns, precond, image, again, f, own_part, ghost_part, patches, ends, *outs):
    statics = own_part, ghost_part, patches
    z = outs[4]
    own = own_lanes(rows, levels)
    kept = {}
    for at in range(0, columns, TILE):
        second = apply_tile(levels, f, statics, ends, at, kept)[1]
        tile = pl.ds(at, TILE)
        z[tile] = jnp.where(coefficient(statics, 7, at) > 0.5, second, again[pl.ds(EDGE + at, TILE)])
    group = REACH * levels
    slab = pl.ds(EDGE, columns)
    for j in range(0, rows, REACH):
        at = slice(own.start + j * levels, own.start + j * levels + group)
        for out, x in zip(outs, (precond[slab, at], image[:, at], again[slab, at], z[:, at])):
            t = x.T
            for i in range(REACH):
                out[pl.ds(j + i, levels, stride=rows), :] = t[i * levels : (i + 1) * levels]


PIECES = 2


def combine_kernel(sums, noise, precond, image, again, along, answer, left, x, y, sems):
    total = jnp.sum(sums[...], axis=1, keepdims=True)
    energy, curve, mixed, last = total[0:1], total[1:2], total[2:3], total[3:4]
    alpha = energy / curve
    beta = alpha / SCALE
    growth = alpha * beta * mixed / energy
    step = energy * (growth - 1.0) / (beta * beta * last - growth * growth * curve)
    keep = alpha + step * growth
    back = step * beta
    size = noise.shape[0] // PIECES
    moves = []
    for k in range(PIECES):
        part = pl.ds(k * size, size)
        x[part] = keep * precond[part] - back * again[part]
        moves.append(pltpu.make_async_copy(x.at[part], answer.at[part], sems.at[0, k]))
        moves[-1].start()
        y[part] = noise[part] - (keep * image[part] - back * along[part])
        moves.append(pltpu.make_async_copy(y.at[part], left.at[part], sems.at[1, k]))
        moves[-1].start()
    for move in moves:
        move.wait()


def doubling(count):
    steps = []
    while 2 ** len(steps) < count:
        steps.append(2 ** len(steps))
    return steps


def summed(x):
    count, bands = lax.axis_size("lon"), lax.axis_size("lat")
    x = x + lax.ppermute(x, "lon", [(i, i ^ 1) for i in range(count)])
    for step in doubling(bands)[::-1]:
        pairs = [(i * bands + j, (i ^ 1) * bands + (j ^ step)) for i in range(count) for j in range(bands)]
        x = x + lax.ppermute(x, ("lon", "lat"), pairs)
    for step in doubling(count)[1:]:
        x = x + lax.ppermute(x, "lon", [(i, i ^ step ^ 1) for i in range(count)])
    return x


def body(near, far, weights, columns_of, noise, kappa2, conduct, land):
    levels, rows, columns = noise.shape
    count = lax.axis_size("lon")
    others = count // 4
    flat = levels * rows
    group = REACH * levels
    lanes = flat + 2 * group
    tall = columns + 2 * EDGE
    rho = circle_kernel(count * columns)[0]
    noise = noise.reshape(flat, columns)
    kappa2 = kappa2.reshape(flat, columns)
    land = land.reshape(flat, columns)
    conduct = conduct.reshape(3, flat, columns)

    sources = (noise, kappa2, conduct, land, near, far, weights, columns_of)
    planes = (PLANES, levels, columns)
    first, second, noise, kappa2, conduct, land, near, far, weights, columns_of = pl.pallas_call(
        functools.partial(band_kernel, rows, levels),
        out_shape=[pltpu.VMEM(planes, jnp.float32)] * 2 + [pltpu.VMEM(x.shape, x.dtype) for x in sources],
        in_specs=[pl.BlockSpec(memory_space=pltpu.HBM)] * len(sources),
        out_specs=whole(2 + len(sources)),
        scratch_shapes=[pltpu.SemaphoreType.DMA((len(sources) + 2,))],
        compiler_params=pltpu.CompilerParams(vmem_limit_bytes=8 << 20),
        name="band_kernel",
    )(*[pltpu.with_memory_space_constraint(x, pltpu.HBM) for x in sources])
    lat_a, lat_b = lat_perms(count, lax.axis_size("lat"))
    to_band = lambda x, pairs: lax.ppermute(x, ("lon", "lat"), pairs)
    got_second, got_first = to_band(second, lat_b), to_band(first, lat_a)

    own_field, mine = call(
        functools.partial(field_kernel, rows, levels), [(columns, flat), (8, flat)], noise, weights
    )
    made, own_edge, to_first, to_second = call(
        functools.partial(own_kernel, rows, levels, columns),
        [(5, columns, flat), (8, flat), (8, flat), (8, flat)],
        kappa2, conduct, land, own_field,
    )
    lon_a, lon_b = lon_perms(count)

    def farther(two, got_two):
        if count == 4:
            return []
        (four,) = call(functools.partial(quad_kernel, rho, columns), [(8, two.shape[1])], two, got_two)
        return [lax.ppermute(four, "lon", [(i, (i + d) % count) for i in range(count)]) for d in range(4, count, 4)]

    got = lax.ppermute(mine, "lon", lon_a)
    (two,) = call(functools.partial(chip_kernel, rho, columns), [(16, flat)], mine, to_second, got)
    got_two = lax.ppermute(two, "lon", lon_b)
    (got_one,) = call(list_kernel, [(16, flat)], got, lax.ppermute(to_first, "lon", lon_a))
    lists = [got_one, got_two] + farther(two, got_two)
    own_spread, own_part = call(
        functools.partial(near_kernel, levels), [(tall, flat), (8, columns, flat)], near, own_field, made
    )
    sent = (*lists[:2], own_edge, *lists[2:])
    heights = 2 * LIST + 2 + sum(x.shape[0] for x in lists[2:])
    side_first, side_second = call(functools.partial(forward_kernel, group), [(heights, group)] * 2, own_spread, *sent)
    side_second, side_first = to_band(side_second, lat_b), to_band(side_first, lat_a)
    ghost_spread, ghost_part, patches = call(
        functools.partial(ghost_kernel, levels, columns),
        [(tall, 2 * group), (8, columns, 2 * group), (3, columns, group)],
        got_first, got_second, near, made, own_part,
    )
    precond, image, ends, rim, to_first, to_second = call(
        functools.partial(first_kernel, rows, levels, columns, others),
        [(tall, lanes), (columns, lanes), (7, 2 * TILE, lanes), (7, 8, lanes), (8, lanes), (8, lanes)],
        own_spread, own_edge, ghost_spread, own_part, ghost_part, patches, far, columns_of, side_first, side_second, *lists,
        scratch=[(tall, lanes)],
    )
    got_one = lax.ppermute(to_first, "lon", lon_a)
    (two,) = call(functools.partial(again_kernel, rho, columns), [(8, lanes)], to_second, got_one)
    got_two = lax.ppermute(two, "lon", lon_b)
    lists = [got_one, got_two] + farther(two, got_two)
    spread, sums = call(
        functools.partial(between_kernel, rows, levels, columns),
        [(tall, lanes), (8, 128)],
        near, own_field, precond, image,
    )
    again, half, sums = call(
        functools.partial(second_kernel, levels, columns, rows, others),
        [(tall, lanes), (tall, lanes), (8, 128)],
        spread, sums, image, own_part, ghost_part, patches, ends, far, rim, *lists,
    )
    sums = summed(sums)
    turned_back = call(
        functools.partial(turn_kernel, rows, levels, columns),
        [(flat, columns)] * 4 + [(columns, lanes)],
        precond, image, again, half, own_part, ghost_part, patches, ends,
    )[:4]
    operands = [pltpu.with_memory_space_constraint(x, pltpu.VMEM) for x in (sums, noise, *turned_back)]
    answer, left = pl.pallas_call(
        combine_kernel,
        out_shape=[jax.ShapeDtypeStruct((flat, columns), jnp.float32)] * 2,
        in_specs=whole(len(operands)),
        out_specs=[pl.BlockSpec(memory_space=pltpu.HBM)] * 2,
        scratch_shapes=[pltpu.VMEM((flat, columns), jnp.float32)] * 2 + [pltpu.SemaphoreType.DMA((2, PIECES))],
        compiler_params=pltpu.CompilerParams(vmem_limit_bytes=8 << 20),
        name="combine_kernel",
    )(*operands)
    return answer.reshape(levels, rows, columns), left.reshape(levels, rows, columns)


def solution(mesh):
    def run(noise, kappa2, conduct, land):
        count = mesh.shape["lon"]
        matrices = circle_matrices(count, noise.shape[2] // count)
        return jax.shard_map(
            functools.partial(body, *matrices),
            mesh=mesh,
            in_specs=(
                P("ens", "lat", "lon"),
                P(None, "lat", "lon"),
                P(None, None, "lat", "lon"),
                P(None, "lat", "lon"),
            ),
            out_specs=(P("ens", "lat", "lon"), P("ens", "lat", "lon")),
            check_vma=False,
        )(noise, kappa2, conduct, land)

    return run
```
